128 devices in a mesh: leaf: 4 (over y), front: 32 (over x, z, core).
Axes of the slice: x: 4, y: 4, z: 4, core: 2. Of those that a mesh axis runs over, the one named last changes fastest.
Arguments:
- child_rhs: bfloat16 [4, 2, 32, 64, 128], P('leaf', None, 'front'), may hold values from -6 to 6
- child_lower: bfloat16 [4, 2, 32, 64, 4096], P('leaf', None, 'front'), may hold values from -0.046875 to 0.046875
- child_inverse: bfloat16 [4, 2, 32, 64, 2048], P('leaf', None, 'front'), may hold values from -0.125 to 0.125
- child_upper: bfloat16 [4, 2, 32, 64, 4096], P('leaf', None, 'front'), may hold values from -0.046875 to 0.046875
- child_coupling: bfloat16 [4, 2, 32, 64, 4096], P('leaf', None, 'front'), may hold values from -0.046875 to 0.046875
- child_update: bfloat16 [4, 4096, 4096], P('leaf', 'front'), may hold values from -0.09375 to 0.09375
- update_owner: int32 [4, 4096, 1], P('leaf', 'front'), may hold values from 0 to 127; in each aligned block of 128 rows (0 to 127, 128 to 255, ..., all dimensions but the last counted through in order) at most 2 rows name the same one
- update_slot: int32 [4, 4096], P('leaf', 'front'), may hold values from 0 to 127
- root_rhs: bfloat16 [2, 128, 64, 128], P(None, ('leaf', 'front')), may hold values from -6 to 6
- root_lower: bfloat16 [2, 128, 64, 16384], P(None, ('leaf', 'front')), may hold values from -0.0234375 to 0.0234375
- root_inverse: bfloat16 [2, 128, 64, 8192], P(None, ('leaf', 'front')), may hold values from -0.0625 to 0.0625
- root_upper: bfloat16 [2, 128, 64, 16384], P(None, ('leaf', 'front')), may hold values from -0.0234375 to 0.0234375
Outputs:
- child_solution: bfloat16 [4, 2, 32, 64, 128], P('leaf', None, 'front')
- root_solution: bfloat16 [2, 128, 64, 128], P(None, ('leaf', 'front'))
The draws below stay inside these ranges and needn't reach their ends.
Inputs may be any that keep to these rules, and one draw needn't show every extreme that they name: `update_owner`: among the contribution rows that one device holds (aligned blocks of 128 rows), at most 2 name the same owner, a bound that some block reaches.
All inputs are finite; a program needn't handle non-finite values.
Results may differ from the reference program's by a relative error of at most 0.014.
Values may be sent and summed in bfloat16 or wider, within the bound.
No kernel may reach another device: no remote copies, remote signals or barrier semaphores. Data moves between devices by JAX's collectives and lax.ppermute only.
A program may use at most 64 MiB of HBM per device.

```python
import math
import jax
import jax.numpy as jnp
import numpy as np

STRIPE = 64
CSTEP = 2
RSTEP = 2
RHS = 128
UC_DEV = 128
KC = 2048
KR = 8192
NC = 4096
UC = 4096
NR = 16384
CAP = 2
N_LEAF = 4
N_FRONT = 32
DEVICES = 128


def set_ends(array, stream_key, least, top_value):
    longest = array.shape.index(max(array.shape))
    spots = []
    for shift in (0, 1):
        where = [jax.random.randint(jax.random.fold_in(stream_key, axis), (), 0, length) for axis, length in enumerate(array.shape)]
        where[longest] = (where[longest] + shift) % array.shape[longest]
        spots.append(tuple(where))
    return array.at[spots[0]].set(least).at[spots[1]].set(top_value)


def block_scale(own_key, shape, pieces, least, high):
    level, own = 1.0, jax.random.fold_in(own_key, 6)
    for axis_at, blocks in pieces:
        draws = jnp.exp(jax.random.uniform(jax.random.fold_in(own, axis_at), (blocks,), jnp.float32, least / len(pieces), high / len(pieces)))
        level = level * jnp.repeat(draws, shape[axis_at] // blocks).reshape([-1 if axis == axis_at else 1 for axis in range(len(shape))])
    return level


def deal_out(own_key, own, number, rows, count, top, most, skew):
    sequence = jax.random.permutation(own_key, count)
    packed, common = portions_of(count, rows * top, most, skew, True), portions_of(count, rows * top, most, skew, False)
    places = jnp.arange(count)

    def named(tallies, rotation):
        used = int((tallies > 0).sum())
        fixed = max(1, used // 4)
        shifted = fixed + (places - fixed + rotation * (used - fixed)) % max(1, count - fixed)
        return jnp.zeros((count,), jnp.int32).at[sequence[jnp.where(places < fixed, places, shifted)]].set(jnp.asarray(tallies, jnp.int32))

    tallies = jnp.where(number % 4 == 0, named(packed, number // 4), named(common, number - number // 4 - 1))
    mixed = jax.random.permutation(jax.random.fold_in(own, 3), count)
    source_of, taker = mixed[0:count // 2 * 2:2], mixed[1:count // 2 * 2:2]
    room = jnp.minimum(tallies[source_of] - 1, most - tallies[taker]) // 2
    room = jnp.where((source_of == sequence[0]) | (taker == sequence[0]) | (tallies[taker] == 0), 0, jnp.maximum(room, 0))
    shifted = jax.random.randint(jax.random.fold_in(own, 4), (count // 2,), 0, 1 << 20) % (room + 1)
    tallies = tallies.at[source_of].add(-shifted).at[taker].add(shifted)
    labels = jnp.searchsorted(jnp.cumsum(tallies), jnp.arange(rows * top), side="right").astype(jnp.int32)
    listing = labels.reshape(top, rows).T
    listing = listing[jax.random.permutation(jax.random.fold_in(own, 1), rows)]
    rotation = jax.random.randint(jax.random.fold_in(own, 2), (rows, 1), 0, top)
    return jnp.take_along_axis(listing, (jnp.arange(top)[None, :] + rotation) % top, axis=1)


def portions_of(count, total, reach, lean, full):
    portions = [(1 << 20) // math.isqrt(standing ** lean) + 1 for standing in range(1, count + 1)]
    largest = reach if full else min(reach, max(-(-total // count), total * portions[0] // sum(portions)))
    least = 1 if total - largest >= count - 1 else 0
    holding, surplus = [largest] + [least] * (count - 1), total - largest - least * (count - 1)
    while surplus > 0:
        free = [i for i in range(1, count) if holding[i] < largest] or [i for i in range(1, count) if holding[i] < reach]
        whole, budget = sum([portions[i] for i in free]), surplus
        for i in free:
            addition = min(reach - holding[i], max(1, budget * portions[i] // whole), surplus)
            holding[i] = holding[i] + addition
            surplus = surplus - addition
    return np.array(holding)


def noise(key, shape, scale, bound, pieces=(), dtype=jnp.bfloat16):
    level = block_scale(key, shape, pieces, -0.22, 0.18) if pieces else 1.0
    values = jax.random.normal(key, shape, jnp.float32) * scale * level
    return jnp.minimum(jnp.maximum(values, -bound), bound).astype(dtype)


def setup_inputs(seed: int = 0) -> dict:
    key_of = jax.random.split(jax.random.key(seed), 13)
    child_rhs = noise(key_of[0], (N_LEAF, CSTEP, N_FRONT, STRIPE, RHS), 1.0, 6.0, ((0, 4), (2, 32)))
    child_lower = noise(key_of[1], (N_LEAF, CSTEP, N_FRONT, STRIPE, NC), (4 * NC) ** -0.5, 0.046875, ((0, 4), (2, 32)))
    child_inverse = noise(key_of[2], (N_LEAF, CSTEP, N_FRONT, STRIPE, KC), KC ** -0.5, 0.125, ((0, 4), (2, 32)))
    child_upper = noise(key_of[3], (N_LEAF, CSTEP, N_FRONT, STRIPE, NC), (4 * NC) ** -0.5, 0.046875, ((0, 4), (2, 32)))
    child_coupling = noise(key_of[4], (N_LEAF, CSTEP, N_FRONT, STRIPE, UC), (4 * UC) ** -0.5, 0.046875, ((0, 4), (2, 32)))
    child_update = noise(key_of[5], (N_LEAF, UC, NC), NC ** -0.5, 0.09375, ((0, 4), (1, 32)))
    update_owner_keys = jax.random.split(jax.random.fold_in(key_of[6], 1), N_LEAF * UC // UC_DEV)
    update_owner_turns = jax.random.permutation(jax.random.fold_in(key_of[6], 3), N_LEAF * UC // UC_DEV)
    update_owner = jax.vmap(lambda own, number: deal_out(jax.random.fold_in(key_of[6], 2), own, number, UC_DEV, DEVICES, 1, CAP, 2))(update_owner_keys, update_owner_turns).reshape((N_LEAF, UC, 1))
    update_slot = set_ends(jax.random.randint(key_of[7], (N_LEAF, UC), 0, RSTEP * STRIPE), jax.random.fold_in(key_of[7], 1), 0, (RSTEP * STRIPE) - 1).astype(jnp.int32)
    root_rhs = noise(key_of[8], (RSTEP, N_LEAF * N_FRONT, STRIPE, RHS), 1.0, 6.0, ((1, 128),))
    root_lower = noise(key_of[9], (RSTEP, N_LEAF * N_FRONT, STRIPE, NR), (4 * NR) ** -0.5, 0.0234375, ((1, 128),))
    root_inverse = noise(key_of[10], (RSTEP, N_LEAF * N_FRONT, STRIPE, KR), KR ** -0.5, 0.0625, ((1, 128),))
    root_upper = noise(key_of[11], (RSTEP, N_LEAF * N_FRONT, STRIPE, NR), (4 * NR) ** -0.5, 0.0234375, ((1, 128),))
    return dict(child_rhs=child_rhs, child_lower=child_lower, child_inverse=child_inverse, child_upper=child_upper, child_coupling=child_coupling, child_update=child_update, update_owner=update_owner, update_slot=update_slot, root_rhs=root_rhs, root_lower=root_lower, root_inverse=root_inverse, root_upper=root_upper)


def block_chain(right_side, factor_rows, backward):
    step_count = right_side.shape[0]
    block_rows = right_side.shape[1]
    solved = [None] * step_count
    if backward:
        block_order = range(step_count - 1, -1, -1)
    else:
        block_order = range(step_count)
    for block_id in block_order:
        partial_sum = right_side[block_id].astype(jnp.float32)
        if backward:
            known_blocks = solved[block_id + 1:]
            column_start = (block_id + 1) * block_rows
        else:
            known_blocks = solved[:block_id]
            column_start = 0
        if len(known_blocks) > 0:
            stacked = jnp.concatenate(known_blocks, axis=0)
            columns = factor_rows[block_id][:, column_start:column_start + stacked.shape[0]]
            partial_sum = partial_sum - jnp.dot(columns, stacked, preferred_element_type=jnp.float32)
        solved[block_id] = partial_sum.astype(jnp.bfloat16)
    return jnp.stack(solved)


def apply_inverse(inverse_blocks, solved):
    return jnp.stack([jnp.dot(inverse_blocks[i], solved[i], preferred_element_type=jnp.float32).astype(jnp.bfloat16) for i in range(solved.shape[0])])


def reference(child_rhs, child_lower, child_inverse, child_upper, child_coupling, child_update, update_owner, update_slot, root_rhs, root_lower, root_inverse, root_upper):
    child_diag = []
    contributions = []
    for leaf_id in range(N_LEAF):
        right_side = child_rhs[leaf_id].reshape(CSTEP, KC, RHS).astype(jnp.float32)
        forward = block_chain(right_side, child_lower[leaf_id].reshape(CSTEP, KC, NC), False)
        child_diag.append(apply_inverse(child_inverse[leaf_id].reshape(CSTEP, KC, KC), forward))
        contributions.append(-jnp.dot(child_update[leaf_id], forward.reshape(NC, RHS), preferred_element_type=jnp.float32))
    root_index = ((update_slot // STRIPE) * KR + update_owner[:, :, 0] * STRIPE + update_slot % STRIPE).astype(jnp.int32)
    root_right = root_rhs.reshape(NR, RHS).astype(jnp.float32).at[root_index.reshape(-1)].add(jnp.concatenate(contributions, axis=0))
    root_forward = block_chain(root_right.reshape(RSTEP, KR, RHS), root_lower.reshape(RSTEP, KR, NR), False)
    root_diag = apply_inverse(root_inverse.reshape(RSTEP, KR, KR), root_forward)
    root_back = block_chain(root_diag.astype(jnp.float32), root_upper.reshape(RSTEP, KR, NR), True)
    root_values = root_back.reshape(NR, RHS)
    child_back = []
    for leaf_id in range(N_LEAF):
        update_x = root_values[root_index[leaf_id]]
        coupled = jnp.dot(child_coupling[leaf_id].reshape(NC, UC), update_x, preferred_element_type=jnp.float32).reshape(CSTEP, KC, RHS)
        right_side = child_diag[leaf_id].astype(jnp.float32) - coupled
        child_back.append(block_chain(right_side, child_upper[leaf_id].reshape(CSTEP, KC, NC), True))
    child_solution = jnp.stack(child_back).reshape(N_LEAF, CSTEP, N_FRONT, STRIPE, RHS)
    root_solution = root_back.reshape(RSTEP, N_LEAF * N_FRONT, STRIPE, RHS)
    return (child_solution, root_solution)
```

```python
import functools

import jax
import jax.numpy as jnp
from jax import lax
from jax.experimental import pallas as pl
from jax.experimental.pallas import tpu as pltpu
from jax.sharding import Mesh
from jax.sharding import PartitionSpec as P

F32 = jnp.float32
BF16 = jnp.bfloat16
ALL = ("y", "x", "z", "c")
PLANE = ("x", "z")
CUBE = ("y", "x", "z")


def gather_rows(piece, axes, count):
    own = lax.all_to_all(jnp.broadcast_to(piece, (count,) + piece.shape), axes, 0, 0)
    other = lax.ppermute(own, "c", [(0, 1), (1, 0)])
    first = lax.axis_index("c") == 0
    return jnp.stack([jnp.where(first, own, other), jnp.where(first, other, own)], axis=1)


def flat(gathered):
    return gathered.reshape(-1, gathered.shape[-1])


def dot(a, b):
    return jnp.dot(a, b, preferred_element_type=F32)


def rows_of(array, block, first, last):
    lead = array.ndim - 4
    start = (0,) * lead + (block, 0, 0, first)
    stop = (1,) * lead + (block + 1, 1, array.shape[-2], last)
    return lax.slice(array, start, stop).reshape(array.shape[-2], last - first)


def pick_kernel(index_ref, x0_ref, x1_ref, coupling_ref, out_ref, wide_ref, picked_ref):
    half = x0_ref.shape[0]
    wide_ref[0:half, :] = x0_ref[...].astype(F32)
    wide_ref[half : 2 * half, :] = x1_ref[...].astype(F32)

    def body(group, carry):
        base = group * 8
        rows = [wide_ref[pl.ds(index_ref[base + j], 1), :] for j in range(8)]
        picked_ref[pl.ds(pl.multiple_of(base, 8), 8), :] = jnp.concatenate(rows, axis=0)
        return carry

    lax.fori_loop(0, picked_ref.shape[0] // 8, body, 0, unroll=4)
    out_ref[...] = jnp.dot(
        coupling_ref[...], picked_ref[...].astype(BF16), preferred_element_type=F32
    )


def pick_and_couple(index, x0, x1, coupling):
    vmem = pl.BlockSpec(memory_space=pltpu.VMEM)
    return pl.pallas_call(
        pick_kernel,
        out_shape=jax.ShapeDtypeStruct((coupling.shape[0], x0.shape[1]), F32),
        in_specs=[pl.BlockSpec(memory_space=pltpu.SMEM), vmem, vmem, vmem],
        out_specs=vmem,
        scratch_shapes=[
            pltpu.VMEM((x0.shape[0] + x1.shape[0], x0.shape[1]), F32),
            pltpu.VMEM((index.shape[0], x0.shape[1]), F32),
        ],
        compiler_params=pltpu.CompilerParams(vmem_limit_bytes=40 << 20),
    )(index, x0, x1, coupling)


def body(
    child_rhs,
    child_lower,
    child_inverse,
    child_upper,
    child_coupling,
    child_update,
    update_owner,
    update_slot,
    root_rhs,
    root_lower,
    root_inverse,
    root_upper,
):
    planes = lax.axis_size("x") * lax.axis_size("z")
    cubes = planes * lax.axis_size("y")
    devices = cubes * lax.axis_size("c")
    stripe = root_rhs.shape[2]
    rhs = root_rhs.shape[3]
    kc = child_inverse.shape[-1]
    kr = root_inverse.shape[-1]
    nc = child_lower.shape[-1]
    owner = update_owner[0, :, 0]
    slot = update_slot[0]
    held = owner.shape[0]

    same = (owner[:, None] == owner[None, :]) & (
        jnp.arange(held)[None, :] < jnp.arange(held)[:, None]
    )
    rank = jnp.sum(same.astype(jnp.int32), axis=1)
    place = owner * 2 + rank
    select = (jnp.arange(devices * 2)[:, None] == place[None, :]).astype(BF16)
    slot_lanes = jnp.where(
        jnp.arange(rhs)[None, :] == 0, (slot + 1)[:, None], 0
    ).astype(BF16)

    marks = jnp.concatenate(
        [owner[None], slot[None], jnp.zeros((6, held), jnp.int32)], axis=0
    ).astype(BF16)
    first_piece = jnp.concatenate([child_rhs[0, 0, 0], marks], axis=0)
    first = gather_rows(first_piece, PLANE, planes)
    y0 = flat(first[:, :, :stripe])
    owners = first[:, :, stripe].astype(jnp.int32).reshape(-1)
    slots = first[:, :, stripe + 1].astype(jnp.int32).reshape(-1)
    index = slots // stripe * kr + owners * stripe + slots % stripe
    y1_own = (
        child_rhs[0, 1, 0].astype(F32) - dot(rows_of(child_lower, 1, 0, kc), y0)
    ).astype(BF16)
    y1 = flat(gather_rows(y1_own, PLANE, planes))
    update = child_update[0]
    contribution = -(dot(update[:, :kc], y0) + dot(update[:, kc:], y1))

    packed = dot(
        select, jnp.concatenate([contribution.astype(BF16), slot_lanes], axis=1)
    ).astype(BF16)
    arrived = lax.all_to_all(packed.reshape(devices, 2, 2 * rhs), ALL, 0, 0)
    arrived = arrived.reshape(devices * 2, 2 * rhs)
    lands = (
        arrived[:, rhs : rhs + 1].astype(jnp.int32) == jnp.arange(1, 2 * stripe + 1)[None, :]
    ).astype(BF16)
    received = lax.dot_general(
        lands, arrived[:, :rhs], (((0,), (0,)), ((), ())), preferred_element_type=F32
    )
    right = root_rhs[:, 0].astype(F32) + received.reshape(2, stripe, rhs)

    r0 = flat(gather_rows(right[0].astype(BF16), CUBE, cubes))
    r1_own = (right[1] - dot(rows_of(root_lower, 1, 0, kr), r0)).astype(BF16)
    r1 = flat(gather_rows(r1_own, CUBE, cubes))
    x1_own = dot(rows_of(root_inverse, 1, 0, kr), r1).astype(BF16)
    x1 = flat(gather_rows(x1_own, CUBE, cubes))
    z0_own = dot(rows_of(root_inverse, 0, 0, kr), r0).astype(BF16)
    x0_own = (
        z0_own.astype(F32) - dot(rows_of(root_upper, 0, kr, 2 * kr), x1)
    ).astype(BF16)
    x0 = flat(gather_rows(x0_own, CUBE, cubes))

    coupling = child_coupling.reshape(2 * stripe, -1)
    coupled = pick_and_couple(index, x0, x1, coupling)
    z0c = dot(rows_of(child_inverse, 0, 0, kc), y0).astype(BF16).astype(F32)
    z1c = dot(rows_of(child_inverse, 1, 0, kc), y1).astype(BF16).astype(F32)
    c1_own = (z1c - coupled[stripe:]).astype(BF16)
    c1 = flat(gather_rows(c1_own, PLANE, planes))
    c0_own = (
        z0c - coupled[:stripe] - dot(rows_of(child_upper, 0, kc, nc), c1)
    ).astype(BF16)
    child_solution = jnp.stack([c0_own, c1_own])[None, :, None]
    root_solution = jnp.stack([x0_own, x1_own])[:, None]
    return child_solution, root_solution


def solution(mesh):
    leaf, front = mesh.devices.shape
    side = {32: (4, 4, 2)}[front]
    fine = Mesh(mesh.devices.reshape((leaf,) + side), ALL)
    subtree = P("y", None, ("x", "z", "c"), None, None)
    ancestor = P(None, ALL, None, None)
    in_specs = (
        subtree,
        subtree,
        subtree,
        subtree,
        subtree,
        P("y", ("x", "z", "c"), None),
        P("y", ("x", "z", "c"), None),
        P("y", ("x", "z", "c")),
        ancestor,
        ancestor,
        ancestor,
        ancestor,
    )
    return jax.shard_map(
        body, mesh=fine, in_specs=in_specs, out_specs=(subtree, ancestor), check_vma=False
    )
```

```python
import functools

import jax
import jax.numpy as jnp
from jax import lax
from jax.experimental import pallas as pl
from jax.experimental.pallas import tpu as pltpu
from jax.sharding import Mesh
from jax.sharding import PartitionSpec as P

F32 = jnp.float32
BF16 = jnp.bfloat16
ALL = ("y", "x", "z", "c")
PLANE = ("x", "z")
CUBE = ("y", "x", "z")
VMEM = pl.BlockSpec(memory_space=pltpu.VMEM)
SMEM = pl.BlockSpec(memory_space=pltpu.SMEM)
MIB = 1 << 20


def swap(array):
    return lax.ppermute(array, "c", [(0, 1), (1, 0)])


def spread(copies, axes):
    return lax.all_to_all(copies, axes, 0, 0)


def in_core_order(own, other, axis):
    first = lax.axis_index("c") == 0
    return jnp.stack([jnp.where(first, own, other), jnp.where(first, other, own)], axis=axis)


def gather_plane(copies):
    own = spread(copies, PLANE)
    return in_core_order(own, swap(own), 1)


def flat(gathered):
    return gathered.reshape(-1, gathered.shape[-1])


def dot(a, b):
    return jnp.dot(a, b, preferred_element_type=F32)


def rows_of(array, block, first, last):
    lead = array.ndim - 4
    start = (0,) * lead + (block, 0, 0, first)
    stop = (1,) * lead + (block + 1, 1, array.shape[-2], last)
    return lax.slice(array, start, stop).reshape(array.shape[-2], last - first)


def product_kernel(subtract, core_ref, blocks_ref, own_ref, other_ref, *refs):
    if subtract:
        base_ref, out_ref = refs
    else:
        (out_ref,) = refs
    count, half, lanes = blocks_ref.shape
    total = jnp.zeros((half, lanes), F32)
    for i in range(count // 2):
        columns = slice(i * 2 * lanes, (i + 1) * 2 * lanes)
        left = jnp.concatenate([blocks_ref[2 * i], blocks_ref[2 * i + 1]], axis=1)
        right = jnp.concatenate([own_ref[0, :, columns], other_ref[0, :, columns]], axis=0)
        total = total + lax.dot_general(
            left, right, (((1,), (1,)), ((), ())), preferred_element_type=F32
        )
    total = jnp.where(core_ref[0] == 0, total, pltpu.roll(total, lanes // 2, 1))
    if subtract:
        total = base_ref[...] - total
    value = total.astype(BF16)
    if len(out_ref.shape) == 2:
        out_ref[...] = value
    else:
        for j in range(out_ref.shape[0]):
            out_ref[j] = value


def product(core, blocks, own, other, which, base, copies):
    count, half, lanes = blocks.shape
    shape = (copies, half, lanes) if copies else (half, lanes)
    matrix = pl.BlockSpec((1,) + own.shape[1:], lambda i: (which, 0, 0))
    args = (core, blocks, own, other) + (() if base is None else (base,))
    whole = lambda a: pl.BlockSpec(a.shape, lambda i: (0,) * a.ndim)
    specs = [SMEM, whole(blocks), matrix, matrix] + ([] if base is None else [whole(base)])
    return pl.pallas_call(
        functools.partial(product_kernel, base is not None),
        grid=(1,),
        out_shape=jax.ShapeDtypeStruct(shape, BF16),
        in_specs=specs,
        out_specs=pl.BlockSpec(shape, lambda i: (0,) * len(shape)),
        compiler_params=pltpu.CompilerParams(vmem_limit_bytes=14 * MIB),
        cost_estimate=pl.CostEstimate(
            flops=2 * count * half * lanes * lanes, bytes_accessed=4 * MIB, transcendentals=0
        ),
    )(*args)


def build_kernel(index_ref, coupling_ref, out_ref, sums_ref, turned_ref):
    def clear(i, carry):
        sums_ref[pl.ds(pl.multiple_of(i * 64, 64), 64), :] = jnp.zeros((64, 128), F32)
        return carry

    lax.fori_loop(0, sums_ref.shape[0] // 64, clear, 0, unroll=4)

    for i in range(turned_ref.shape[0] // 128):
        block = coupling_ref[:, i * 128 : (i + 1) * 128].astype(F32)
        turned_ref[i * 128 : (i + 1) * 128, :] = block.T

    def add(group, carry):
        base = pl.multiple_of(group * 8, 8)
        block = turned_ref[pl.ds(base, 8), :]
        for part in range(2):
            at = [index_ref[base + part * 4 + j] for j in range(4)]
            terms = [block[part * 4 + j : part * 4 + j + 1] for j in range(4)]
            old = [sums_ref[pl.ds(at[j], 1), :] for j in range(4)]
            for j in range(4):
                value = old[j] + terms[j]
                for m in range(j):
                    value = value + jnp.where(at[m] == at[j], terms[m], 0.0)
                sums_ref[pl.ds(at[j], 1), :] = value
        return carry

    lax.fori_loop(0, turned_ref.shape[0] // 8, add, 0, unroll=2)

    def settle(i, carry):
        rows = pl.ds(pl.multiple_of(i * 64, 64), 64)
        out_ref[rows, :] = sums_ref[rows, :].astype(BF16)
        return carry

    lax.fori_loop(0, sums_ref.shape[0] // 64, settle, 0, unroll=4)


def build_coupling(index, coupling, root_rows):
    rows, columns = coupling.shape
    return pl.pallas_call(
        build_kernel,
        out_shape=jax.ShapeDtypeStruct((root_rows, rows), BF16),
        in_specs=[SMEM, VMEM],
        out_specs=VMEM,
        scratch_shapes=[
            pltpu.VMEM((root_rows, rows), F32),
            pltpu.VMEM((columns, rows), F32),
        ],
        compiler_params=pltpu.CompilerParams(vmem_limit_bytes=20 * MIB),
        cost_estimate=pl.CostEstimate(flops=0, bytes_accessed=40 * MIB, transcendentals=0),
    )(index, coupling)


def couple_kernel(blocks_ref, matrix_ref, *refs):
    out_ref = refs[-1]
    count, half, lanes = blocks_ref.shape
    total = refs[0][...] if len(refs) == 2 else jnp.zeros((half, matrix_ref.shape[1]), F32)
    for i in range(count // 2):
        left = jnp.concatenate([blocks_ref[2 * i], blocks_ref[2 * i + 1]], axis=1)
        right = matrix_ref[i * 2 * lanes : (i + 1) * 2 * lanes, :]
        total = total + jnp.dot(left, right, preferred_element_type=F32)
    out_ref[...] = total


def couple(blocks, matrix, which, base):
    count, half, lanes = blocks.shape
    whole = lambda a: pl.BlockSpec(a.shape, lambda i: (0,) * a.ndim)
    args = (blocks, matrix) + (() if base is None else (base,))
    shape = (half, matrix.shape[1])
    return pl.pallas_call(
        couple_kernel,
        grid=(1,),
        out_shape=jax.ShapeDtypeStruct(shape, F32),
        in_specs=[whole(blocks), pl.BlockSpec((count * lanes, shape[1]), lambda i: (which, 0))]
        + ([] if base is None else [whole(base)]),
        out_specs=pl.BlockSpec(shape, lambda i: (0, 0)),
        compiler_params=pltpu.CompilerParams(vmem_limit_bytes=14 * MIB),
        cost_estimate=pl.CostEstimate(
            flops=2 * count * half * lanes * lanes, bytes_accessed=3 * MIB, transcendentals=0
        ),
    )(*args)


def body(
    child_rhs,
    child_lower,
    child_inverse,
    child_upper,
    child_coupling,
    child_update,
    update_owner,
    update_slot,
    root_rhs,
    root_lower,
    root_inverse,
    root_upper,
):
    planes = lax.axis_size("x") * lax.axis_size("z")
    cubes = planes * lax.axis_size("y")
    devices = cubes * 2
    stripe, rhs = root_rhs.shape[2:]
    half = rhs // 2
    kc = child_inverse.shape[-1]
    kr = root_inverse.shape[-1]
    nc = child_lower.shape[-1]
    owner = update_owner[0, :, 0]
    slot = update_slot[0]
    held = owner.shape[0]
    me = lax.axis_index("c")
    core = me.astype(jnp.int32).reshape(1)

    own = jnp.stack(
        [
            rows_of(root_lower, 1, 0, kr),
            rows_of(root_inverse, 1, 0, kr),
            rows_of(root_inverse, 0, 0, kr),
            rows_of(root_upper, 0, kr, 2 * kr),
        ]
    )
    other = swap(own)

    turned = jnp.transpose(root_rhs[:, 0], (2, 0, 1)).reshape(2, half, 2, stripe)
    kept = lax.dynamic_index_in_dim(turned, me, 0, keepdims=False)
    given = lax.dynamic_index_in_dim(turned, 1 - me, 0, keepdims=False)
    right_base = in_core_order(kept, swap(given), 2).reshape(half, -1).astype(F32)

    same = (owner[:, None] == owner[None, :]) & (
        jnp.arange(held)[None, :] < jnp.arange(held)[:, None]
    )
    rank = jnp.sum(same.astype(jnp.int32), axis=1)
    place = owner * 2 + rank
    select = (jnp.arange(devices * 2)[:, None] == place[None, :]).astype(BF16)
    target = slot // stripe * (2 * stripe) + owner % 2 * stripe + slot % stripe + 1
    target_lanes = jnp.where(jnp.arange(half)[None, :] == 0, target[:, None], 0).astype(BF16)

    marks = jnp.concatenate(
        [owner[None], slot[None], jnp.zeros((6, held), jnp.int32)], axis=0
    ).astype(BF16)
    first_piece = jnp.concatenate([child_rhs[0, 0, 0], marks], axis=0)
    first = gather_plane(jnp.broadcast_to(first_piece, (planes,) + first_piece.shape))
    y0 = flat(first[:, :, :stripe])
    owners = first[:, :, stripe].astype(jnp.int32).reshape(-1)
    slots = first[:, :, stripe + 1].astype(jnp.int32).reshape(-1)
    index = slots // stripe * kr + owners * stripe + slots % stripe
    y1_own = (
        child_rhs[0, 1, 0].astype(F32) - dot(rows_of(child_lower, 1, 0, kc), y0)
    ).astype(BF16)
    y1 = flat(gather_plane(jnp.broadcast_to(y1_own, (planes,) + y1_own.shape)))
    update = child_update[0]
    contribution = (-(dot(update[:, :kc], y0) + dot(update[:, kc:], y1))).astype(BF16)

    packed = [
        dot(
            select,
            jnp.concatenate([contribution[:, h * half : (h + 1) * half], target_lanes], axis=1),
        )
        .astype(BF16)
        .reshape(cubes, 1, 4, rhs)
        for h in range(2)
    ]
    arrived = spread(jnp.concatenate(packed, axis=1).reshape(devices, 4, rhs), ALL)
    arrived = arrived.reshape(devices * 4, rhs)
    lands = (
        arrived[:, half : half + 1].astype(jnp.int32)
        == jnp.arange(1, 4 * stripe + 1)[None, :]
    ).astype(BF16)
    received = lax.dot_general(
        arrived, lands, (((0,), (0,)), ((), ())), preferred_element_type=F32
    )[:half]
    right = right_base + received

    r0_own = right[:, : 2 * stripe].astype(BF16)
    r0 = spread(jnp.broadcast_to(r0_own, (cubes,) + r0_own.shape), CUBE)
    r1 = spread(product(core, r0, own, other, 0, right[:, 2 * stripe :], cubes), CUBE)
    x1 = spread(product(core, r1, own, other, 1, None, cubes), CUBE)
    z0_own = product(core, r0, own, other, 2, None, 0).astype(F32)
    x0_copies = product(core, x1, own, other, 3, z0_own, cubes)
    x0 = spread(x0_copies, CUBE)

    summed = build_coupling(index, child_coupling.reshape(2 * stripe, -1), 2 * kr)
    x1_other = swap(x1)
    x0_other = swap(x0)
    coupled_own = couple(x0, summed, 0, couple(x1, summed, 1, None))
    coupled_other = couple(x0_other, summed, 0, couple(x1_other, summed, 1, None))
    coupled = in_core_order(coupled_own, coupled_other, 0).reshape(rhs, 2 * stripe).T
    z0c = dot(rows_of(child_inverse, 0, 0, kc), y0).astype(BF16).astype(F32)
    z1c = dot(rows_of(child_inverse, 1, 0, kc), y1).astype(BF16).astype(F32)
    c1_own = (z1c - coupled[stripe:]).astype(BF16)
    c1 = flat(gather_plane(jnp.broadcast_to(c1_own, (planes,) + c1_own.shape)))
    c0_own = (
        z0c - coupled[:stripe] - dot(rows_of(child_upper, 0, kc, nc), c1)
    ).astype(BF16)
    child_solution = jnp.stack([c0_own, c1_own])[None, :, None]

    chip = (lax.axis_index("y") * planes + lax.axis_index("x") * lax.axis_size("z")) + (
        lax.axis_index("z")
    )

    def own_rows(mine, others):
        pair = in_core_order(
            lax.dynamic_index_in_dim(mine, chip, 0, keepdims=False),
            lax.dynamic_index_in_dim(others, chip, 0, keepdims=False),
            0,
        ).reshape(rhs, 2 * stripe)
        return lax.dynamic_slice_in_dim(pair.T, me * stripe, stripe, 0)

    root_solution = jnp.stack([own_rows(x0, x0_other), own_rows(x1, x1_other)])[:, None]
    return child_solution, root_solution


def solution(mesh):
    leaf, front = mesh.devices.shape
    fine = Mesh(mesh.devices.reshape((leaf, 4, front // 8, 2)), ALL)
    subtree = P("y", None, ("x", "z", "c"), None, None)
    ancestor = P(None, ALL, None, None)
    in_specs = (
        subtree,
        subtree,
        subtree,
        subtree,
        subtree,
        P("y", ("x", "z", "c"), None),
        P("y", ("x", "z", "c"), None),
        P("y", ("x", "z", "c")),
        ancestor,
        ancestor,
        ancestor,
        ancestor,
    )
    return jax.shard_map(
        body, mesh=fine, in_specs=in_specs, out_specs=(subtree, ancestor), check_vma=False
    )
```

```python
import functools

import jax
import jax.numpy as jnp
from jax import lax
from jax.experimental import pallas as pl
from jax.experimental.pallas import tpu as pltpu
from jax.sharding import Mesh
from jax.sharding import PartitionSpec as P

F32 = jnp.float32
BF16 = jnp.bfloat16
ALL = ("y", "x", "z", "c")
PLANE = ("x", "z")
CUBE = ("y", "x", "z")
VMEM = pl.BlockSpec(memory_space=pltpu.VMEM)
SMEM = pl.BlockSpec(memory_space=pltpu.SMEM)
MIB = 1 << 20
SMALL = 4 * MIB


def swap(array):
    return lax.ppermute(array, "c", [(0, 1), (1, 0)])


def spread(copies, axes):
    return lax.all_to_all(copies, axes, 0, 0)


def in_core_order(own, other, axis):
    first = lax.axis_index("c") == 0
    return jnp.stack([jnp.where(first, own, other), jnp.where(first, other, own)], axis=axis)


def flat(gathered):
    return gathered.reshape(-1, gathered.shape[-1])


def dot(a, b):
    return jnp.dot(a, b, preferred_element_type=F32)


def rows_of(array, block, first, last):
    lead = array.ndim - 4
    start = (0,) * lead + (block, 0, 0, first)
    stop = (1,) * lead + (block + 1, 1, array.shape[-2], last)
    return lax.slice(array, start, stop).reshape(array.shape[-2], last - first)


def opening_kernel(rhs_ref, owner_ref, slot_ref, out_ref):
    row = lax.broadcasted_iota(jnp.int32, (8, 128), 0)
    marks = jnp.where(row == 0, owner_ref[...], jnp.where(row == 1, slot_ref[...], 0))
    marks = marks.astype(F32).astype(BF16)
    rows = rhs_ref.shape[3]
    for j in range(out_ref.shape[0]):
        out_ref[j, 0:rows] = rhs_ref[0, 0, 0]
        out_ref[j, rows : rows + 8] = marks


def opening(child_rhs, owner, slot, copies):
    rows, lanes = child_rhs.shape[3:]
    return pl.pallas_call(
        opening_kernel,
        out_shape=jax.ShapeDtypeStruct((copies, rows + 8, lanes), BF16),
        in_specs=[VMEM] * 3,
        out_specs=VMEM,
        compiler_params=pltpu.CompilerParams(vmem_limit_bytes=SMALL),
    )(child_rhs, owner, slot)


def pair_dot(blocks_ref, rights):
    count, half, lanes = blocks_ref.shape
    total = None
    for i in range(count // 2):
        left = jnp.concatenate([blocks_ref[2 * i], blocks_ref[2 * i + 1]], axis=1)
        term = rights(left, slice(i * 2 * lanes, (i + 1) * 2 * lanes))
        total = term if total is None else total + term
    return total


def product_kernel(number, subtract, core_ref, blocks_ref, *refs):
    matrices, outs = refs[: 2 * number], refs[2 * number :]
    if subtract:
        base_ref, outs = outs[0], outs[1:]
    lanes = blocks_ref.shape[2]
    rights = lambda left, columns: lax.dot_general(
        left,
        jnp.concatenate([m[:, columns] for m in matrices], axis=0),
        (((1,), (1,)), ((), ())),
        preferred_element_type=F32,
    )
    both = pair_dot(blocks_ref, rights)
    for n, out_ref in enumerate(outs):
        total = both[:, n * lanes : (n + 1) * lanes]
        total = jnp.where(core_ref[0] == 0, total, pltpu.roll(total, lanes // 2, 1))
        if n == 0:
            if subtract:
                total = base_ref[...] - total
            value = total.astype(BF16)
            for j in range(out_ref.shape[0]):
                out_ref[j] = value
        else:
            out_ref[...] = total.astype(BF16).astype(F32)


def product(core, blocks, matrices, base):
    count, half, lanes = blocks.shape
    number = len(matrices) // 2
    args = (core, blocks, *matrices) + (() if base is None else (base,))
    shapes = [jax.ShapeDtypeStruct((count, half, lanes), BF16)]
    shapes += [jax.ShapeDtypeStruct((half, lanes), F32)] * (number - 1)
    return pl.pallas_call(
        functools.partial(product_kernel, number, base is not None),
        out_shape=shapes,
        in_specs=[SMEM] + [VMEM] * (len(args) - 1),
        out_specs=[VMEM] * len(shapes),
        compiler_params=pltpu.CompilerParams(vmem_limit_bytes=SMALL),
        cost_estimate=pl.CostEstimate(
            flops=2 * number * count * half * lanes * lanes,
            bytes_accessed=(2 + 2 * number) * MIB,
            transcendentals=0,
        ),
    )(*args)


def build_kernel(index_ref, own_ref, other_ref, out_ref, sums_ref, turned_ref):
    width = out_ref.shape[1]
    half = width // 2

    def clear(i, carry):
        sums_ref[pl.ds(pl.multiple_of(i * 64, 64), 64), :] = jnp.zeros((64, width), F32)
        return carry

    lax.fori_loop(0, sums_ref.shape[0] // 64, clear, 0, unroll=4)

    for i in range(turned_ref.shape[0] // 128):
        rows = slice(i * 128, (i + 1) * 128)
        turned_ref[rows, 0:half] = own_ref[:, rows].astype(F32).T
        turned_ref[rows, half:width] = other_ref[:, rows].astype(F32).T

    def add(group, carry):
        base = pl.multiple_of(group * 8, 8)
        block = turned_ref[pl.ds(base, 8), :]
        for part in range(2):
            at = [index_ref[base + part * 4 + j] for j in range(4)]
            terms = [block[part * 4 + j : part * 4 + j + 1] for j in range(4)]
            old = [sums_ref[pl.ds(at[j], 1), :] for j in range(4)]
            for j in range(4):
                value = old[j] + terms[j]
                for m in range(j):
                    value = value + jnp.where(at[m] == at[j], terms[m], 0.0)
                sums_ref[pl.ds(at[j], 1), :] = value
        return carry

    lax.fori_loop(0, turned_ref.shape[0] // 8, add, 0, unroll=2)

    def settle(i, carry):
        rows = pl.ds(pl.multiple_of(i * 64, 64), 64)
        out_ref[rows, :] = sums_ref[rows, :].astype(BF16)
        return carry

    lax.fori_loop(0, sums_ref.shape[0] // 64, settle, 0, unroll=4)


def build_coupling(index, own, other, root_rows):
    rows, columns = own.shape
    return pl.pallas_call(
        build_kernel,
        out_shape=jax.ShapeDtypeStruct((root_rows, 2 * rows), BF16),
        in_specs=[SMEM, VMEM, VMEM],
        out_specs=VMEM,
        scratch_shapes=[
            pltpu.VMEM((root_rows, 2 * rows), F32),
            pltpu.VMEM((columns, 2 * rows), F32),
        ],
        compiler_params=pltpu.CompilerParams(vmem_limit_bytes=32 * MIB),
        cost_estimate=pl.CostEstimate(flops=0, bytes_accessed=40 * MIB, transcendentals=0),
    )(index, own, other)


def couple_kernel(x0_ref, x1_ref, matrix_ref, own_ref, other_ref):
    count, half, lanes = x0_ref.shape

    def product_with(blocks_ref, start):
        return pair_dot(
            blocks_ref,
            lambda left, columns: jnp.dot(
                left,
                matrix_ref[start + columns.start : start + columns.stop, :],
                preferred_element_type=F32,
            ),
        )

    total = product_with(x0_ref, 0) + product_with(x1_ref, count * lanes)
    own_ref[...] = total[:, : total.shape[1] // 2]
    other_ref[...] = total[:, total.shape[1] // 2 :]


def couple(x0, x1, matrix):
    count, half, lanes = x0.shape
    width = matrix.shape[1]
    return pl.pallas_call(
        couple_kernel,
        out_shape=[jax.ShapeDtypeStruct((half, width // 2), F32)] * 2,
        in_specs=[VMEM] * 3,
        out_specs=[VMEM] * 2,
        compiler_params=pltpu.CompilerParams(vmem_limit_bytes=SMALL),
        cost_estimate=pl.CostEstimate(
            flops=4 * count * half * lanes * width, bytes_accessed=10 * MIB, transcendentals=0
        ),
    )(x0, x1, matrix)


def settle_kernel(core_ref, mine_ref, theirs_ref, z0_ref, z1_ref, copies_ref, rest_ref):
    mine, theirs = mine_ref[...], theirs_ref[...]
    first = core_ref[0] == 0
    both = jnp.concatenate(
        [jnp.where(first, mine, theirs), jnp.where(first, theirs, mine)], axis=0
    ).T
    stripe = z0_ref.shape[0]
    rest_ref[...] = z0_ref[...] - both[:stripe]
    value = (z1_ref[...] - both[stripe:]).astype(BF16)
    for j in range(copies_ref.shape[0]):
        copies_ref[j] = value


def settle_coupling(core, mine, theirs, z0, z1, copies):
    return pl.pallas_call(
        settle_kernel,
        out_shape=[
            jax.ShapeDtypeStruct((copies,) + z1.shape, BF16),
            jax.ShapeDtypeStruct(z0.shape, F32),
        ],
        in_specs=[SMEM] + [VMEM] * 4,
        out_specs=[VMEM] * 2,
        compiler_params=pltpu.CompilerParams(vmem_limit_bytes=SMALL),
    )(core, mine, theirs, z0, z1)


def body(
    child_rhs,
    child_lower,
    child_inverse,
    child_upper,
    child_coupling,
    child_update,
    update_owner,
    update_slot,
    root_rhs,
    root_lower,
    root_inverse,
    root_upper,
):
    planes = lax.axis_size("x") * lax.axis_size("z")
    cubes = planes * lax.axis_size("y")
    devices = cubes * 2
    stripe, rhs = root_rhs.shape[2:]
    half = rhs // 2
    kc = child_inverse.shape[-1]
    kr = root_inverse.shape[-1]
    nc = child_lower.shape[-1]
    owner = update_owner[0, :, 0]
    slot = update_slot[0]
    held = owner.shape[0]
    me = lax.axis_index("c")
    core = me.astype(jnp.int32).reshape(1)

    tie = lax.optimization_barrier

    own_first = spread(opening(child_rhs, owner[None], slot[None], planes), PLANE)
    own = [
        rows_of(root_lower, 1, 0, kr),
        rows_of(root_inverse, 0, 0, kr),
        rows_of(root_inverse, 1, 0, kr),
        rows_of(root_upper, 0, kr, 2 * kr),
    ]
    own_first, own = tie((own_first, own))
    first = in_core_order(own_first, swap(own_first), 1)
    y0 = flat(first[:, :, :stripe])
    y1_own = (child_rhs[0, 1, 0].astype(F32) - dot(rows_of(child_lower, 1, 0, kc), y0)).astype(BF16)
    own_second = spread(jnp.broadcast_to(y1_own, (planes,) + y1_own.shape), PLANE)

    own, coupling, first = tie((own, child_coupling.reshape(2 * stripe, -1), first))
    lower, low_inverse, high_inverse, upper = [(m, swap(m)) for m in own]
    coupling_other = swap(coupling)
    turned = jnp.transpose(root_rhs[:, 0], (2, 0, 1)).reshape(2, half, 2, stripe)
    kept = jnp.where(me == 0, turned[0], turned[1])
    given = jnp.where(me == 0, turned[1], turned[0])
    right_base = in_core_order(kept, swap(given), 2).reshape(half, -1).astype(F32)
    z0c = dot(rows_of(child_inverse, 0, 0, kc), y0).astype(BF16).astype(F32)
    owners = first[:, :, stripe].astype(jnp.int32).reshape(-1)
    slots = first[:, :, stripe + 1].astype(jnp.int32).reshape(-1)
    index = slots // stripe * kr + owners * stripe + slots % stripe
    same = (owner[:, None] == owner[None, :]) & (
        jnp.arange(held)[None, :] < jnp.arange(held)[:, None]
    )
    rank = jnp.sum(same.astype(jnp.int32), axis=1)
    place = owner * 2 + rank
    select = (jnp.arange(devices * 2)[:, None] == place[None, :]).astype(BF16)
    target = slot // stripe * (2 * stripe) + owner % 2 * stripe + slot % stripe + 1
    target_lanes = jnp.where(jnp.arange(half)[None, :] == 0, target[:, None], 0).astype(BF16)
    update = child_update[0]
    part = dot(update[:, :kc], y0)
    own_second, z0c, index, select, target_lanes, part = tie(
        (own_second, z0c, index, select, target_lanes, part)
    )
    y1 = flat(in_core_order(own_second, swap(own_second), 1))
    contribution = (-(part + dot(update[:, kc:], y1))).astype(BF16)

    packed = [
        dot(
            select,
            jnp.concatenate([contribution[:, h * half : (h + 1) * half], target_lanes], axis=1),
        )
        .astype(BF16)
        .reshape(cubes, 1, 4, rhs)
        for h in range(2)
    ]
    arrived = spread(jnp.concatenate(packed, axis=1).reshape(devices, 4, rhs), ALL)
    z1c = dot(rows_of(child_inverse, 1, 0, kc), y1).astype(BF16).astype(F32)
    arrived, z1c, right_base, coupling_other, lower, low_inverse = tie(
        (arrived, z1c, right_base, coupling_other, lower, low_inverse)
    )
    arrived = arrived.reshape(devices * 4, rhs)
    lands = (
        arrived[:, half : half + 1].astype(jnp.int32)
        == jnp.arange(1, 4 * stripe + 1)[None, :]
    ).astype(BF16)
    received = lax.dot_general(
        arrived, lands, (((0,), (0,)), ((), ())), preferred_element_type=F32
    )[:half]
    right = right_base + received

    r0_own = right[:, : 2 * stripe].astype(BF16)
    r0 = spread(jnp.broadcast_to(r0_own, (cubes,) + r0_own.shape), CUBE)
    summed = build_coupling(index, coupling, coupling_other, 2 * kr)
    r0, summed, high_inverse, upper = tie((r0, summed, high_inverse, upper))
    r1_copies, z0_own = product(core, r0, lower + low_inverse, right[:, 2 * stripe :])
    r1 = spread(r1_copies, CUBE)
    (x1_copies,) = product(core, r1, high_inverse, None)
    x1 = spread(x1_copies, CUBE)
    (x0_copies,) = product(core, x1, upper, z0_own)
    x0 = spread(x0_copies, CUBE)

    x0, x0_copies, x1_copies = tie((x0, x0_copies, x1_copies))
    mine, given = couple(x0, x1, summed)
    c1_copies, rest = settle_coupling(core, mine, swap(given), z0c, z1c, planes)
    c1_copies, x0_own, x1_own = tie((c1_copies, x0_copies[0], x1_copies[0]))
    own_c1 = spread(c1_copies, PLANE)

    def own_rows(half_rows):
        pair = in_core_order(half_rows, swap(half_rows), 0).reshape(rhs, 2 * stripe)
        rows = pair.T
        return jnp.where(me == 0, rows[:stripe], rows[stripe:])

    root_solution = jnp.stack([own_rows(x0_own), own_rows(x1_own)])[:, None]
    own_c1, root_solution = tie((own_c1, root_solution))
    c1 = flat(in_core_order(own_c1, swap(own_c1), 1))
    c0_own = (rest - dot(rows_of(child_upper, 0, kc, nc), c1)).astype(BF16)
    child_solution = jnp.stack([c0_own, c1_copies[0]])[None, :, None]
    return child_solution, root_solution


def solution(mesh):
    leaf, front = mesh.devices.shape
    fine = Mesh(mesh.devices.reshape((leaf, 4, front // 8, 2)), ALL)
    subtree = P("y", None, ("x", "z", "c"), None, None)
    ancestor = P(None, ALL, None, None)
    in_specs = (
        subtree,
        subtree,
        subtree,
        subtree,
        subtree,
        P("y", ("x", "z", "c"), None),
        P("y", ("x", "z", "c"), None),
        P("y", ("x", "z", "c")),
        ancestor,
        ancestor,
        ancestor,
        ancestor,
    )
    return jax.shard_map(
        body, mesh=fine, in_specs=in_specs, out_specs=(subtree, ancestor), check_vma=False
    )
```

```python
import functools

import jax
import jax.numpy as jnp
from jax import lax
from jax.experimental import pallas as pl
from jax.experimental.pallas import tpu as pltpu
from jax.sharding import Mesh
from jax.sharding import PartitionSpec as P

F32 = jnp.float32
BF16 = jnp.bfloat16
ALL = ("y", "x", "z", "c")
PLANE = ("x", "z")
CUBE = ("y", "x", "z")
VMEM = pl.BlockSpec(memory_space=pltpu.VMEM)
SMEM = pl.BlockSpec(memory_space=pltpu.SMEM)
HBM = pl.BlockSpec(memory_space=pltpu.HBM)
DMA = pltpu.SemaphoreType.DMA
MIB = 1 << 20
tie = lax.optimization_barrier


def swap(array):
    return lax.ppermute(array, "c", [(0, 1), (1, 0)])


def spread(copies, axes):
    return lax.all_to_all(copies, axes, 0, 0)


def in_core_order(own, other, axis):
    first = lax.axis_index("c") == 0
    return jnp.stack([jnp.where(first, own, other), jnp.where(first, other, own)], axis=axis)


def rows_of(array, block, first, last):
    lead = array.ndim - 4
    start = (0,) * lead + (block, 0, 0, first)
    stop = (1,) * lead + (block + 1, 1, array.shape[-2], last)
    return lax.slice(array, start, stop).reshape(array.shape[-2], last - first)


def like(shape, dtype=BF16):
    return jax.ShapeDtypeStruct(shape, dtype)


def kernel_call(body, args, specs, shapes, out_specs, scratch=(), limit=None, flops=0, moved=0):
    return pl.pallas_call(
        body,
        out_shape=shapes,
        in_specs=specs,
        out_specs=out_specs,
        scratch_shapes=list(scratch),
        compiler_params=pltpu.CompilerParams(
            vmem_limit_bytes=None if limit is None else limit * MIB
        ),
        cost_estimate=pl.CostEstimate(flops=flops, bytes_accessed=moved, transcendentals=0),
    )(*args)


def by_core(core_ref, own_refs, other_refs, work):
    @pl.when(core_ref[0] == 0)
    def _():
        work(own_refs, other_refs)

    @pl.when(core_ref[0] != 0)
    def _():
        work(other_refs, own_refs)


def plane_dot(matrix_ref, first_ref, second_ref, rows):
    total = None
    for p in range(first_ref.shape[0] // 2):
        block = jnp.concatenate(
            [
                first_ref[2 * p, 0:rows],
                second_ref[2 * p, 0:rows],
                first_ref[2 * p + 1, 0:rows],
                second_ref[2 * p + 1, 0:rows],
            ],
            axis=0,
        )
        term = jnp.dot(
            matrix_ref[:, p * 4 * rows : (p + 1) * 4 * rows], block, preferred_element_type=F32
        )
        total = term if total is None else total + term
    return total


def opening_kernel(rhs_ref, owner_ref, slot_ref, out_ref):
    row = lax.broadcasted_iota(jnp.int32, (8, 128), 0)
    marks = jnp.where(row == 0, owner_ref[...], jnp.where(row == 1, slot_ref[...], 0))
    marks = marks.astype(F32).astype(BF16)
    rows = rhs_ref.shape[3]
    for j in range(out_ref.shape[0]):
        out_ref[j, 0:rows] = rhs_ref[0, 0, 0]
        out_ref[j, rows : rows + 8] = marks


def turn_kernel(core_ref, rhs_ref, lower_ref, kept_ref, given_ref, low_ref, sem):
    copy = pltpu.make_async_copy(
        lower_ref.at[0, 1, 0, :, pl.ds(0, low_ref.shape[1])], low_ref, sem
    )
    copy.start()
    both = jnp.concatenate(
        [rhs_ref[0, 0].astype(F32).T, rhs_ref[1, 0].astype(F32).T], axis=1
    ).astype(BF16)
    half = both.shape[0] // 2

    @pl.when(core_ref[0] == 0)
    def _():
        kept_ref[...] = both[:half]
        given_ref[...] = both[half:]

    @pl.when(core_ref[0] != 0)
    def _():
        kept_ref[...] = both[half:]
        given_ref[...] = both[:half]

    copy.wait()


def advance_kernel(core_ref, own_ref, other_ref, low_ref, rhs_ref, out_ref):
    rows = out_ref.shape[1]

    def work(first, second):
        total = rhs_ref[0, 1, 0].astype(F32) - plane_dot(low_ref, first, second, rows)
        value = total.astype(BF16)
        for j in range(out_ref.shape[0]):
            out_ref[j] = value

    by_core(core_ref, own_ref, other_ref, work)


def aside_kernel(
    rows, kr, core_ref, own_ref, other_ref, update_ref, inverse_ref,
    part_ref, z0_ref, index_ref, low_ref, diag_ref, sems
):
    kc = low_ref.shape[1]
    copies = [
        pltpu.make_async_copy(update_ref.at[0, :, pl.ds(0, kc)], low_ref, sems.at[0]),
        pltpu.make_async_copy(inverse_ref.at[0, 0, 0], diag_ref, sems.at[1]),
    ]
    for copy in copies:
        copy.start()

    def work(first, second):
        for j in range(own_ref.shape[0]):
            for c, source in enumerate((first, second)):
                marks = source[j, rows : rows + 8].astype(F32).astype(jnp.int32)
                owner, slot = marks[0:1], marks[1:2]
                index_ref[2 * j + c : 2 * j + c + 1, :] = (
                    (slot // rows) * kr + owner * rows + slot % rows
                )
        copies[0].wait()
        part_ref[...] = plane_dot(low_ref, first, second, rows)
        copies[1].wait()
        z0_ref[...] = plane_dot(diag_ref, first, second, rows).astype(BF16).astype(F32)

    by_core(core_ref, own_ref, other_ref, work)


def contribute_kernel(
    core_ref, own_ref, other_ref, update_ref, part_ref, owner_ref, slot_ref, out_ref, high_ref, sem
):
    kc = high_ref.shape[1]
    copy = pltpu.make_async_copy(update_ref.at[0, :, pl.ds(kc, kc)], high_ref, sem)
    copy.start()
    rows = own_ref.shape[1]
    held = owner_ref.shape[1]
    owner = owner_ref[...].astype(F32)
    owners = jnp.broadcast_to(owner, (held, held))
    above = lax.broadcasted_iota(jnp.int32, (held, held), 0) < lax.broadcasted_iota(
        jnp.int32, (held, held), 1
    )
    same = jnp.where((owners == owners.T) & above, 1.0, 0.0)
    place = owner * 2.0 + jnp.sum(same, axis=0, keepdims=True)
    row = lax.broadcasted_iota(jnp.int32, (out_ref.shape[0], held), 0)
    wanted = (row // 8 * 4 + row % 4).astype(F32)
    select = jnp.where(wanted == place, 1.0, 0.0).astype(BF16)
    slot = slot_ref[...]
    target = slot // rows * (2 * rows) + owner_ref[...] % 2 * rows + slot % rows + 1
    targets = jnp.broadcast_to(target.astype(F32), (held, held)).T[:, :rows].astype(BF16)

    copy.wait()

    def work(first, second):
        contribution = -(part_ref[...] + plane_dot(high_ref, first, second, rows))
        contribution = contribution.astype(BF16)
        half = contribution.shape[1] // 2
        source = jnp.concatenate(
            [contribution[:, :half], targets, contribution[:, half:], targets], axis=1
        )
        both = jnp.dot(select, source, preferred_element_type=F32)
        lanes = 2 * half
        upper = lax.broadcasted_iota(jnp.int32, (both.shape[0], lanes), 0) % 8 >= 4
        out_ref[...] = jnp.where(upper, both[:, lanes:], both[:, :lanes]).astype(BF16)

    by_core(core_ref, own_ref, other_ref, work)


def diagonal_kernel(core_ref, own_ref, other_ref, inverse_ref, z1_ref, diag_ref, sem):
    copy = pltpu.make_async_copy(inverse_ref.at[0, 1, 0], diag_ref, sem)
    copy.start()
    copy.wait()

    def work(first, second):
        total = plane_dot(diag_ref, first, second, own_ref.shape[1])
        z1_ref[...] = total.astype(BF16).astype(F32)

    by_core(core_ref, own_ref, other_ref, work)


def unpack_kernel(core_ref, arrived_ref, kept_ref, got_ref, copies_ref, right_ref):
    half, lanes = right_ref.shape
    arrived = arrived_ref[...]
    code = arrived[:, half : half + 1].astype(F32)
    lane = lax.broadcasted_iota(jnp.int32, (arrived.shape[0], 2 * lanes), 1).astype(F32)
    lands = jnp.where(code == lane + 1.0, 1.0, 0.0).astype(BF16)
    received = lax.dot_general(
        arrived, lands, (((0,), (0,)), ((), ())), preferred_element_type=F32
    )[:half]

    def work(first, second):
        bases = [
            jnp.concatenate(
                [first[:, r * half : (r + 1) * half], second[:, r * half : (r + 1) * half]], axis=1
            ).astype(F32)
            for r in range(2)
        ]
        value = (bases[0] + received[:, :lanes]).astype(BF16)
        for j in range(copies_ref.shape[0]):
            copies_ref[j] = value
        right_ref[...] = bases[1] + received[:, lanes:]

    by_core(core_ref, kept_ref, got_ref, work)


def build_kernel(index_ref, coupling_ref, out_ref, raw_ref, turned_ref, sums_ref, done_ref, sems):
    rows, width = sums_ref.shape
    half = width // 2
    loads = [
        pltpu.make_async_copy(
            coupling_ref.at[0, r, 0], raw_ref.at[pl.ds(r * half, half)], sems.at[r]
        )
        for r in range(2)
    ]
    for load in loads:
        load.start()

    def clear(i, carry):
        sums_ref[pl.ds(pl.multiple_of(i * 128, 128), 128), :] = jnp.zeros((128, width), F32)
        return carry

    lax.fori_loop(0, rows // 128, clear, 0, unroll=4)
    for load in loads:
        load.wait()
    for i in range(turned_ref.shape[0] // 128):
        part = slice(i * 128, (i + 1) * 128)
        turned_ref[part, :] = raw_ref[:, part].astype(F32).T

    def add(group, carry):
        base = pl.multiple_of(group * 8, 8)
        block = turned_ref[pl.ds(base, 8), :]
        for part in range(2):
            at = []
            for j in range(4):
                u = base + part * 4 + j
                at.append(index_ref[u // 128, u % 128])
            terms = [block[part * 4 + j : part * 4 + j + 1] for j in range(4)]
            old = [sums_ref[pl.ds(at[j], 1), :] for j in range(4)]
            for j in range(4):
                value = old[j] + terms[j]
                for m in range(j):
                    value = value + jnp.where(at[m] == at[j], terms[m], 0.0)
                sums_ref[pl.ds(at[j], 1), :] = value
        return carry

    lax.fori_loop(0, turned_ref.shape[0] // 8, add, 0, unroll=2)
    parts = sems.shape[0] - 2
    size = rows // parts
    stores = []
    for i in range(parts):
        part = pl.ds(i * size, size)
        done_ref[part, :] = sums_ref[part, :].astype(BF16)
        store = pltpu.make_async_copy(done_ref.at[part], out_ref.at[part], sems.at[2 + i])
        store.start()
        stores.append(store)
    for store in stores:
        store.wait()


def build_coupling(index, coupling, root_rows):
    rows, columns = 2 * coupling.shape[-2], coupling.shape[-1]
    return kernel_call(
        build_kernel,
        (index, coupling),
        [SMEM, HBM],
        like((root_rows, rows)),
        HBM,
        scratch=[
            pltpu.VMEM((rows, columns), BF16),
            pltpu.VMEM((columns, rows), F32),
            pltpu.VMEM((root_rows, rows), F32),
            pltpu.VMEM((root_rows, rows), BF16),
            DMA((10,)),
        ],
        limit=61,
        moved=30 * MIB,
    )


def pair_dot(blocks_ref, start, stop, rights):
    lanes = blocks_ref.shape[2]
    total = None
    for i in range(start // 2, stop // 2):
        left = jnp.concatenate([blocks_ref[2 * i], blocks_ref[2 * i + 1]], axis=1)
        term = rights(left, slice(i * 2 * lanes, (i + 1) * 2 * lanes))
        total = term if total is None else total + term
    return total


def against(*parts):
    return lambda left, columns: lax.dot_general(
        left,
        jnp.concatenate([part[:, columns] for part in parts], axis=0),
        (((1,), (1,)), ((), ())),
        preferred_element_type=F32,
    )


def ordered(core_ref, total):
    return jnp.where(core_ref[0] == 0, total, pltpu.roll(total, total.shape[1] // 2, 1))


def write_copies(copies_ref, value):
    for j in range(copies_ref.shape[0]):
        copies_ref[j] = value


def first_product_kernel(
    core_ref, blocks_ref, lower_ref, inverse_ref, upper_ref,
    lower_other, low_other, high_other, upper_other, base_ref,
    copies_ref, z0_ref, high_ref, top_ref, held_ref, sems
):
    kr = held_ref.shape[2]
    chips, half, lanes = blocks_ref.shape
    steps = 4
    width, span = kr // steps, chips // steps
    copies = []
    for i in range(steps):
        columns = pl.ds(i * width, width)
        pairs = [
            (lower_ref.at[1, 0, :, columns], held_ref.at[0, :, columns]),
            (lower_other.at[:, columns], held_ref.at[1, :, columns]),
            (inverse_ref.at[0, 0, :, columns], held_ref.at[2, :, columns]),
            (low_other.at[:, columns], held_ref.at[3, :, columns]),
        ]
        copies.append(
            [pltpu.make_async_copy(a, b, sems.at[i, n]) for n, (a, b) in enumerate(pairs)]
        )
    later = [
        (inverse_ref.at[1, 0], high_ref.at[0]),
        (high_other, high_ref.at[1]),
        (upper_ref.at[0, 0, :, pl.ds(kr, kr)], top_ref.at[0]),
        (upper_other, top_ref.at[1]),
    ]
    later = [pltpu.make_async_copy(a, b, sems.at[steps, n]) for n, (a, b) in enumerate(later)]
    for group in copies:
        for copy in group:
            copy.start()
    for copy in later:
        copy.start()
    rights = against(*(held_ref.at[n] for n in range(4)))
    both = None
    for i, group in enumerate(copies):
        for copy in group:
            copy.wait()
        term = pair_dot(blocks_ref, i * span, (i + 1) * span, rights)
        both = term if both is None else both + term
    total = base_ref[...] - ordered(core_ref, both[:, :lanes])
    write_copies(copies_ref, total.astype(BF16))
    z0_ref[...] = ordered(core_ref, both[:, lanes:]).astype(BF16).astype(F32)
    for copy in later:
        copy.wait()


def product_kernel(subtract, core_ref, blocks_ref, matrix_ref, *refs):
    copies_ref = refs[-1]
    total = pair_dot(
        blocks_ref, 0, blocks_ref.shape[0], against(matrix_ref.at[0], matrix_ref.at[1])
    )
    total = ordered(core_ref, total)
    if subtract:
        total = refs[0][...] - total
    write_copies(copies_ref, total.astype(BF16))


def product(core, blocks, matrix, base):
    args = (core, blocks, matrix) + (() if base is None else (base,))
    count, half, lanes = blocks.shape
    return kernel_call(
        functools.partial(product_kernel, base is not None),
        args,
        [SMEM] + [VMEM] * (len(args) - 1),
        like(blocks.shape),
        VMEM,
        limit=6,
        flops=2 * count * half * lanes * lanes,
        moved=4 * MIB,
    )


def couple_kernel(x0_ref, x1_ref, own_ref, other_ref, mine_ref, theirs_ref):
    count, half, lanes = x0_ref.shape
    total = None
    for start, blocks_ref in ((0, x0_ref), (count * lanes, x1_ref)):

        def rights(left, columns):
            rows = slice(start + columns.start, start + columns.stop)
            return jnp.dot(
                left,
                jnp.concatenate([own_ref[rows, :], other_ref[rows, :]], axis=1),
                preferred_element_type=F32,
            )

        term = pair_dot(blocks_ref, 0, count, rights)
        total = term if total is None else total + term
    width = mine_ref.shape[1]
    mine_ref[...] = total[:, :width]
    theirs_ref[...] = total[:, width:]


def settle_kernel(core_ref, mine_ref, got_ref, z0_ref, z1_ref, upper_ref,
                  copies_ref, rest_ref, top_ref, sem):
    width = top_ref.shape[1]
    copy = pltpu.make_async_copy(upper_ref.at[0, 0, 0, :, pl.ds(width, width)], top_ref, sem)
    copy.start()
    stripe = z0_ref.shape[0]

    def work(first, second):
        both = jnp.concatenate([first[...], second[...]], axis=0).T
        rest_ref[...] = z0_ref[...] - both[:stripe]
        write_copies(copies_ref, (z1_ref[...] - both[stripe:]).astype(BF16))

    by_core(core_ref, mine_ref, got_ref, work)
    copy.wait()


def closing_kernel(core_ref, own_ref, other_ref, top_ref, rest_ref, copies_ref, out_ref):
    out_ref[0, 1, 0] = copies_ref[0]

    def work(first, second):
        total = rest_ref[...] - plane_dot(top_ref, first, second, own_ref.shape[1])
        out_ref[0, 0, 0] = total.astype(BF16)

    by_core(core_ref, own_ref, other_ref, work)


def body(
    child_rhs,
    child_lower,
    child_inverse,
    child_upper,
    child_coupling,
    child_update,
    update_owner,
    update_slot,
    root_rhs,
    root_lower,
    root_inverse,
    root_upper,
):
    planes = lax.axis_size("x") * lax.axis_size("z")
    cubes = planes * lax.axis_size("y")
    devices = cubes * 2
    stripe, rhs = root_rhs.shape[2:]
    half = rhs // 2
    kc = child_inverse.shape[-1]
    kr = root_inverse.shape[-1]
    held = update_slot.shape[1]
    owner = update_owner.reshape(1, held)
    slot = update_slot
    me = lax.axis_index("c")
    core = me.astype(jnp.int32).reshape(1)
    piece = (planes, stripe, rhs)

    opened = kernel_call(
        opening_kernel, (child_rhs, owner, slot), [VMEM] * 3,
        like((planes, stripe + 8, rhs)), VMEM,
    )
    opened, root_rhs, child_lower, root_lower, root_inverse, root_upper = tie(
        (opened, root_rhs, child_lower, root_lower, root_inverse, root_upper)
    )
    own_first = spread(opened, PLANE)
    kept, given, low = kernel_call(
        turn_kernel, (core, root_rhs, child_lower), [SMEM, VMEM, HBM],
        [like((half, rhs)), like((half, rhs)), pltpu.VMEM((stripe, kc), BF16)], [VMEM] * 3,
        scratch=[DMA], limit=2, moved=MIB,
    )
    own = [
        rows_of(root_lower, 1, 0, kr),
        rows_of(root_inverse, 0, 0, kr),
        rows_of(root_inverse, 1, 0, kr),
        rows_of(root_upper, 0, kr, 2 * kr),
    ]
    own_first, own, kept, given, low = tie((own_first, own, kept, given, low))
    other_first = swap(own_first)
    y1_copies = kernel_call(
        advance_kernel, (core, own_first, other_first, low, child_rhs), [SMEM] + [VMEM] * 4,
        like(piece), VMEM, limit=2, moved=MIB,
    )
    y1_copies, own, given = tie((y1_copies, own, given))
    own_second = spread(y1_copies, PLANE)

    lower_other, low_other, high_other, upper_other = [swap(m) for m in own]
    got = swap(given)
    part, z0c, index = kernel_call(
        functools.partial(aside_kernel, stripe, kr),
        (core, own_first, other_first, child_update, child_inverse),
        [SMEM, VMEM, VMEM, HBM, HBM],
        [
            like((held, rhs), F32),
            like((stripe, rhs), F32),
            like((2 * planes, held), jnp.int32),
        ],
        [VMEM] * 3,
        scratch=[pltpu.VMEM((held, kc), BF16), pltpu.VMEM((stripe, kc), BF16), DMA((2,))],
        limit=4, moved=2 * MIB,
    )
    own_second, part, z0c, index, got = tie((own_second, part, z0c, index, got))
    other_second = swap(own_second)

    packed = kernel_call(
        contribute_kernel, (core, own_second, other_second, child_update, part, owner, slot),
        [SMEM, VMEM, VMEM, HBM] + [VMEM] * 3, like((devices * 4, rhs)), VMEM,
        scratch=[pltpu.VMEM((held, kc), BF16), DMA], limit=4, moved=MIB,
    )
    arrived = spread(packed.reshape(devices, 4, rhs), ALL)
    z1c = kernel_call(
        diagonal_kernel, (core, own_second, other_second, child_inverse),
        [SMEM, VMEM, VMEM, HBM], like((stripe, rhs), F32), VMEM,
        scratch=[pltpu.VMEM((stripe, kc), BF16), DMA], limit=2, moved=MIB,
    )
    arrived, z1c, lower_other, low_other, high_other, upper_other = tie(
        (arrived, z1c, lower_other, low_other, high_other, upper_other)
    )

    r0_copies, right = kernel_call(
        unpack_kernel, (core, arrived.reshape(devices * 4, rhs), kept, got), [SMEM] + [VMEM] * 3,
        [like((cubes, half, rhs)), like((half, rhs), F32)], [VMEM] * 2, limit=4, moved=MIB,
    )
    r0 = spread(r0_copies, CUBE)
    summed = build_coupling(index, child_coupling, 2 * kr)
    r0, summed = tie((r0, summed))
    whole = (cubes, half, rhs)
    r1_copies, z0_own, high_inverse, top = kernel_call(
        first_product_kernel,
        (core, r0, root_lower, root_inverse, root_upper,
         lower_other, low_other, high_other, upper_other, right),
        [SMEM, VMEM] + [HBM] * 7 + [VMEM],
        [
            like(whole),
            like((half, rhs), F32),
            pltpu.VMEM((2, stripe, kr), BF16),
            pltpu.VMEM((2, stripe, kr), BF16),
        ],
        [VMEM] * 4,
        scratch=[pltpu.VMEM((4, stripe, kr), BF16), DMA((5, 4))],
        limit=57, moved=10 * MIB,
    )
    r1_copies, summed = tie((r1_copies, summed))
    summed_other = swap(summed)
    r1 = spread(r1_copies, CUBE)
    x1_copies = product(core, r1, high_inverse, None)
    x1 = spread(x1_copies, CUBE)
    x1, summed_other = tie((x1, summed_other))
    x0_copies = product(core, x1, top, z0_own)
    x0, x0_copies, x1_copies = tie((spread(x0_copies, CUBE), x0_copies, x1_copies))

    mine, given = kernel_call(
        couple_kernel, (x0, x1, summed, summed_other), [VMEM] * 4,
        [like((half, 2 * stripe), F32)] * 2, [VMEM] * 2,
        limit=4, flops=8 * cubes * half * rhs * rhs, moved=10 * MIB,
    )
    c1_copies, rest, top_child = kernel_call(
        settle_kernel, (core, mine, swap(given), z0c, z1c, child_upper),
        [SMEM] + [VMEM] * 4 + [HBM],
        [like(piece), like((stripe, rhs), F32), pltpu.VMEM((stripe, kc), BF16)], [VMEM] * 3,
        scratch=[DMA], limit=2, moved=MIB,
    )
    c1_copies, x0_own, x1_own = tie((c1_copies, x0_copies[0], x1_copies[0]))
    own_c1 = spread(c1_copies, PLANE)

    def own_rows(half_rows):
        pair = in_core_order(half_rows, swap(half_rows), 0).reshape(rhs, 2 * stripe)
        rows = pair.T
        return jnp.where(me == 0, rows[:stripe], rows[stripe:])

    root_solution = jnp.stack([own_rows(x0_own), own_rows(x1_own)])[:, None]
    own_c1, root_solution = tie((own_c1, root_solution))
    child_solution = kernel_call(
        closing_kernel, (core, own_c1, swap(own_c1), top_child, rest, c1_copies),
        [SMEM] + [VMEM] * 5, like(child_rhs.shape), VMEM, limit=2, moved=MIB,
    )
    return child_solution, root_solution


def solution(mesh):
    leaf, front = mesh.devices.shape
    fine = Mesh(mesh.devices.reshape((leaf, 4, front // 8, 2)), ALL)
    subtree = P("y", None, ("x", "z", "c"), None, None)
    ancestor = P(None, ALL, None, None)
    in_specs = (
        subtree,
        subtree,
        subtree,
        subtree,
        subtree,
        P("y", ("x", "z", "c"), None),
        P("y", ("x", "z", "c"), None),
        P("y", ("x", "z", "c")),
        ancestor,
        ancestor,
        ancestor,
        ancestor,
    )
    return jax.shard_map(
        body, mesh=fine, in_specs=in_specs, out_specs=(subtree, ancestor), check_vma=False
    )
```

```python
import functools

import jax
import jax.numpy as jnp
from jax import lax
from jax.experimental import pallas as pl
from jax.experimental.pallas import tpu as pltpu
from jax.sharding import Mesh
from jax.sharding import PartitionSpec as P

F32 = jnp.float32
BF16 = jnp.bfloat16
ALL = ("y", "x", "z", "c")
PLANE = ("x", "z")
CUBE = ("y", "x", "z")
VMEM = pl.BlockSpec(memory_space=pltpu.VMEM)
SMEM = pl.BlockSpec(memory_space=pltpu.SMEM)
HBM = pl.BlockSpec(memory_space=pltpu.HBM)
DMA = pltpu.SemaphoreType.DMA
MIB = 1 << 20
BATCH = 8
tie = lax.optimization_barrier


def swap(array):
    return lax.ppermute(array, "c", [(0, 1), (1, 0)])


def spread(copies, axes):
    return lax.all_to_all(copies, axes, 0, 0)


def in_core_order(own, other, axis):
    first = lax.axis_index("c") == 0
    return jnp.stack([jnp.where(first, own, other), jnp.where(first, other, own)], axis=axis)


def rows_of(array, block, first, last):
    lead = array.ndim - 4
    start = (0,) * lead + (block, 0, 0, first)
    stop = (1,) * lead + (block + 1, 1, array.shape[-2], last)
    return lax.slice(array, start, stop).reshape(array.shape[-2], last - first)


def like(shape, dtype=BF16):
    return jax.ShapeDtypeStruct(shape, dtype)


def kernel_call(body, args, specs, shapes, out_specs, scratch=(), limit=None, flops=0, moved=0):
    return pl.pallas_call(
        body,
        out_shape=shapes,
        in_specs=specs,
        out_specs=out_specs,
        scratch_shapes=list(scratch),
        compiler_params=pltpu.CompilerParams(
            vmem_limit_bytes=None if limit is None else limit * MIB
        ),
        cost_estimate=pl.CostEstimate(flops=flops, bytes_accessed=moved, transcendentals=0),
    )(*args)


def by_core(core_ref, own_refs, other_refs, work):
    @pl.when(core_ref[0] == 0)
    def _():
        work(own_refs, other_refs)

    @pl.when(core_ref[0] != 0)
    def _():
        work(other_refs, own_refs)


def plane_dot(matrix_ref, first_ref, second_ref, rows):
    total = None
    for p in range(first_ref.shape[0] // 2):
        block = jnp.concatenate(
            [
                first_ref[2 * p, 0:rows],
                second_ref[2 * p, 0:rows],
                first_ref[2 * p + 1, 0:rows],
                second_ref[2 * p + 1, 0:rows],
            ],
            axis=0,
        )
        term = jnp.dot(
            matrix_ref[:, p * 4 * rows : (p + 1) * 4 * rows], block, preferred_element_type=F32
        )
        total = term if total is None else total + term
    return total


def opening_kernel(rhs_ref, owner_ref, slot_ref, out_ref):
    row = lax.broadcasted_iota(jnp.int32, (8, 128), 0)
    marks = jnp.where(row == 0, owner_ref[...], jnp.where(row == 1, slot_ref[...], 0))
    marks = marks.astype(F32).astype(BF16)
    rows = rhs_ref.shape[3]
    for j in range(out_ref.shape[0]):
        out_ref[j, 0:rows] = rhs_ref[0, 0, 0]
        out_ref[j, rows : rows + 8] = marks


def turn_kernel(core_ref, rhs_ref, lower_ref, kept_ref, given_ref, low_ref, sem):
    copy = pltpu.make_async_copy(
        lower_ref.at[0, 1, 0, :, pl.ds(0, low_ref.shape[1])], low_ref, sem
    )
    copy.start()
    both = jnp.concatenate(
        [rhs_ref[0, 0].astype(F32).T, rhs_ref[1, 0].astype(F32).T], axis=1
    ).astype(BF16)
    half = both.shape[0] // 2

    @pl.when(core_ref[0] == 0)
    def _():
        kept_ref[...] = both[:half]
        given_ref[...] = both[half:]

    @pl.when(core_ref[0] != 0)
    def _():
        kept_ref[...] = both[half:]
        given_ref[...] = both[:half]

    copy.wait()


def advance_kernel(core_ref, own_ref, other_ref, low_ref, rhs_ref, out_ref):
    rows = out_ref.shape[1]

    def work(first, second):
        total = rhs_ref[0, 1, 0].astype(F32) - plane_dot(low_ref, first, second, rows)
        value = total.astype(BF16)
        for j in range(out_ref.shape[0]):
            out_ref[j] = value

    by_core(core_ref, own_ref, other_ref, work)


def aside_kernel(
    rows, kr, core_ref, own_ref, other_ref, update_ref, inverse_ref,
    part_ref, z0_ref, index_ref, repeats_ref, low_ref, diag_ref, sems
):
    kc = low_ref.shape[1]
    copies = [
        pltpu.make_async_copy(update_ref.at[0, :, pl.ds(0, kc)], low_ref, sems.at[0]),
        pltpu.make_async_copy(inverse_ref.at[0, 0, 0], diag_ref, sems.at[1]),
    ]
    for copy in copies:
        copy.start()

    def work(first, second):
        for j in range(own_ref.shape[0]):
            for c, source in enumerate((first, second)):
                marks = source[j, rows : rows + 8].astype(F32).astype(jnp.int32)
                owner, slot = marks[0:1], marks[1:2]
                index_ref[2 * j + c : 2 * j + c + 1, :] = (
                    (slot // rows) * kr + owner * rows + slot % rows
                )
        index = index_ref[...]
        lane = lax.broadcasted_iota(jnp.int32, index.shape, 1) % BATCH
        found = jnp.zeros(index.shape, jnp.int32)
        for d in range(1, BATCH):
            again = (pltpu.roll(index, d, 1) == index) & (lane >= d)
            found = jnp.maximum(found, jnp.where(again, 1, 0))
        repeats_ref[...] = jnp.broadcast_to(
            jnp.max(found, axis=1, keepdims=True), repeats_ref.shape
        )
        copies[0].wait()
        part_ref[...] = plane_dot(low_ref, first, second, rows)
        copies[1].wait()
        z0_ref[...] = plane_dot(diag_ref, first, second, rows).astype(BF16).astype(F32)

    by_core(core_ref, own_ref, other_ref, work)


def contribute_kernel(
    core_ref, own_ref, other_ref, update_ref, part_ref, owner_ref, slot_ref, out_ref, high_ref, sem
):
    kc = high_ref.shape[1]
    copy = pltpu.make_async_copy(update_ref.at[0, :, pl.ds(kc, kc)], high_ref, sem)
    copy.start()
    rows = own_ref.shape[1]
    held = owner_ref.shape[1]
    owner = owner_ref[...].astype(F32)
    owners = jnp.broadcast_to(owner, (held, held))
    above = lax.broadcasted_iota(jnp.int32, (held, held), 0) < lax.broadcasted_iota(
        jnp.int32, (held, held), 1
    )
    same = jnp.where((owners == owners.T) & above, 1.0, 0.0)
    place = owner * 2.0 + jnp.sum(same, axis=0, keepdims=True)
    row = lax.broadcasted_iota(jnp.int32, (out_ref.shape[0], held), 0)
    wanted = (row // 8 * 4 + row % 4).astype(F32)
    select = jnp.where(wanted == place, 1.0, 0.0).astype(BF16)
    slot = slot_ref[...]
    target = slot // rows * (2 * rows) + owner_ref[...] % 2 * rows + slot % rows + 1
    targets = jnp.broadcast_to(target.astype(F32), (held, held)).T[:, :rows].astype(BF16)

    copy.wait()

    def work(first, second):
        contribution = -(part_ref[...] + plane_dot(high_ref, first, second, rows))
        contribution = contribution.astype(BF16)
        half = contribution.shape[1] // 2
        source = jnp.concatenate(
            [contribution[:, :half], targets, contribution[:, half:], targets], axis=1
        )
        both = jnp.dot(select, source, preferred_element_type=F32)
        lanes = 2 * half
        upper = lax.broadcasted_iota(jnp.int32, (both.shape[0], lanes), 0) % 8 >= 4
        out_ref[...] = jnp.where(upper, both[:, lanes:], both[:, :lanes]).astype(BF16)

    by_core(core_ref, own_ref, other_ref, work)


def diagonal_kernel(core_ref, own_ref, other_ref, inverse_ref, z1_ref, diag_ref, sem):
    copy = pltpu.make_async_copy(inverse_ref.at[0, 1, 0], diag_ref, sem)
    copy.start()
    copy.wait()

    def work(first, second):
        total = plane_dot(diag_ref, first, second, own_ref.shape[1])
        z1_ref[...] = total.astype(BF16).astype(F32)

    by_core(core_ref, own_ref, other_ref, work)


def unpack_kernel(core_ref, arrived_ref, kept_ref, got_ref, copies_ref, right_ref):
    half, lanes = right_ref.shape
    arrived = arrived_ref[...]
    code = arrived[:, half : half + 1].astype(F32)
    lane = lax.broadcasted_iota(jnp.int32, (arrived.shape[0], 2 * lanes), 1).astype(F32)
    lands = jnp.where(code == lane + 1.0, 1.0, 0.0).astype(BF16)
    received = lax.dot_general(
        arrived, lands, (((0,), (0,)), ((), ())), preferred_element_type=F32
    )[:half]

    def work(first, second):
        bases = [
            jnp.concatenate(
                [first[:, r * half : (r + 1) * half], second[:, r * half : (r + 1) * half]], axis=1
            ).astype(F32)
            for r in range(2)
        ]
        value = (bases[0] + received[:, :lanes]).astype(BF16)
        for j in range(copies_ref.shape[0]):
            copies_ref[j] = value
        right_ref[...] = bases[1] + received[:, lanes:]

    by_core(core_ref, kept_ref, got_ref, work)


def build_kernel(index_ref, repeats_ref, coupling_ref, out_ref, raw_ref, turned_ref, sums_ref, done_ref, sems):
    rows, width = sums_ref.shape
    half = width // 2
    loads = [
        pltpu.make_async_copy(
            coupling_ref.at[0, r, 0], raw_ref.at[pl.ds(r * half, half)], sems.at[r]
        )
        for r in range(2)
    ]
    for load in loads:
        load.start()

    def clear(i, carry):
        sums_ref[pl.ds(pl.multiple_of(i * 128, 128), 128), :] = jnp.zeros((128, width), F32)
        return carry

    lax.fori_loop(0, rows // 128, clear, 0, unroll=4)
    for load in loads:
        load.wait()
    for i in range(turned_ref.shape[0] // 128):
        part = slice(i * 128, (i + 1) * 128)
        turned_ref[part, :] = raw_ref[:, part].astype(F32).T

    def add_line(line, carry):
        start = pl.multiple_of(line * 128, 128)

        def add_apart(group, carry):
            base = pl.multiple_of(start + group * BATCH, BATCH)
            block = turned_ref[pl.ds(base, BATCH), :]
            at = [pl.ds(index_ref[base + j], 1) for j in range(BATCH)]
            values = [sums_ref[at[j], :] + block[j : j + 1] for j in range(BATCH)]
            for j in range(BATCH):
                sums_ref[at[j], :] = values[j]
            return carry

        def add_in_turn(group, carry):
            base = pl.multiple_of(start + group * BATCH, BATCH)
            block = turned_ref[pl.ds(base, BATCH), :]
            for j in range(BATCH):
                at = pl.ds(index_ref[base + j], 1)
                sums_ref[at, :] = sums_ref[at, :] + block[j : j + 1]
            return carry

        @pl.when(repeats_ref[line] == 0)
        def _():
            lax.fori_loop(0, 128 // BATCH, add_apart, 0, unroll=4)

        @pl.when(repeats_ref[line] != 0)
        def _():
            lax.fori_loop(0, 128 // BATCH, add_in_turn, 0)

        return carry

    lax.fori_loop(0, turned_ref.shape[0] // 128, add_line, 0)
    parts = sems.shape[0] - 2
    size = rows // parts
    stores = []
    for i in range(parts):
        part = pl.ds(i * size, size)
        done_ref[part, :] = sums_ref[part, :].astype(BF16)
        store = pltpu.make_async_copy(done_ref.at[part], out_ref.at[part], sems.at[2 + i])
        store.start()
        stores.append(store)
    for store in stores:
        store.wait()


def build_coupling(index, repeats, coupling, root_rows):
    rows, columns = 2 * coupling.shape[-2], coupling.shape[-1]
    return kernel_call(
        build_kernel,
        (index, repeats, coupling),
        [SMEM, SMEM, HBM],
        like((root_rows, rows)),
        HBM,
        scratch=[
            pltpu.VMEM((rows, columns), BF16),
            pltpu.VMEM((columns, rows), F32),
            pltpu.VMEM((root_rows, rows), F32),
            pltpu.VMEM((root_rows, rows), BF16),
            DMA((10,)),
        ],
        limit=60,
        moved=30 * MIB,
    )


def pair_dot(blocks_ref, start, stop, rights):
    lanes = blocks_ref.shape[2]
    total = None
    for i in range(start // 2, stop // 2):
        left = jnp.concatenate([blocks_ref[2 * i], blocks_ref[2 * i + 1]], axis=1)
        term = rights(left, slice(i * 2 * lanes, (i + 1) * 2 * lanes))
        total = term if total is None else total + term
    return total


def against(*parts):
    return lambda left, columns: lax.dot_general(
        left,
        jnp.concatenate([part[:, columns] for part in parts], axis=0),
        (((1,), (1,)), ((), ())),
        preferred_element_type=F32,
    )


def ordered(core_ref, total):
    return jnp.where(core_ref[0] == 0, total, pltpu.roll(total, total.shape[1] // 2, 1))


def write_copies(copies_ref, value):
    for j in range(copies_ref.shape[0]):
        copies_ref[j] = value


def first_product_kernel(
    core_ref, blocks_ref, lower_ref, other_ref, base_ref, copies_ref, held_ref, sems
):
    kr = held_ref.shape[2]
    chips = blocks_ref.shape[0]
    steps = sems.shape[0]
    width, span = kr // steps, chips // steps
    copies = []
    for i in range(steps):
        columns = pl.ds(i * width, width)
        pairs = [
            (lower_ref.at[:, columns], held_ref.at[0, :, columns]),
            (other_ref.at[:, columns], held_ref.at[1, :, columns]),
        ]
        copies.append(
            [pltpu.make_async_copy(a, b, sems.at[i, n]) for n, (a, b) in enumerate(pairs)]
        )
    for group in copies:
        for copy in group:
            copy.start()
    total = base_ref[...]
    for i, group in enumerate(copies):
        for copy in group:
            copy.wait()
        term = pair_dot(
            blocks_ref, i * span, (i + 1) * span, against(held_ref.at[0], held_ref.at[1])
        )
        total = total - ordered(core_ref, term)
    write_copies(copies_ref, total.astype(BF16))


def product_kernel(core_ref, blocks_ref, own_ref, other_ref, copies_ref):
    total = pair_dot(blocks_ref, 0, blocks_ref.shape[0], against(own_ref, other_ref))
    write_copies(copies_ref, ordered(core_ref, total).astype(BF16))


def last_product_kernel(
    core_ref, r0_ref, low_own_ref, low_other_ref, x1_ref, top_own_ref, top_other_ref, copies_ref
):
    chips = x1_ref.shape[0]
    diagonal = pair_dot(r0_ref, 0, chips, against(low_own_ref, low_other_ref))
    diagonal = diagonal.astype(BF16).astype(F32)
    total = diagonal - pair_dot(x1_ref, 0, chips, against(top_own_ref, top_other_ref))
    write_copies(copies_ref, ordered(core_ref, total).astype(BF16))


def couple_kernel(x0_ref, x1_ref, own_ref, other_ref, mine_ref, theirs_ref):
    count, half, lanes = x0_ref.shape
    total = None
    for start, blocks_ref in ((0, x0_ref), (count * lanes, x1_ref)):

        def rights(left, columns):
            rows = slice(start + columns.start, start + columns.stop)
            return jnp.dot(
                left,
                jnp.concatenate([own_ref[rows, :], other_ref[rows, :]], axis=1),
                preferred_element_type=F32,
            )

        term = pair_dot(blocks_ref, 0, count, rights)
        total = term if total is None else total + term
    width = mine_ref.shape[1]
    mine_ref[...] = total[:, :width]
    theirs_ref[...] = total[:, width:]


def settle_kernel(core_ref, mine_ref, got_ref, z0_ref, z1_ref, upper_ref,
                  copies_ref, rest_ref, top_ref, sem):
    width = top_ref.shape[1]
    copy = pltpu.make_async_copy(upper_ref.at[0, 0, 0, :, pl.ds(width, width)], top_ref, sem)
    copy.start()
    stripe = z0_ref.shape[0]

    def work(first, second):
        both = jnp.concatenate([first[...], second[...]], axis=0).T
        rest_ref[...] = z0_ref[...] - both[:stripe]
        write_copies(copies_ref, (z1_ref[...] - both[stripe:]).astype(BF16))

    by_core(core_ref, mine_ref, got_ref, work)
    copy.wait()


def closing_kernel(core_ref, own_ref, other_ref, top_ref, rest_ref, copies_ref, out_ref):
    out_ref[0, 1, 0] = copies_ref[0]

    def work(first, second):
        total = rest_ref[...] - plane_dot(top_ref, first, second, own_ref.shape[1])
        out_ref[0, 0, 0] = total.astype(BF16)

    by_core(core_ref, own_ref, other_ref, work)


def body(
    child_rhs,
    child_lower,
    child_inverse,
    child_upper,
    child_coupling,
    child_update,
    update_owner,
    update_slot,
    root_rhs,
    root_lower,
    root_inverse,
    root_upper,
):
    planes = lax.axis_size("x") * lax.axis_size("z")
    cubes = planes * lax.axis_size("y")
    devices = cubes * 2
    stripe, rhs = root_rhs.shape[2:]
    half = rhs // 2
    kc = child_inverse.shape[-1]
    kr = root_inverse.shape[-1]
    held = update_slot.shape[1]
    owner = update_owner.reshape(1, held)
    slot = update_slot
    me = lax.axis_index("c")
    core = me.astype(jnp.int32).reshape(1)
    piece = (planes, stripe, rhs)

    opened = kernel_call(
        opening_kernel, (child_rhs, owner, slot), [VMEM] * 3,
        like((planes, stripe + 8, rhs)), VMEM,
    )
    opened, root_rhs, child_lower, root_lower, root_inverse, root_upper = tie(
        (opened, root_rhs, child_lower, root_lower, root_inverse, root_upper)
    )
    own_first = spread(opened, PLANE)
    kept, given, low = kernel_call(
        turn_kernel, (core, root_rhs, child_lower), [SMEM, VMEM, HBM],
        [like((half, rhs)), like((half, rhs)), pltpu.VMEM((stripe, kc), BF16)], [VMEM] * 3,
        scratch=[DMA], limit=2, moved=MIB,
    )
    own = [
        rows_of(root_lower, 1, 0, kr),
        rows_of(root_inverse, 0, 0, kr),
        rows_of(root_inverse, 1, 0, kr),
        rows_of(root_upper, 0, kr, 2 * kr),
    ]
    own_first, own, kept, given, low = tie((own_first, own, kept, given, low))
    other_first = swap(own_first)
    y1_copies = kernel_call(
        advance_kernel, (core, own_first, other_first, low, child_rhs), [SMEM] + [VMEM] * 4,
        like(piece), VMEM, limit=2, moved=MIB,
    )
    y1_copies, own, given = tie((y1_copies, own, given))
    own_second = spread(y1_copies, PLANE)

    lower_other, low_other, high_other, upper_other = [swap(m) for m in own]
    got = swap(given)
    part, z0c, index, repeats = kernel_call(
        functools.partial(aside_kernel, stripe, kr),
        (core, own_first, other_first, child_update, child_inverse),
        [SMEM, VMEM, VMEM, HBM, HBM],
        [
            like((held, rhs), F32),
            like((stripe, rhs), F32),
            like((2 * planes, held), jnp.int32),
            like((2 * planes, held), jnp.int32),
        ],
        [VMEM] * 4,
        scratch=[pltpu.VMEM((held, kc), BF16), pltpu.VMEM((stripe, kc), BF16), DMA((2,))],
        limit=4, moved=2 * MIB,
    )
    index, repeats = index.reshape(-1), repeats[:, 0]
    own_second, part, z0c, index, repeats, got = tie(
        (own_second, part, z0c, index, repeats, got)
    )
    other_second = swap(own_second)

    packed = kernel_call(
        contribute_kernel, (core, own_second, other_second, child_update, part, owner, slot),
        [SMEM, VMEM, VMEM, HBM] + [VMEM] * 3, like((devices * 4, rhs)), VMEM,
        scratch=[pltpu.VMEM((held, kc), BF16), DMA], limit=4, moved=MIB,
    )
    arrived = spread(packed.reshape(devices, 4, rhs), ALL)
    z1c = kernel_call(
        diagonal_kernel, (core, own_second, other_second, child_inverse),
        [SMEM, VMEM, VMEM, HBM], like((stripe, rhs), F32), VMEM,
        scratch=[pltpu.VMEM((stripe, kc), BF16), DMA], limit=2, moved=MIB,
    )
    arrived, z1c, lower_other, low_other, high_other, upper_other = tie(
        (arrived, z1c, lower_other, low_other, high_other, upper_other)
    )

    r0_copies, right = kernel_call(
        unpack_kernel, (core, arrived.reshape(devices * 4, rhs), kept, got), [SMEM] + [VMEM] * 3,
        [like((cubes, half, rhs)), like((half, rhs), F32)], [VMEM] * 2, limit=4, moved=MIB,
    )
    r0 = spread(r0_copies, CUBE)
    summed = build_coupling(index, repeats, child_coupling, 2 * kr)
    summed_other = swap(summed)
    r0, summed = tie((r0, summed))
    whole = (cubes, half, rhs)
    r1_copies = kernel_call(
        first_product_kernel, (core, r0, own[0], lower_other, right),
        [SMEM, VMEM, HBM, HBM, VMEM], like(whole), VMEM,
        scratch=[pltpu.VMEM((2, stripe, kr), BF16), DMA((4, 2))], limit=50, moved=4 * MIB,
    )
    r1 = spread(r1_copies, CUBE)
    x1_copies = kernel_call(
        product_kernel, (core, r1, own[2], high_other), [SMEM] + [VMEM] * 3, like(whole), VMEM,
        limit=4, flops=2 * cubes * half * rhs * rhs, moved=4 * MIB,
    )
    x1 = spread(x1_copies, CUBE)
    x1, summed_other = tie((x1, summed_other))
    x0_copies = kernel_call(
        last_product_kernel, (core, r0, own[1], low_other, x1, own[3], upper_other),
        [SMEM] + [VMEM] * 6, like(whole), VMEM,
        limit=4, flops=4 * cubes * half * rhs * rhs, moved=7 * MIB,
    )
    x0, x0_copies, x1_copies = tie((spread(x0_copies, CUBE), x0_copies, x1_copies))

    mine, given = kernel_call(
        couple_kernel, (x0, x1, summed, summed_other), [VMEM] * 4,
        [like((half, 2 * stripe), F32)] * 2, [VMEM] * 2,
        limit=4, flops=8 * cubes * half * rhs * rhs, moved=10 * MIB,
    )
    c1_copies, rest, top_child = kernel_call(
        settle_kernel, (core, mine, swap(given), z0c, z1c, child_upper),
        [SMEM] + [VMEM] * 4 + [HBM],
        [like(piece), like((stripe, rhs), F32), pltpu.VMEM((stripe, kc), BF16)], [VMEM] * 3,
        scratch=[DMA], limit=2, moved=MIB,
    )
    c1_copies, x0_own, x1_own = tie((c1_copies, x0_copies[0], x1_copies[0]))
    own_c1 = spread(c1_copies, PLANE)

    def own_rows(half_rows):
        pair = in_core_order(half_rows, swap(half_rows), 0).reshape(rhs, 2 * stripe)
        rows = pair.T
        return jnp.where(me == 0, rows[:stripe], rows[stripe:])

    root_solution = jnp.stack([own_rows(x0_own), own_rows(x1_own)])[:, None]
    own_c1, root_solution = tie((own_c1, root_solution))
    child_solution = kernel_call(
        closing_kernel, (core, own_c1, swap(own_c1), top_child, rest, c1_copies),
        [SMEM] + [VMEM] * 5, like(child_rhs.shape), VMEM, limit=2, moved=MIB,
    )
    return child_solution, root_solution


def solution(mesh):
    leaf, front = mesh.devices.shape
    fine = Mesh(mesh.devices.reshape((leaf, 4, front // 8, 2)), ALL)
    subtree = P("y", None, ("x", "z", "c"), None, None)
    ancestor = P(None, ALL, None, None)
    in_specs = (
        subtree,
        subtree,
        subtree,
        subtree,
        subtree,
        P("y", ("x", "z", "c"), None),
        P("y", ("x", "z", "c"), None),
        P("y", ("x", "z", "c")),
        ancestor,
        ancestor,
        ancestor,
        ancestor,
    )
    return jax.shard_map(
        body, mesh=fine, in_specs=in_specs, out_specs=(subtree, ancestor), check_vma=False
    )
```

```python
import functools

import jax
import jax.numpy as jnp
from jax import lax
from jax.experimental import pallas as pl
from jax.experimental.pallas import tpu as pltpu
from jax.sharding import Mesh
from jax.sharding import PartitionSpec as P

F32 = jnp.float32
BF16 = jnp.bfloat16
ALL = ("y", "x", "z", "c")
PLANE = ("x", "z")
CUBE = ("y", "x", "z")
VMEM = pl.BlockSpec(memory_space=pltpu.VMEM)
SMEM = pl.BlockSpec(memory_space=pltpu.SMEM)
HBM = pl.BlockSpec(memory_space=pltpu.HBM)
DMA = pltpu.SemaphoreType.DMA
MIB = 1 << 20
BATCH = 8
tie = lax.optimization_barrier


def swap(array):
    return lax.ppermute(array, "c", [(0, 1), (1, 0)])


def spread(copies, axes):
    return lax.all_to_all(copies, axes, 0, 0)


def in_core_order(own, other, axis):
    first = lax.axis_index("c") == 0
    return jnp.stack([jnp.where(first, own, other), jnp.where(first, other, own)], axis=axis)


def rows_of(array, block, first, last):
    lead = array.ndim - 4
    start = (0,) * lead + (block, 0, 0, first)
    stop = (1,) * lead + (block + 1, 1, array.shape[-2], last)
    return lax.slice(array, start, stop).reshape(array.shape[-2], last - first)


def like(shape, dtype=BF16):
    return jax.ShapeDtypeStruct(shape, dtype)


def kernel_call(body, args, specs, shapes, out_specs, scratch=(), limit=None, flops=0, moved=0):
    return pl.pallas_call(
        body,
        out_shape=shapes,
        in_specs=specs,
        out_specs=out_specs,
        scratch_shapes=list(scratch),
        compiler_params=pltpu.CompilerParams(
            vmem_limit_bytes=None if limit is None else limit * MIB
        ),
        cost_estimate=pl.CostEstimate(flops=flops, bytes_accessed=moved, transcendentals=0),
    )(*args)


def by_core(core_ref, own_refs, other_refs, work):
    @pl.when(core_ref[0] == 0)
    def _():
        work(own_refs, other_refs)

    @pl.when(core_ref[0] != 0)
    def _():
        work(other_refs, own_refs)


def plane_dot(matrix_ref, first_ref, second_ref, rows):
    total = None
    for p in range(first_ref.shape[0] // 2):
        block = jnp.concatenate(
            [
                first_ref[2 * p, 0:rows],
                second_ref[2 * p, 0:rows],
                first_ref[2 * p + 1, 0:rows],
                second_ref[2 * p + 1, 0:rows],
            ],
            axis=0,
        )
        term = jnp.dot(
            matrix_ref[:, p * 4 * rows : (p + 1) * 4 * rows], block, preferred_element_type=F32
        )
        total = term if total is None else total + term
    return total


def opening_kernel(rhs_ref, owner_ref, slot_ref, out_ref):
    row = lax.broadcasted_iota(jnp.int32, (8, 128), 0)
    marks = jnp.where(row == 0, owner_ref[...], jnp.where(row == 1, slot_ref[...], 0))
    marks = marks.astype(F32).astype(BF16)
    rows = rhs_ref.shape[3]
    for j in range(out_ref.shape[0]):
        out_ref[j, 0:rows] = rhs_ref[0, 0, 0]
        out_ref[j, rows : rows + 8] = marks


def turn_kernel(core_ref, rhs_ref, kept_ref, given_ref):
    both = jnp.concatenate(
        [rhs_ref[0, 0].astype(F32).T, rhs_ref[1, 0].astype(F32).T], axis=1
    ).astype(BF16)
    half = both.shape[0] // 2

    @pl.when(core_ref[0] == 0)
    def _():
        kept_ref[...] = both[:half]
        given_ref[...] = both[half:]

    @pl.when(core_ref[0] != 0)
    def _():
        kept_ref[...] = both[half:]
        given_ref[...] = both[:half]


def extract_kernel(lower_ref, inverse_ref, upper_ref, out_ref, sems):
    kr = out_ref.shape[2]
    copies = [
        pltpu.make_async_copy(lower_ref.at[1, 0, :, pl.ds(0, kr)], out_ref.at[0], sems.at[0]),
        pltpu.make_async_copy(inverse_ref.at[1, 0], out_ref.at[1], sems.at[1]),
        pltpu.make_async_copy(inverse_ref.at[0, 0], out_ref.at[2], sems.at[2]),
        pltpu.make_async_copy(upper_ref.at[0, 0, :, pl.ds(kr, kr)], out_ref.at[3], sems.at[3]),
    ]
    for copy in copies:
        copy.start()
    for copy in copies:
        copy.wait()


def advance_kernel(core_ref, own_ref, other_ref, low_ref, rhs_ref, out_ref):
    rows = out_ref.shape[1]

    def work(first, second):
        total = rhs_ref[0, 1, 0].astype(F32) - plane_dot(low_ref, first, second, rows)
        value = total.astype(BF16)
        for j in range(out_ref.shape[0]):
            out_ref[j] = value

    by_core(core_ref, own_ref, other_ref, work)


def aside_kernel(
    rows, kr, core_ref, own_ref, other_ref, update_ref, inverse_ref, owner_ref, slot_ref,
    part_ref, z0_ref, index_ref, repeats_ref, select_ref, targets_ref, low_ref, diag_ref, sems
):
    kc = low_ref.shape[1]
    copies = [
        pltpu.make_async_copy(update_ref.at[0, :, pl.ds(0, kc)], low_ref, sems.at[0]),
        pltpu.make_async_copy(inverse_ref.at[0, 0, 0], diag_ref, sems.at[1]),
    ]
    for copy in copies:
        copy.start()

    held = owner_ref.shape[1]
    owner = owner_ref[...].astype(F32)
    owners = jnp.broadcast_to(owner, (held, held))
    above = lax.broadcasted_iota(jnp.int32, (held, held), 0) < lax.broadcasted_iota(
        jnp.int32, (held, held), 1
    )
    same = jnp.where((owners == owners.T) & above, 1.0, 0.0)
    place = owner * 2.0 + jnp.sum(same, axis=0, keepdims=True)
    row = lax.broadcasted_iota(jnp.int32, (select_ref.shape[0], held), 0)
    wanted = (row // 8 * 4 + row % 4).astype(F32)
    select_ref[...] = jnp.where(wanted == place, 1.0, 0.0).astype(BF16)
    slot = slot_ref[...]
    target = slot // rows * (2 * rows) + owner_ref[...] % 2 * rows + slot % rows + 1
    targets_ref[...] = jnp.broadcast_to(target.astype(F32), (held, held)).T.astype(BF16)


    def work(first, second):
        for j in range(own_ref.shape[0]):
            for c, source in enumerate((first, second)):
                marks = source[j, rows : rows + 8].astype(F32).astype(jnp.int32)
                owner, slot = marks[0:1], marks[1:2]
                index_ref[2 * j + c : 2 * j + c + 1, :] = (
                    (slot // rows) * kr + owner * rows + slot % rows
                )
        index = index_ref[...]
        lane = lax.broadcasted_iota(jnp.int32, index.shape, 1) % BATCH
        found = jnp.zeros(index.shape, jnp.int32)
        for d in range(1, BATCH):
            again = (pltpu.roll(index, d, 1) == index) & (lane >= d)
            found = jnp.maximum(found, jnp.where(again, 1, 0))
        repeats_ref[...] = jnp.broadcast_to(
            jnp.max(found, axis=1, keepdims=True), repeats_ref.shape
        )
        copies[0].wait()
        part_ref[...] = plane_dot(low_ref, first, second, rows)
        copies[1].wait()
        z0_ref[...] = plane_dot(diag_ref, first, second, rows).astype(BF16).astype(F32)

    by_core(core_ref, own_ref, other_ref, work)


def contribute_kernel(
    core_ref, own_ref, other_ref, update_ref, inverse_ref, part_ref, select_ref, targets_ref,
    out_ref, z1_ref, high_ref, diag_ref, sems
):
    kc = high_ref.shape[1]
    load = pltpu.make_async_copy(update_ref.at[0, :, pl.ds(kc, kc)], high_ref, sems.at[0])
    later = pltpu.make_async_copy(inverse_ref.at[0, 1, 0], diag_ref, sems.at[1])
    load.start()
    later.start()
    rows = own_ref.shape[1]
    load.wait()

    def work(first, second):
        contribution = -(part_ref[...] + plane_dot(high_ref, first, second, rows))
        contribution = contribution.astype(BF16)
        half = contribution.shape[1] // 2
        targets = targets_ref[:, :half]
        source = jnp.concatenate(
            [contribution[:, :half], targets, contribution[:, half:], targets], axis=1
        )
        both = jnp.dot(select_ref[...], source, preferred_element_type=F32)
        lanes = 2 * half
        upper = lax.broadcasted_iota(jnp.int32, (both.shape[0], lanes), 0) % 8 >= 4
        out_ref[...] = jnp.where(upper, both[:, lanes:], both[:, :lanes]).astype(BF16)
        later.wait()
        z1_ref[...] = plane_dot(diag_ref, first, second, rows).astype(BF16).astype(F32)

    by_core(core_ref, own_ref, other_ref, work)


def unpack_kernel(core_ref, arrived_ref, kept_ref, got_ref, copies_ref, right_ref):
    half, lanes = right_ref.shape
    arrived = arrived_ref[...]
    code = arrived[:, half : half + 1].astype(F32)
    lane = lax.broadcasted_iota(jnp.int32, (arrived.shape[0], 2 * lanes), 1).astype(F32)
    lands = jnp.where(code == lane + 1.0, 1.0, 0.0).astype(BF16)
    received = lax.dot_general(
        arrived, lands, (((0,), (0,)), ((), ())), preferred_element_type=F32
    )[:half]

    def work(first, second):
        bases = [
            jnp.concatenate(
                [first[:, r * half : (r + 1) * half], second[:, r * half : (r + 1) * half]], axis=1
            ).astype(F32)
            for r in range(2)
        ]
        value = (bases[0] + received[:, :lanes]).astype(BF16)
        for j in range(copies_ref.shape[0]):
            copies_ref[j] = value
        right_ref[...] = bases[1] + received[:, lanes:]

    by_core(core_ref, kept_ref, got_ref, work)


def build_kernel(index_ref, repeats_ref, coupling_ref, out_ref, raw_ref, turned_ref, sums_ref, done_ref, sems):
    rows, width = sums_ref.shape
    half = width // 2
    loads = [
        pltpu.make_async_copy(
            coupling_ref.at[0, r, 0], raw_ref.at[pl.ds(r * half, half)], sems.at[r]
        )
        for r in range(2)
    ]
    for load in loads:
        load.start()

    def clear(i, carry):
        sums_ref[pl.ds(pl.multiple_of(i * 128, 128), 128), :] = jnp.zeros((128, width), F32)
        return carry

    lax.fori_loop(0, rows // 128, clear, 0, unroll=4)
    for load in loads:
        load.wait()
    for i in range(turned_ref.shape[0] // 128):
        part = slice(i * 128, (i + 1) * 128)
        turned_ref[part, :] = raw_ref[:, part].astype(F32).T

    def add_line(line, carry):
        start = pl.multiple_of(line * 128, 128)

        def add_apart(group, carry):
            base = pl.multiple_of(start + group * BATCH, BATCH)
            block = turned_ref[pl.ds(base, BATCH), :]
            at = [pl.ds(index_ref[base + j], 1) for j in range(BATCH)]
            values = [sums_ref[at[j], :] + block[j : j + 1] for j in range(BATCH)]
            for j in range(BATCH):
                sums_ref[at[j], :] = values[j]
            return carry

        def add_in_turn(group, carry):
            base = pl.multiple_of(start + group * BATCH, BATCH)
            block = turned_ref[pl.ds(base, BATCH), :]
            for j in range(BATCH):
                at = pl.ds(index_ref[base + j], 1)
                sums_ref[at, :] = sums_ref[at, :] + block[j : j + 1]
            return carry

        @pl.when(repeats_ref[line] == 0)
        def _():
            lax.fori_loop(0, 128 // BATCH, add_apart, 0, unroll=4)

        @pl.when(repeats_ref[line] != 0)
        def _():
            lax.fori_loop(0, 128 // BATCH, add_in_turn, 0)

        return carry

    lax.fori_loop(0, turned_ref.shape[0] // 128, add_line, 0)
    parts = sems.shape[0] - 2
    size = rows // parts
    stores = []
    for i in range(parts):
        part = pl.ds(i * size, size)
        done_ref[part, :] = sums_ref[part, :].astype(BF16)
        store = pltpu.make_async_copy(done_ref.at[part], out_ref.at[part], sems.at[2 + i])
        store.start()
        stores.append(store)
    for store in stores:
        store.wait()


def build_coupling(index, repeats, coupling, root_rows):
    rows, columns = 2 * coupling.shape[-2], coupling.shape[-1]
    return kernel_call(
        build_kernel,
        (index, repeats, coupling),
        [SMEM, SMEM, HBM],
        like((root_rows, rows)),
        HBM,
        scratch=[
            pltpu.VMEM((rows, columns), BF16),
            pltpu.VMEM((columns, rows), F32),
            pltpu.VMEM((root_rows, rows), F32),
            pltpu.VMEM((root_rows, rows), BF16),
            DMA((10,)),
        ],
        limit=60,
        moved=30 * MIB,
    )


def pair_dot(blocks_ref, start, stop, rights):
    lanes = blocks_ref.shape[2]
    total = None
    for i in range(start // 2, stop // 2):
        left = jnp.concatenate([blocks_ref[2 * i], blocks_ref[2 * i + 1]], axis=1)
        term = rights(left, slice(i * 2 * lanes, (i + 1) * 2 * lanes))
        total = term if total is None else total + term
    return total


def against(*parts):
    return lambda left, columns: lax.dot_general(
        left,
        jnp.concatenate([part[:, columns] for part in parts], axis=0),
        (((1,), (1,)), ((), ())),
        preferred_element_type=F32,
    )


def ordered(core_ref, total):
    return jnp.where(core_ref[0] == 0, total, pltpu.roll(total, total.shape[1] // 2, 1))


def write_copies(copies_ref, value):
    for j in range(copies_ref.shape[0]):
        copies_ref[j] = value


def product_kernel(which, subtract, core_ref, blocks_ref, own_ref, other_ref, *refs):
    copies_ref = refs[-1]
    rights = against(own_ref.at[which], other_ref.at[which])
    total = ordered(core_ref, pair_dot(blocks_ref, 0, blocks_ref.shape[0], rights))
    if subtract:
        total = refs[0][...] - total
    write_copies(copies_ref, total.astype(BF16))


def last_product_kernel(core_ref, r0_ref, x1_ref, own_ref, other_ref, copies_ref):
    chips = x1_ref.shape[0]
    diagonal = pair_dot(r0_ref, 0, chips, against(own_ref.at[2], other_ref.at[2]))
    diagonal = diagonal.astype(BF16).astype(F32)
    total = diagonal - pair_dot(x1_ref, 0, chips, against(own_ref.at[3], other_ref.at[3]))
    write_copies(copies_ref, ordered(core_ref, total).astype(BF16))


def couple_kernel(x0_ref, x1_ref, own_ref, other_ref, mine_ref, theirs_ref):
    count, half, lanes = x0_ref.shape
    total = None
    for start, blocks_ref in ((0, x0_ref), (count * lanes, x1_ref)):

        def rights(left, columns):
            rows = slice(start + columns.start, start + columns.stop)
            return jnp.dot(
                left,
                jnp.concatenate([own_ref[rows, :], other_ref[rows, :]], axis=1),
                preferred_element_type=F32,
            )

        term = pair_dot(blocks_ref, 0, count, rights)
        total = term if total is None else total + term
    width = mine_ref.shape[1]
    mine_ref[...] = total[:, :width]
    theirs_ref[...] = total[:, width:]


def settle_kernel(core_ref, mine_ref, got_ref, z0_ref, z1_ref, copies_ref, rest_ref):
    stripe = z0_ref.shape[0]

    def work(first, second):
        both = jnp.concatenate([first[...], second[...]], axis=0).T
        rest_ref[...] = z0_ref[...] - both[:stripe]
        write_copies(copies_ref, (z1_ref[...] - both[stripe:]).astype(BF16))

    by_core(core_ref, mine_ref, got_ref, work)


def closing_kernel(core_ref, own_ref, other_ref, top_ref, rest_ref, copies_ref, out_ref):
    out_ref[0, 1, 0] = copies_ref[0]

    def work(first, second):
        total = rest_ref[...] - plane_dot(top_ref, first, second, own_ref.shape[1])
        out_ref[0, 0, 0] = total.astype(BF16)

    by_core(core_ref, own_ref, other_ref, work)


def body(
    child_rhs,
    child_lower,
    child_inverse,
    child_upper,
    child_coupling,
    child_update,
    update_owner,
    update_slot,
    root_rhs,
    root_lower,
    root_inverse,
    root_upper,
):
    planes = lax.axis_size("x") * lax.axis_size("z")
    cubes = planes * lax.axis_size("y")
    devices = cubes * 2
    stripe, rhs = root_rhs.shape[2:]
    half = rhs // 2
    kc = child_inverse.shape[-1]
    kr = root_inverse.shape[-1]
    nc = child_lower.shape[-1]
    held = update_slot.shape[1]
    owner = update_owner.reshape(1, held)
    slot = update_slot
    me = lax.axis_index("c")
    core = me.astype(jnp.int32).reshape(1)
    piece = (planes, stripe, rhs)

    opened = kernel_call(
        opening_kernel, (child_rhs, owner, slot), [VMEM] * 3,
        like((planes, stripe + 8, rhs)), VMEM,
    )
    opened, root_rhs, root_lower, root_inverse, root_upper, child_lower, child_upper = tie(
        (opened, root_rhs, root_lower, root_inverse, root_upper, child_lower, child_upper)
    )
    own_first = spread(opened, PLANE)
    kept, given = kernel_call(
        turn_kernel, (core, root_rhs), [SMEM, VMEM], [like((half, rhs))] * 2, [VMEM] * 2,
        limit=2, moved=MIB,
    )
    low = rows_of(child_lower, 1, 0, kc)
    top = rows_of(child_upper, 0, kc, nc)
    own = kernel_call(
        extract_kernel, (root_lower, root_inverse, root_upper), [HBM] * 3,
        like((4, stripe, kr)), HBM, scratch=[DMA((4,))], limit=62, moved=8 * MIB,
    )
    own_first, own, kept, given, low, top = tie((own_first, own, kept, given, low, top))
    other_first = swap(own_first)
    y1_copies = kernel_call(
        advance_kernel, (core, own_first, other_first, low, child_rhs), [SMEM] + [VMEM] * 4,
        like(piece), VMEM, limit=2, moved=MIB,
    )
    y1_copies, own, given = tie((y1_copies, own, given))
    own_second = spread(y1_copies, PLANE)

    part, z0c, index, repeats, select, targets = kernel_call(
        functools.partial(aside_kernel, stripe, kr),
        (core, own_first, other_first, child_update, child_inverse, owner, slot),
        [SMEM, VMEM, VMEM, HBM, HBM, VMEM, VMEM],
        [
            like((held, rhs), F32),
            like((stripe, rhs), F32),
            like((2 * planes, held), jnp.int32),
            like((2 * planes, held), jnp.int32),
            like((devices * 4, held)),
            like((held, held)),
        ],
        [VMEM] * 6,
        scratch=[pltpu.VMEM((held, kc), BF16), pltpu.VMEM((stripe, kc), BF16), DMA((2,))],
        limit=4, moved=2 * MIB,
    )
    index, repeats = index.reshape(-1), repeats[:, 0]
    got = swap(given)
    own_second, part, z0c, index, repeats, select, targets, got = tie(
        (own_second, part, z0c, index, repeats, select, targets, got)
    )
    other_second = swap(own_second)

    packed, z1c = kernel_call(
        contribute_kernel,
        (core, own_second, other_second, child_update, child_inverse, part, select, targets),
        [SMEM, VMEM, VMEM, HBM, HBM] + [VMEM] * 3,
        [like((devices * 4, rhs)), like((stripe, rhs), F32)], [VMEM] * 2,
        scratch=[pltpu.VMEM((held, kc), BF16), pltpu.VMEM((stripe, kc), BF16), DMA((2,))],
        limit=4, moved=MIB,
    )
    packed, z1c, index, repeats = tie((packed, z1c, index, repeats))
    arrived = spread(packed.reshape(devices, 4, rhs), ALL)
    summed = build_coupling(index, repeats, child_coupling, 2 * kr)
    arrived, summed, own = tie((arrived, summed, own))

    r0_copies, right = kernel_call(
        unpack_kernel, (core, arrived.reshape(devices * 4, rhs), kept, got), [SMEM] + [VMEM] * 3,
        [like((cubes, half, rhs)), like((half, rhs), F32)], [VMEM] * 2, limit=4, moved=MIB,
    )
    other = swap(own)
    whole = (cubes, half, rhs)
    work = dict(limit=4, flops=2 * cubes * half * rhs * rhs, moved=4 * MIB)
    r0, other = tie((spread(r0_copies, CUBE), other))
    r1_copies = kernel_call(
        functools.partial(product_kernel, 0, True), (core, r0, own, other, right),
        [SMEM] + [VMEM] * 4, like(whole), VMEM, **work,
    )
    r1_copies, summed = tie((r1_copies, summed))
    summed_other = swap(summed)
    r1 = spread(r1_copies, CUBE)
    x1_copies = kernel_call(
        functools.partial(product_kernel, 1, False), (core, r1, own, other),
        [SMEM] + [VMEM] * 3, like(whole), VMEM, **work,
    )
    x1 = spread(x1_copies, CUBE)
    x1, summed_other = tie((x1, summed_other))
    x0_copies = kernel_call(
        last_product_kernel, (core, r0, x1, own, other), [SMEM] + [VMEM] * 4,
        like(whole), VMEM, **work,
    )
    x0, x0_copies, x1_copies = tie((spread(x0_copies, CUBE), x0_copies, x1_copies))

    mine, given = kernel_call(
        couple_kernel, (x0, x1, summed, summed_other), [VMEM] * 4,
        [like((half, 2 * stripe), F32)] * 2, [VMEM] * 2,
        limit=4, flops=8 * cubes * half * rhs * rhs, moved=10 * MIB,
    )
    c1_copies, rest = kernel_call(
        settle_kernel, (core, mine, swap(given), z0c, z1c), [SMEM] + [VMEM] * 4,
        [like(piece), like((stripe, rhs), F32)], [VMEM] * 2, limit=2, moved=MIB,
    )
    c1_copies, x0_own, x1_own = tie((c1_copies, x0_copies[0], x1_copies[0]))
    own_c1 = spread(c1_copies, PLANE)

    def own_rows(half_rows):
        pair = in_core_order(half_rows, swap(half_rows), 0).reshape(rhs, 2 * stripe)
        rows = pair.T
        return jnp.where(me == 0, rows[:stripe], rows[stripe:])

    root_solution = jnp.stack([own_rows(x0_own), own_rows(x1_own)])[:, None]
    own_c1, root_solution = tie((own_c1, root_solution))
    child_solution = kernel_call(
        closing_kernel, (core, own_c1, swap(own_c1), top, rest, c1_copies),
        [SMEM] + [VMEM] * 5, like(child_rhs.shape), VMEM, limit=2, moved=MIB,
    )
    return child_solution, root_solution


def solution(mesh):
    leaf, front = mesh.devices.shape
    fine = Mesh(mesh.devices.reshape((leaf, 4, front // 8, 2)), ALL)
    subtree = P("y", None, ("x", "z", "c"), None, None)
    ancestor = P(None, ALL, None, None)
    in_specs = (
        subtree,
        subtree,
        subtree,
        subtree,
        subtree,
        P("y", ("x", "z", "c"), None),
        P("y", ("x", "z", "c"), None),
        P("y", ("x", "z", "c")),
        ancestor,
        ancestor,
        ancestor,
        ancestor,
    )
    return jax.shard_map(
        body, mesh=fine, in_specs=in_specs, out_specs=(subtree, ancestor), check_vma=False
    )
```

```python
import functools

import jax
import jax.numpy as jnp
from jax import lax
from jax.experimental import pallas as pl
from jax.experimental.pallas import tpu as pltpu
from jax.sharding import Mesh
from jax.sharding import PartitionSpec as P

F32 = jnp.float32
BF16 = jnp.bfloat16
ALL = ("y", "x", "z", "c")
PLANE = ("x", "z")
CUBE = ("y", "x", "z")
VMEM = pl.BlockSpec(memory_space=pltpu.VMEM)
SMEM = pl.BlockSpec(memory_space=pltpu.SMEM)
HBM = pl.BlockSpec(memory_space=pltpu.HBM)
DMA = pltpu.SemaphoreType.DMA
MIB = 1 << 20
FIRST = 50
BATCH = 8
tie = lax.optimization_barrier


def swap(array):
    return lax.ppermute(array, "c", [(0, 1), (1, 0)])


def spread(copies, axes):
    return lax.all_to_all(copies, axes, 0, 0)


def in_core_order(own, other, axis):
    first = lax.axis_index("c") == 0
    return jnp.stack([jnp.where(first, own, other), jnp.where(first, other, own)], axis=axis)


def rows_of(array, block, first, last):
    lead = array.ndim - 4
    start = (0,) * lead + (block, 0, 0, first)
    stop = (1,) * lead + (block + 1, 1, array.shape[-2], last)
    return lax.slice(array, start, stop).reshape(array.shape[-2], last - first)


def like(shape, dtype=BF16):
    return jax.ShapeDtypeStruct(shape, dtype)


def kernel_call(body, args, specs, shapes, out_specs, scratch=(), limit=None, flops=0, moved=0):
    return pl.pallas_call(
        body,
        out_shape=shapes,
        in_specs=specs,
        out_specs=out_specs,
        scratch_shapes=list(scratch),
        compiler_params=pltpu.CompilerParams(
            vmem_limit_bytes=None if limit is None else limit * MIB
        ),
        cost_estimate=pl.CostEstimate(flops=flops, bytes_accessed=moved, transcendentals=0),
    )(*args)


def by_core(core_ref, own_refs, other_refs, work):
    @pl.when(core_ref[0] == 0)
    def _():
        work(own_refs, other_refs)

    @pl.when(core_ref[0] != 0)
    def _():
        work(other_refs, own_refs)


def plane_dot(matrix_ref, first_ref, second_ref, rows):
    total = None
    for p in range(first_ref.shape[0] // 2):
        block = jnp.concatenate(
            [
                first_ref[2 * p, 0:rows],
                second_ref[2 * p, 0:rows],
                first_ref[2 * p + 1, 0:rows],
                second_ref[2 * p + 1, 0:rows],
            ],
            axis=0,
        )
        term = jnp.dot(
            matrix_ref[:, p * 4 * rows : (p + 1) * 4 * rows], block, preferred_element_type=F32
        )
        total = term if total is None else total + term
    return total


def opening_kernel(rhs_ref, owner_ref, slot_ref, out_ref):
    row = lax.broadcasted_iota(jnp.int32, (8, 128), 0)
    marks = jnp.where(row == 0, owner_ref[...], jnp.where(row == 1, slot_ref[...], 0))
    marks = marks.astype(F32).astype(BF16)
    rows = rhs_ref.shape[3]
    for j in range(out_ref.shape[0]):
        out_ref[j, 0:rows] = rhs_ref[0, 0, 0]
        out_ref[j, rows : rows + 8] = marks


def turn_kernel(core_ref, rhs_ref, kept_ref, given_ref):
    both = jnp.concatenate(
        [rhs_ref[0, 0].astype(F32).T, rhs_ref[1, 0].astype(F32).T], axis=1
    ).astype(BF16)
    half = both.shape[0] // 2

    @pl.when(core_ref[0] == 0)
    def _():
        kept_ref[...] = both[:half]
        given_ref[...] = both[half:]

    @pl.when(core_ref[0] != 0)
    def _():
        kept_ref[...] = both[half:]
        given_ref[...] = both[:half]


def advance_kernel(core_ref, own_ref, other_ref, low_ref, rhs_ref, out_ref):
    rows = out_ref.shape[1]

    def work(first, second):
        total = rhs_ref[0, 1, 0].astype(F32) - plane_dot(low_ref, first, second, rows)
        value = total.astype(BF16)
        for j in range(out_ref.shape[0]):
            out_ref[j] = value

    by_core(core_ref, own_ref, other_ref, work)


def aside_kernel(
    rows, kr, core_ref, own_ref, other_ref, update_ref, inverse_ref, owner_ref, slot_ref,
    part_ref, z0_ref, index_ref, repeats_ref, select_ref, targets_ref, low_ref, diag_ref, sems
):
    kc = low_ref.shape[1]
    copies = [
        pltpu.make_async_copy(update_ref.at[0, :, pl.ds(0, kc)], low_ref, sems.at[0]),
        pltpu.make_async_copy(inverse_ref.at[0, 0, 0], diag_ref, sems.at[1]),
    ]
    for copy in copies:
        copy.start()

    held = owner_ref.shape[1]
    owner = owner_ref[...].astype(F32)
    owners = jnp.broadcast_to(owner, (held, held))
    above = lax.broadcasted_iota(jnp.int32, (held, held), 0) < lax.broadcasted_iota(
        jnp.int32, (held, held), 1
    )
    same = jnp.where((owners == owners.T) & above, 1.0, 0.0)
    place = owner * 2.0 + jnp.sum(same, axis=0, keepdims=True)
    row = lax.broadcasted_iota(jnp.int32, (select_ref.shape[0], held), 0)
    wanted = (row // 8 * 4 + row % 4).astype(F32)
    select_ref[...] = jnp.where(wanted == place, 1.0, 0.0).astype(BF16)
    slot = slot_ref[...]
    target = slot // rows * (2 * rows) + owner_ref[...] % 2 * rows + slot % rows + 1
    targets_ref[...] = jnp.broadcast_to(target.astype(F32), (held, held)).T.astype(BF16)


    def work(first, second):
        for j in range(own_ref.shape[0]):
            for c, source in enumerate((first, second)):
                marks = source[j, rows : rows + 8].astype(F32).astype(jnp.int32)
                owner, slot = marks[0:1], marks[1:2]
                index_ref[2 * j + c : 2 * j + c + 1, :] = (
                    (slot // rows) * kr + owner * rows + slot % rows
                )
        index = index_ref[...]
        lane = lax.broadcasted_iota(jnp.int32, index.shape, 1) % BATCH
        found = jnp.zeros(index.shape, jnp.int32)
        for d in range(1, BATCH):
            again = (pltpu.roll(index, d, 1) == index) & (lane >= d)
            found = jnp.maximum(found, jnp.where(again, 1, 0))
        repeats_ref[...] = jnp.broadcast_to(
            jnp.max(found, axis=1, keepdims=True), repeats_ref.shape
        )
        copies[0].wait()
        part_ref[...] = plane_dot(low_ref, first, second, rows)
        copies[1].wait()
        z0_ref[...] = plane_dot(diag_ref, first, second, rows).astype(BF16).astype(F32)

    by_core(core_ref, own_ref, other_ref, work)


def contribute_kernel(
    core_ref, own_ref, other_ref, update_ref, inverse_ref, part_ref, select_ref, targets_ref,
    out_ref, z1_ref, high_ref, diag_ref, sems
):
    kc = high_ref.shape[1]
    load = pltpu.make_async_copy(update_ref.at[0, :, pl.ds(kc, kc)], high_ref, sems.at[0])
    later = pltpu.make_async_copy(inverse_ref.at[0, 1, 0], diag_ref, sems.at[1])
    load.start()
    later.start()
    rows = own_ref.shape[1]
    load.wait()

    def work(first, second):
        contribution = -(part_ref[...] + plane_dot(high_ref, first, second, rows))
        contribution = contribution.astype(BF16)
        half = contribution.shape[1] // 2
        targets = targets_ref[:, :half]
        source = jnp.concatenate(
            [contribution[:, :half], targets, contribution[:, half:], targets], axis=1
        )
        both = jnp.dot(select_ref[...], source, preferred_element_type=F32)
        lanes = 2 * half
        upper = lax.broadcasted_iota(jnp.int32, (both.shape[0], lanes), 0) % 8 >= 4
        out_ref[...] = jnp.where(upper, both[:, lanes:], both[:, :lanes]).astype(BF16)
        later.wait()
        z1_ref[...] = plane_dot(diag_ref, first, second, rows).astype(BF16).astype(F32)

    by_core(core_ref, own_ref, other_ref, work)


def unpack_kernel(core_ref, arrived_ref, kept_ref, got_ref, copies_ref, right_ref):
    half, lanes = right_ref.shape
    arrived = arrived_ref[...]
    code = arrived[:, half : half + 1].astype(F32)
    lane = lax.broadcasted_iota(jnp.int32, (arrived.shape[0], 2 * lanes), 1).astype(F32)
    lands = jnp.where(code == lane + 1.0, 1.0, 0.0).astype(BF16)
    received = lax.dot_general(
        arrived, lands, (((0,), (0,)), ((), ())), preferred_element_type=F32
    )[:half]

    def work(first, second):
        bases = [
            jnp.concatenate(
                [first[:, r * half : (r + 1) * half], second[:, r * half : (r + 1) * half]], axis=1
            ).astype(F32)
            for r in range(2)
        ]
        value = (bases[0] + received[:, :lanes]).astype(BF16)
        for j in range(copies_ref.shape[0]):
            copies_ref[j] = value
        right_ref[...] = bases[1] + received[:, lanes:]

    by_core(core_ref, kept_ref, got_ref, work)


def build_kernel(index_ref, repeats_ref, coupling_ref, out_ref, raw_ref, turned_ref, sums_ref, done_ref, sems):
    rows, width = sums_ref.shape
    half = width // 2
    loads = [
        pltpu.make_async_copy(
            coupling_ref.at[0, r, 0], raw_ref.at[pl.ds(r * half, half)], sems.at[r]
        )
        for r in range(2)
    ]
    for load in loads:
        load.start()

    def clear(i, carry):
        sums_ref[pl.ds(pl.multiple_of(i * 128, 128), 128), :] = jnp.zeros((128, width), F32)
        return carry

    lax.fori_loop(0, rows // 128, clear, 0, unroll=4)
    for load in loads:
        load.wait()
    for i in range(turned_ref.shape[0] // 128):
        part = slice(i * 128, (i + 1) * 128)
        turned_ref[part, :] = raw_ref[:, part].astype(F32).T

    def add_line(line, carry):
        start = pl.multiple_of(line * 128, 128)

        def add_apart(group, carry):
            base = pl.multiple_of(start + group * BATCH, BATCH)
            block = turned_ref[pl.ds(base, BATCH), :]
            at = [pl.ds(index_ref[base + j], 1) for j in range(BATCH)]
            values = [sums_ref[at[j], :] + block[j : j + 1] for j in range(BATCH)]
            for j in range(BATCH):
                sums_ref[at[j], :] = values[j]
            return carry

        def add_in_turn(group, carry):
            base = pl.multiple_of(start + group * BATCH, BATCH)
            block = turned_ref[pl.ds(base, BATCH), :]
            for j in range(BATCH):
                at = pl.ds(index_ref[base + j], 1)
                sums_ref[at, :] = sums_ref[at, :] + block[j : j + 1]
            return carry

        @pl.when(repeats_ref[line] == 0)
        def _():
            lax.fori_loop(0, 128 // BATCH, add_apart, 0, unroll=4)

        @pl.when(repeats_ref[line] != 0)
        def _():
            lax.fori_loop(0, 128 // BATCH, add_in_turn, 0)

        return carry

    lax.fori_loop(0, turned_ref.shape[0] // 128, add_line, 0)
    parts = sems.shape[0] - 2
    size = rows // parts
    stores = []
    for i in range(parts):
        part = pl.ds(i * size, size)
        done_ref[part, :] = sums_ref[part, :].astype(BF16)
        store = pltpu.make_async_copy(done_ref.at[part], out_ref.at[part], sems.at[2 + i])
        store.start()
        stores.append(store)
    for store in stores:
        store.wait()


def build_coupling(index, repeats, coupling, root_rows):
    rows, columns = 2 * coupling.shape[-2], coupling.shape[-1]
    return kernel_call(
        build_kernel,
        (index, repeats, coupling),
        [SMEM, SMEM, HBM],
        like((root_rows, rows)),
        HBM,
        scratch=[
            pltpu.VMEM((rows, columns), BF16),
            pltpu.VMEM((columns, rows), F32),
            pltpu.VMEM((root_rows, rows), F32),
            pltpu.VMEM((root_rows, rows), BF16),
            DMA((10,)),
        ],
        limit=60,
        moved=30 * MIB,
    )


def pair_dot(blocks_ref, start, stop, rights):
    lanes = blocks_ref.shape[2]
    total = None
    for i in range(start // 2, stop // 2):
        left = jnp.concatenate([blocks_ref[2 * i], blocks_ref[2 * i + 1]], axis=1)
        term = rights(left, slice(i * 2 * lanes, (i + 1) * 2 * lanes))
        total = term if total is None else total + term
    return total


def against(*parts):
    return lambda left, columns: lax.dot_general(
        left,
        jnp.concatenate([part[:, columns] for part in parts], axis=0),
        (((1,), (1,)), ((), ())),
        preferred_element_type=F32,
    )


def ordered(core_ref, total):
    return jnp.where(core_ref[0] == 0, total, pltpu.roll(total, total.shape[1] // 2, 1))


def write_copies(copies_ref, value):
    for j in range(copies_ref.shape[0]):
        copies_ref[j] = value


def first_product_kernel(
    core_ref, blocks_ref, lower_ref, other_ref, base_ref, copies_ref, held_ref, sems
):
    kr = held_ref.shape[2]
    chips = blocks_ref.shape[0]
    steps = sems.shape[0]
    width, span = kr // steps, chips // steps
    loads = []
    for i in range(steps):
        columns = pl.ds(i * width, width)
        pairs = [
            (lower_ref.at[1, 0, :, columns], held_ref.at[0, :, columns]),
            (other_ref.at[:, columns], held_ref.at[1, :, columns]),
        ]
        loads.append(
            [pltpu.make_async_copy(a, b, sems.at[i, n]) for n, (a, b) in enumerate(pairs)]
        )
    for group in loads:
        for load in group:
            load.start()
    total = None
    for i, group in enumerate(loads):
        for load in group:
            load.wait()
        term = pair_dot(
            blocks_ref, i * span, (i + 1) * span, against(held_ref.at[0], held_ref.at[1])
        )
        total = term if total is None else total + term
    write_copies(copies_ref, (base_ref[...] - ordered(core_ref, total)).astype(BF16))


def product_kernel(core_ref, blocks_ref, own_ref, other_ref, copies_ref):
    rights = against(own_ref.at[1, 0], other_ref.at[1, 0])
    total = pair_dot(blocks_ref, 0, blocks_ref.shape[0], rights)
    write_copies(copies_ref, ordered(core_ref, total).astype(BF16))


def last_product_kernel(
    core_ref, r0_ref, x1_ref, own_ref, other_ref, upper_own_ref, upper_other_ref, copies_ref
):
    chips = x1_ref.shape[0]
    diagonal = pair_dot(r0_ref, 0, chips, against(own_ref.at[0, 0], other_ref.at[0, 0]))
    diagonal = diagonal.astype(BF16).astype(F32)
    total = diagonal - pair_dot(x1_ref, 0, chips, against(upper_own_ref, upper_other_ref))
    write_copies(copies_ref, ordered(core_ref, total).astype(BF16))


def couple_kernel(x0_ref, x1_ref, own_ref, other_ref, mine_ref, theirs_ref):
    count, half, lanes = x0_ref.shape
    total = None
    for start, blocks_ref in ((0, x0_ref), (count * lanes, x1_ref)):

        def rights(left, columns):
            rows = slice(start + columns.start, start + columns.stop)
            return jnp.dot(
                left,
                jnp.concatenate([own_ref[rows, :], other_ref[rows, :]], axis=1),
                preferred_element_type=F32,
            )

        term = pair_dot(blocks_ref, 0, count, rights)
        total = term if total is None else total + term
    width = mine_ref.shape[1]
    mine_ref[...] = total[:, :width]
    theirs_ref[...] = total[:, width:]


def settle_kernel(core_ref, mine_ref, got_ref, z0_ref, z1_ref, copies_ref, rest_ref):
    stripe = z0_ref.shape[0]

    def work(first, second):
        both = jnp.concatenate([first[...], second[...]], axis=0).T
        rest_ref[...] = z0_ref[...] - both[:stripe]
        write_copies(copies_ref, (z1_ref[...] - both[stripe:]).astype(BF16))

    by_core(core_ref, mine_ref, got_ref, work)


def closing_kernel(core_ref, own_ref, other_ref, top_ref, rest_ref, copies_ref, out_ref):
    out_ref[0, 1, 0] = copies_ref[0]

    def work(first, second):
        total = rest_ref[...] - plane_dot(top_ref, first, second, own_ref.shape[1])
        out_ref[0, 0, 0] = total.astype(BF16)

    by_core(core_ref, own_ref, other_ref, work)


def body(
    child_rhs,
    child_lower,
    child_inverse,
    child_upper,
    child_coupling,
    child_update,
    update_owner,
    update_slot,
    root_rhs,
    root_lower,
    root_inverse,
    root_upper,
):
    planes = lax.axis_size("x") * lax.axis_size("z")
    cubes = planes * lax.axis_size("y")
    devices = cubes * 2
    stripe, rhs = root_rhs.shape[2:]
    half = rhs // 2
    kc = child_inverse.shape[-1]
    kr = root_inverse.shape[-1]
    nc = child_lower.shape[-1]
    held = update_slot.shape[1]
    owner = update_owner.reshape(1, held)
    slot = update_slot
    me = lax.axis_index("c")
    core = me.astype(jnp.int32).reshape(1)
    piece = (planes, stripe, rhs)

    opened = kernel_call(
        opening_kernel, (child_rhs, owner, slot), [VMEM] * 3,
        like((planes, stripe + 8, rhs)), VMEM,
    )
    opened, root_rhs, root_lower, root_inverse, root_upper, child_lower, child_upper = tie(
        (opened, root_rhs, root_lower, root_inverse, root_upper, child_lower, child_upper)
    )
    own_first = spread(opened, PLANE)
    kept, given = kernel_call(
        turn_kernel, (core, root_rhs), [SMEM, VMEM], [like((half, rhs))] * 2, [VMEM] * 2,
        limit=2, moved=MIB,
    )
    low = rows_of(child_lower, 1, 0, kc)
    top = rows_of(child_upper, 0, kc, nc)
    lower_own = rows_of(root_lower, 1, 0, kr)
    upper_own = rows_of(root_upper, 0, kr, 2 * kr)
    own_first, lower_own, upper_own, kept, given, low, top = tie(
        (own_first, lower_own, upper_own, kept, given, low, top)
    )
    other_first = swap(own_first)
    y1_copies = kernel_call(
        advance_kernel, (core, own_first, other_first, low, child_rhs), [SMEM] + [VMEM] * 4,
        like(piece), VMEM, limit=2, moved=MIB,
    )
    y1_copies, given = tie((y1_copies, given))
    own_second = spread(y1_copies, PLANE)

    part, z0c, index, repeats, select, targets = kernel_call(
        functools.partial(aside_kernel, stripe, kr),
        (core, own_first, other_first, child_update, child_inverse, owner, slot),
        [SMEM, VMEM, VMEM, HBM, HBM, VMEM, VMEM],
        [
            like((held, rhs), F32),
            like((stripe, rhs), F32),
            like((2 * planes, held), jnp.int32),
            like((2 * planes, held), jnp.int32),
            like((devices * 4, held)),
            like((held, held)),
        ],
        [VMEM] * 6,
        scratch=[pltpu.VMEM((held, kc), BF16), pltpu.VMEM((stripe, kc), BF16), DMA((2,))],
        limit=4, moved=2 * MIB,
    )
    index, repeats = index.reshape(-1), repeats[:, 0]
    got = swap(given)
    own_second, part, z0c, index, repeats, select, targets, got = tie(
        (own_second, part, z0c, index, repeats, select, targets, got)
    )
    other_second = swap(own_second)

    packed, z1c = kernel_call(
        contribute_kernel,
        (core, own_second, other_second, child_update, child_inverse, part, select, targets),
        [SMEM, VMEM, VMEM, HBM, HBM] + [VMEM] * 3,
        [like((devices * 4, rhs)), like((stripe, rhs), F32)], [VMEM] * 2,
        scratch=[pltpu.VMEM((held, kc), BF16), pltpu.VMEM((stripe, kc), BF16), DMA((2,))],
        limit=4, moved=MIB,
    )
    packed, z1c, lower_own = tie((packed, z1c, lower_own))
    arrived = spread(packed.reshape(devices, 4, rhs), ALL)
    lower_other = swap(lower_own)

    r0_copies, right = kernel_call(
        unpack_kernel, (core, arrived.reshape(devices * 4, rhs), kept, got), [SMEM] + [VMEM] * 3,
        [like((cubes, half, rhs)), like((half, rhs), F32)], [VMEM] * 2, limit=4, moved=MIB,
    )
    r0_copies, index, repeats = tie((r0_copies, index, repeats))
    summed = build_coupling(index, repeats, child_coupling, 2 * kr)
    whole = (cubes, half, rhs)
    work = dict(flops=2 * cubes * half * rhs * rhs, moved=4 * MIB)
    r0, summed, lower_other = tie((spread(r0_copies, CUBE), summed, lower_other))
    r1_copies = kernel_call(
        first_product_kernel, (core, r0, root_lower, lower_other, right),
        [SMEM, VMEM, HBM, HBM, VMEM], like(whole), VMEM,
        scratch=[pltpu.VMEM((2, stripe, kr), BF16), DMA((4, 2))], limit=FIRST, **work,
    )
    r1_copies, inverse, upper_own = tie((r1_copies, root_inverse, upper_own))
    inverse_other, upper_other = swap(inverse), swap(upper_own)
    r1, inverse_other, upper_other = tie((spread(r1_copies, CUBE), inverse_other, upper_other))
    x1_copies = kernel_call(
        product_kernel, (core, r1, root_inverse, inverse_other), [SMEM] + [VMEM] * 3,
        like(whole), VMEM, limit=4, **work,
    )
    x1_copies, summed = tie((x1_copies, summed))
    summed_other = swap(summed)
    x1, summed_other = tie((spread(x1_copies, CUBE), summed_other))
    x0_copies = kernel_call(
        last_product_kernel, (core, r0, x1, root_inverse, inverse_other, upper_own, upper_other),
        [SMEM] + [VMEM] * 6, like(whole), VMEM, limit=4, **work,
    )
    x0, x0_copies, x1_copies = tie((spread(x0_copies, CUBE), x0_copies, x1_copies))

    mine, given = kernel_call(
        couple_kernel, (x0, x1, summed, summed_other), [VMEM] * 4,
        [like((half, 2 * stripe), F32)] * 2, [VMEM] * 2,
        limit=4, flops=8 * cubes * half * rhs * rhs, moved=10 * MIB,
    )
    c1_copies, rest = kernel_call(
        settle_kernel, (core, mine, swap(given), z0c, z1c), [SMEM] + [VMEM] * 4,
        [like(piece), like((stripe, rhs), F32)], [VMEM] * 2, limit=2, moved=MIB,
    )
    c1_copies, x0_own, x1_own = tie((c1_copies, x0_copies[0], x1_copies[0]))
    own_c1 = spread(c1_copies, PLANE)

    def own_rows(half_rows):
        pair = in_core_order(half_rows, swap(half_rows), 0).reshape(rhs, 2 * stripe)
        rows = pair.T
        return jnp.where(me == 0, rows[:stripe], rows[stripe:])

    root_solution = jnp.stack([own_rows(x0_own), own_rows(x1_own)])[:, None]
    own_c1, root_solution = tie((own_c1, root_solution))
    child_solution = kernel_call(
        closing_kernel, (core, own_c1, swap(own_c1), top, rest, c1_copies),
        [SMEM] + [VMEM] * 5, like(child_rhs.shape), VMEM, limit=2, moved=MIB,
    )
    return child_solution, root_solution


def solution(mesh):
    leaf, front = mesh.devices.shape
    fine = Mesh(mesh.devices.reshape((leaf, 4, front // 8, 2)), ALL)
    subtree = P("y", None, ("x", "z", "c"), None, None)
    ancestor = P(None, ALL, None, None)
    in_specs = (
        subtree,
        subtree,
        subtree,
        subtree,
        subtree,
        P("y", ("x", "z", "c"), None),
        P("y", ("x", "z", "c"), None),
        P("y", ("x", "z", "c")),
        ancestor,
        ancestor,
        ancestor,
        ancestor,
    )
    return jax.shard_map(
        body, mesh=fine, in_specs=in_specs, out_specs=(subtree, ancestor), check_vma=False
    )
```

```python
import functools

import jax
import jax.numpy as jnp
from jax import lax
from jax.experimental import pallas as pl
from jax.experimental.pallas import tpu as pltpu
from jax.sharding import Mesh
from jax.sharding import PartitionSpec as P

F32 = jnp.float32
BF16 = jnp.bfloat16
ALL = ("y", "x", "z", "c")
PLANE = ("x", "z")
CUBE = ("y", "x", "z")
VMEM = pl.BlockSpec(memory_space=pltpu.VMEM)
SMEM = pl.BlockSpec(memory_space=pltpu.SMEM)
HBM = pl.BlockSpec(memory_space=pltpu.HBM)
DMA = pltpu.SemaphoreType.DMA
MIB = 1 << 20
BATCH = 8
tie = lax.optimization_barrier


def swap(array):
    return lax.ppermute(array, "c", [(0, 1), (1, 0)])


def spread(copies, axes):
    return lax.all_to_all(copies, axes, 0, 0)


def in_core_order(own, other, axis):
    first = lax.axis_index("c") == 0
    return jnp.stack([jnp.where(first, own, other), jnp.where(first, other, own)], axis=axis)


def rows_of(array, block, first, last):
    lead = array.ndim - 4
    start = (0,) * lead + (block, 0, 0, first)
    stop = (1,) * lead + (block + 1, 1, array.shape[-2], last)
    return lax.slice(array, start, stop).reshape(array.shape[-2], last - first)


def like(shape, dtype=BF16):
    return jax.ShapeDtypeStruct(shape, dtype)


def kernel_call(body, args, specs, shapes, out_specs, scratch=(), limit=None, flops=0, moved=0):
    return pl.pallas_call(
        body,
        out_shape=shapes,
        in_specs=specs,
        out_specs=out_specs,
        scratch_shapes=list(scratch),
        compiler_params=pltpu.CompilerParams(
            vmem_limit_bytes=None if limit is None else limit * MIB
        ),
        cost_estimate=pl.CostEstimate(flops=flops, bytes_accessed=moved, transcendentals=0),
    )(*args)


def by_core(core_ref, own_refs, other_refs, work):
    @pl.when(core_ref[0] == 0)
    def _():
        work(own_refs, other_refs)

    @pl.when(core_ref[0] != 0)
    def _():
        work(other_refs, own_refs)


def plane_dot(matrix_ref, first_ref, second_ref, rows):
    total = None
    for p in range(first_ref.shape[0] // 2):
        block = jnp.concatenate(
            [
                first_ref[2 * p, 0:rows],
                second_ref[2 * p, 0:rows],
                first_ref[2 * p + 1, 0:rows],
                second_ref[2 * p + 1, 0:rows],
            ],
            axis=0,
        )
        term = jnp.dot(
            matrix_ref[:, p * 4 * rows : (p + 1) * 4 * rows], block, preferred_element_type=F32
        )
        total = term if total is None else total + term
    return total


def opening_kernel(rhs_ref, owner_ref, slot_ref, out_ref):
    row = lax.broadcasted_iota(jnp.int32, (8, 128), 0)
    marks = jnp.where(row == 0, owner_ref[...], jnp.where(row == 1, slot_ref[...], 0))
    marks = marks.astype(F32).astype(BF16)
    rows = rhs_ref.shape[3]
    for j in range(out_ref.shape[0]):
        out_ref[j, 0:rows] = rhs_ref[0, 0, 0]
        out_ref[j, rows : rows + 8] = marks


def turn_kernel(core_ref, rhs_ref, kept_ref, given_ref):
    both = jnp.concatenate(
        [rhs_ref[0, 0].astype(F32).T, rhs_ref[1, 0].astype(F32).T], axis=1
    ).astype(BF16)
    half = both.shape[0] // 2

    @pl.when(core_ref[0] == 0)
    def _():
        kept_ref[...] = both[:half]
        given_ref[...] = both[half:]

    @pl.when(core_ref[0] != 0)
    def _():
        kept_ref[...] = both[half:]
        given_ref[...] = both[:half]


def advance_kernel(core_ref, own_ref, other_ref, low_ref, rhs_ref, out_ref):
    rows = out_ref.shape[1]

    def work(first, second):
        total = rhs_ref[0, 1, 0].astype(F32) - plane_dot(low_ref, first, second, rows)
        value = total.astype(BF16)
        for j in range(out_ref.shape[0]):
            out_ref[j] = value

    by_core(core_ref, own_ref, other_ref, work)


def aside_kernel(
    rows, kr, core_ref, own_ref, other_ref, update_ref, inverse_ref, owner_ref, slot_ref,
    part_ref, z0_ref, index_ref, repeats_ref, select_ref, targets_ref, low_ref, diag_ref, sems
):
    kc = low_ref.shape[1]
    copies = [
        pltpu.make_async_copy(update_ref.at[0, :, pl.ds(0, kc)], low_ref, sems.at[0]),
        pltpu.make_async_copy(inverse_ref.at[0, 0, 0], diag_ref, sems.at[1]),
    ]
    for copy in copies:
        copy.start()

    held = owner_ref.shape[1]
    owner = owner_ref[...].astype(F32)
    owners = jnp.broadcast_to(owner, (held, held))
    above = lax.broadcasted_iota(jnp.int32, (held, held), 0) < lax.broadcasted_iota(
        jnp.int32, (held, held), 1
    )
    same = jnp.where((owners == owners.T) & above, 1.0, 0.0)
    place = owner * 2.0 + jnp.sum(same, axis=0, keepdims=True)
    row = lax.broadcasted_iota(jnp.int32, (select_ref.shape[0], held), 0)
    wanted = (row // 8 * 4 + row % 4).astype(F32)
    select_ref[...] = jnp.where(wanted == place, 1.0, 0.0).astype(BF16)
    slot = slot_ref[...]
    target = slot // rows * (2 * rows) + owner_ref[...] % 2 * rows + slot % rows + 1
    targets_ref[...] = jnp.broadcast_to(target.astype(F32), (held, held)).T.astype(BF16)


    def work(first, second):
        for j in range(own_ref.shape[0]):
            for c, source in enumerate((first, second)):
                marks = source[j, rows : rows + 8].astype(F32).astype(jnp.int32)
                owner, slot = marks[0:1], marks[1:2]
                index_ref[2 * j + c : 2 * j + c + 1, :] = (
                    (slot // rows) * kr + owner * rows + slot % rows
                )
        index = index_ref[...]
        lane = lax.broadcasted_iota(jnp.int32, index.shape, 1) % BATCH
        found = jnp.zeros(index.shape, jnp.int32)
        for d in range(1, BATCH):
            again = (pltpu.roll(index, d, 1) == index) & (lane >= d)
            found = jnp.maximum(found, jnp.where(again, 1, 0))
        repeats_ref[...] = jnp.broadcast_to(
            jnp.max(found, axis=1, keepdims=True), repeats_ref.shape
        )
        copies[0].wait()
        part_ref[...] = plane_dot(low_ref, first, second, rows)
        copies[1].wait()
        z0_ref[...] = plane_dot(diag_ref, first, second, rows).astype(BF16).astype(F32)

    by_core(core_ref, own_ref, other_ref, work)


def contribute_kernel(
    core_ref, own_ref, other_ref, update_ref, inverse_ref, part_ref, select_ref, targets_ref,
    out_ref, z1_ref, high_ref, diag_ref, sems
):
    kc = high_ref.shape[1]
    load = pltpu.make_async_copy(update_ref.at[0, :, pl.ds(kc, kc)], high_ref, sems.at[0])
    later = pltpu.make_async_copy(inverse_ref.at[0, 1, 0], diag_ref, sems.at[1])
    load.start()
    later.start()
    rows = own_ref.shape[1]
    load.wait()

    def work(first, second):
        contribution = -(part_ref[...] + plane_dot(high_ref, first, second, rows))
        contribution = contribution.astype(BF16)
        half = contribution.shape[1] // 2
        targets = targets_ref[:, :half]
        source = jnp.concatenate(
            [contribution[:, :half], targets, contribution[:, half:], targets], axis=1
        )
        both = jnp.dot(select_ref[...], source, preferred_element_type=F32)
        lanes = 2 * half
        upper = lax.broadcasted_iota(jnp.int32, (both.shape[0], lanes), 0) % 8 >= 4
        out_ref[...] = jnp.where(upper, both[:, lanes:], both[:, :lanes]).astype(BF16)
        later.wait()
        z1_ref[...] = plane_dot(diag_ref, first, second, rows).astype(BF16).astype(F32)

    by_core(core_ref, own_ref, other_ref, work)


def unpack_kernel(core_ref, arrived_ref, kept_ref, got_ref, copies_ref, right_ref):
    half, lanes = right_ref.shape
    arrived = arrived_ref[...]
    code = arrived[:, half : half + 1].astype(F32)
    lane = lax.broadcasted_iota(jnp.int32, (arrived.shape[0], 2 * lanes), 1).astype(F32)
    lands = jnp.where(code == lane + 1.0, 1.0, 0.0).astype(BF16)
    received = lax.dot_general(
        arrived, lands, (((0,), (0,)), ((), ())), preferred_element_type=F32
    )[:half]

    def work(first, second):
        bases = [
            jnp.concatenate(
                [first[:, r * half : (r + 1) * half], second[:, r * half : (r + 1) * half]], axis=1
            ).astype(F32)
            for r in range(2)
        ]
        value = (bases[0] + received[:, :lanes]).astype(BF16)
        for j in range(copies_ref.shape[0]):
            copies_ref[j] = value
        right_ref[...] = bases[1] + received[:, lanes:]

    by_core(core_ref, kept_ref, got_ref, work)


def build_kernel(index_ref, repeats_ref, coupling_ref, out_ref, raw_ref, turned_ref, sums_ref, done_ref, sems):
    rows, width = sums_ref.shape
    half = width // 2
    loads = [
        pltpu.make_async_copy(
            coupling_ref.at[0, r, 0], raw_ref.at[pl.ds(r * half, half)], sems.at[r]
        )
        for r in range(2)
    ]
    for load in loads:
        load.start()

    def clear(i, carry):
        sums_ref[pl.ds(pl.multiple_of(i * 128, 128), 128), :] = jnp.zeros((128, width), F32)
        return carry

    lax.fori_loop(0, rows // 128, clear, 0, unroll=4)
    for load in loads:
        load.wait()
    for i in range(turned_ref.shape[0] // 128):
        part = slice(i * 128, (i + 1) * 128)
        turned_ref[part, :] = raw_ref[:, part].astype(F32).T

    def add_line(line, carry):
        start = pl.multiple_of(line * 128, 128)

        def add_apart(group, carry):
            base = pl.multiple_of(start + group * BATCH, BATCH)
            block = turned_ref[pl.ds(base, BATCH), :]
            at = [pl.ds(index_ref[base + j], 1) for j in range(BATCH)]
            values = [sums_ref[at[j], :] + block[j : j + 1] for j in range(BATCH)]
            for j in range(BATCH):
                sums_ref[at[j], :] = values[j]
            return carry

        def add_in_turn(group, carry):
            base = pl.multiple_of(start + group * BATCH, BATCH)
            block = turned_ref[pl.ds(base, BATCH), :]
            for j in range(BATCH):
                at = pl.ds(index_ref[base + j], 1)
                sums_ref[at, :] = sums_ref[at, :] + block[j : j + 1]
            return carry

        @pl.when(repeats_ref[line] == 0)
        def _():
            lax.fori_loop(0, 128 // BATCH, add_apart, 0, unroll=4)

        @pl.when(repeats_ref[line] != 0)
        def _():
            lax.fori_loop(0, 128 // BATCH, add_in_turn, 0)

        return carry

    lax.fori_loop(0, turned_ref.shape[0] // 128, add_line, 0)
    parts = sems.shape[0] - 2
    size = rows // parts
    stores = []
    for i in range(parts):
        part = pl.ds(i * size, size)
        done_ref[part, :] = sums_ref[part, :].astype(BF16)
        store = pltpu.make_async_copy(done_ref.at[part], out_ref.at[part], sems.at[2 + i])
        store.start()
        stores.append(store)
    for store in stores:
        store.wait()


def build_coupling(index, repeats, coupling, root_rows):
    rows, columns = 2 * coupling.shape[-2], coupling.shape[-1]
    return kernel_call(
        build_kernel,
        (index, repeats, coupling),
        [SMEM, SMEM, HBM],
        like((root_rows, rows)),
        HBM,
        scratch=[
            pltpu.VMEM((rows, columns), BF16),
            pltpu.VMEM((columns, rows), F32),
            pltpu.VMEM((root_rows, rows), F32),
            pltpu.VMEM((root_rows, rows), BF16),
            DMA((10,)),
        ],
        limit=60,
        moved=30 * MIB,
    )


def pair_dot(blocks_ref, start, stop, rights):
    lanes = blocks_ref.shape[2]
    total = None
    for i in range(start // 2, stop // 2):
        left = jnp.concatenate([blocks_ref[2 * i], blocks_ref[2 * i + 1]], axis=1)
        term = rights(left, slice(i * 2 * lanes, (i + 1) * 2 * lanes))
        total = term if total is None else total + term
    return total


def against(*parts):
    return lambda left, columns: lax.dot_general(
        left,
        jnp.concatenate([part[:, columns] for part in parts], axis=0),
        (((1,), (1,)), ((), ())),
        preferred_element_type=F32,
    )


def ordered(core_ref, total):
    return jnp.where(core_ref[0] == 0, total, pltpu.roll(total, total.shape[1] // 2, 1))


def write_copies(copies_ref, value):
    for j in range(copies_ref.shape[0]):
        copies_ref[j] = value


def fetch_kernel(lower_ref, other_ref, out_ref, sems):
    kr = out_ref.shape[2]
    loads = [
        pltpu.make_async_copy(lower_ref.at[1, 0, :, pl.ds(0, kr)], out_ref.at[0], sems.at[0]),
        pltpu.make_async_copy(other_ref, out_ref.at[1], sems.at[1]),
    ]
    for load in loads:
        load.start()
    for load in loads:
        load.wait()


def first_product_kernel(core_ref, blocks_ref, pair_ref, base_ref, copies_ref):
    rights = against(pair_ref.at[0], pair_ref.at[1])
    total = ordered(core_ref, pair_dot(blocks_ref, 0, blocks_ref.shape[0], rights))
    write_copies(copies_ref, (base_ref[...] - total).astype(BF16))


def product_kernel(core_ref, blocks_ref, own_ref, other_ref, copies_ref):
    rights = against(own_ref.at[1, 0], other_ref.at[1, 0])
    total = pair_dot(blocks_ref, 0, blocks_ref.shape[0], rights)
    write_copies(copies_ref, ordered(core_ref, total).astype(BF16))


def last_product_kernel(
    core_ref, r0_ref, x1_ref, own_ref, other_ref, upper_own_ref, upper_other_ref, copies_ref
):
    chips = x1_ref.shape[0]
    diagonal = pair_dot(r0_ref, 0, chips, against(own_ref.at[0, 0], other_ref.at[0, 0]))
    diagonal = diagonal.astype(BF16).astype(F32)
    total = diagonal - pair_dot(x1_ref, 0, chips, against(upper_own_ref, upper_other_ref))
    write_copies(copies_ref, ordered(core_ref, total).astype(BF16))


def couple_kernel(x0_ref, x1_ref, matrix_ref, out_ref):
    count, half, lanes = x0_ref.shape
    total = None
    for start, blocks_ref in ((0, x0_ref), (count * lanes, x1_ref)):

        def rights(left, columns):
            rows = slice(start + columns.start, start + columns.stop)
            return jnp.dot(left, matrix_ref[rows, :], preferred_element_type=F32)

        term = pair_dot(blocks_ref, 0, count, rights)
        total = term if total is None else total + term
    out_ref[...] = total


def settle_kernel(core_ref, mine_ref, got_ref, z0_ref, z1_ref, copies_ref, c1_ref, rest_ref):
    stripe = z0_ref.shape[0]

    def work(first, second):
        both = jnp.concatenate([first[...], second[...]], axis=0).T
        rest_ref[...] = z0_ref[...] - both[:stripe]
        value = (z1_ref[...] - both[stripe:]).astype(BF16)
        write_copies(copies_ref, value)
        c1_ref[...] = value

    by_core(core_ref, mine_ref, got_ref, work)


def closing_kernel(core_ref, own_ref, other_ref, top_ref, rest_ref, c1_ref, out_ref):
    out_ref[0, 1, 0] = c1_ref[...]

    def work(first, second):
        total = rest_ref[...] - plane_dot(top_ref, first, second, own_ref.shape[1])
        out_ref[0, 0, 0] = total.astype(BF16)

    by_core(core_ref, own_ref, other_ref, work)


def body(
    child_rhs,
    child_lower,
    child_inverse,
    child_upper,
    child_coupling,
    child_update,
    update_owner,
    update_slot,
    root_rhs,
    root_lower,
    root_inverse,
    root_upper,
):
    planes = lax.axis_size("x") * lax.axis_size("z")
    cubes = planes * lax.axis_size("y")
    devices = cubes * 2
    stripe, rhs = root_rhs.shape[2:]
    half = rhs // 2
    kc = child_inverse.shape[-1]
    kr = root_inverse.shape[-1]
    nc = child_lower.shape[-1]
    held = update_slot.shape[1]
    owner = update_owner.reshape(1, held)
    slot = update_slot
    me = lax.axis_index("c")
    core = me.astype(jnp.int32).reshape(1)
    piece = (planes, stripe, rhs)

    opened = kernel_call(
        opening_kernel, (child_rhs, owner, slot), [VMEM] * 3,
        like((planes, stripe + 8, rhs)), VMEM,
    )
    opened, root_rhs, root_lower, root_inverse, root_upper, child_lower, child_upper = tie(
        (opened, root_rhs, root_lower, root_inverse, root_upper, child_lower, child_upper)
    )
    own_first = spread(opened, PLANE)
    kept, given = kernel_call(
        turn_kernel, (core, root_rhs), [SMEM, VMEM], [like((half, rhs))] * 2, [VMEM] * 2,
        limit=2, moved=MIB,
    )
    low = rows_of(child_lower, 1, 0, kc)
    top = rows_of(child_upper, 0, kc, nc)
    lower_own = rows_of(root_lower, 1, 0, kr)
    upper_own = rows_of(root_upper, 0, kr, 2 * kr)
    own_first, lower_own, upper_own, kept, given, low, top = tie(
        (own_first, lower_own, upper_own, kept, given, low, top)
    )
    other_first = swap(own_first)
    y1_copies = kernel_call(
        advance_kernel, (core, own_first, other_first, low, child_rhs), [SMEM] + [VMEM] * 4,
        like(piece), VMEM, limit=2, moved=MIB,
    )
    y1_copies, given = tie((y1_copies, given))
    own_second = spread(y1_copies, PLANE)

    part, z0c, index, repeats, select, targets = kernel_call(
        functools.partial(aside_kernel, stripe, kr),
        (core, own_first, other_first, child_update, child_inverse, owner, slot),
        [SMEM, VMEM, VMEM, HBM, HBM, VMEM, VMEM],
        [
            like((held, rhs), F32),
            like((stripe, rhs), F32),
            like((2 * planes, held), jnp.int32),
            like((2 * planes, held), jnp.int32),
            like((devices * 4, held)),
            like((held, held)),
        ],
        [VMEM] * 6,
        scratch=[pltpu.VMEM((held, kc), BF16), pltpu.VMEM((stripe, kc), BF16), DMA((2,))],
        limit=4, moved=2 * MIB,
    )
    index, repeats = index.reshape(-1), repeats[:, 0]
    got = swap(given)
    own_second, part, z0c, index, repeats, select, targets, got = tie(
        (own_second, part, z0c, index, repeats, select, targets, got)
    )
    other_second = swap(own_second)

    packed, z1c = kernel_call(
        contribute_kernel,
        (core, own_second, other_second, child_update, child_inverse, part, select, targets),
        [SMEM, VMEM, VMEM, HBM, HBM] + [VMEM] * 3,
        [like((devices * 4, rhs)), like((stripe, rhs), F32)], [VMEM] * 2,
        scratch=[pltpu.VMEM((held, kc), BF16), pltpu.VMEM((stripe, kc), BF16), DMA((2,))],
        limit=4, moved=MIB,
    )
    packed, z1c, lower_own = tie((packed, z1c, lower_own))
    arrived = spread(packed.reshape(devices, 4, rhs), ALL)
    lower_other = swap(lower_own)

    r0_copies, right = kernel_call(
        unpack_kernel, (core, arrived.reshape(devices * 4, rhs), kept, got), [SMEM] + [VMEM] * 3,
        [like((cubes, half, rhs)), like((half, rhs), F32)], [VMEM] * 2, limit=4, moved=MIB,
    )
    r0_copies, index, repeats = tie((r0_copies, index, repeats))
    summed = build_coupling(index, repeats, child_coupling, 2 * kr)
    whole = (cubes, half, rhs)
    work = dict(flops=2 * cubes * half * rhs * rhs, moved=4 * MIB)
    summed, lower_other = tie((summed, lower_other))
    pair = kernel_call(
        fetch_kernel, (root_lower, lower_other), [HBM, HBM], pltpu.VMEM((2, stripe, kr), BF16),
        VMEM, scratch=[DMA((2,))], limit=60, moved=4 * MIB,
    )
    r0, summed, pair = tie((spread(r0_copies, CUBE), summed, pair))
    r1_copies = kernel_call(
        first_product_kernel, (core, r0, pair, right), [SMEM] + [VMEM] * 3, like(whole), VMEM,
        limit=4, **work,
    )
    r1_copies, inverse, upper_own = tie((r1_copies, root_inverse, upper_own))
    inverse_other, upper_other = swap(inverse), swap(upper_own)
    r1, inverse_other, upper_other = tie((spread(r1_copies, CUBE), inverse_other, upper_other))
    x1_copies = kernel_call(
        product_kernel, (core, r1, root_inverse, inverse_other), [SMEM] + [VMEM] * 3,
        like(whole), VMEM, limit=4, **work,
    )
    x1_copies, summed = tie((x1_copies, summed))
    summed_other = swap(summed)
    x1, summed_other = tie((spread(x1_copies, CUBE), summed_other))
    x0_copies = kernel_call(
        last_product_kernel, (core, r0, x1, root_inverse, inverse_other, upper_own, upper_other),
        [SMEM] + [VMEM] * 6, like(whole), VMEM, limit=4, **work,
    )
    x0, x0_copies, x1_copies = tie((spread(x0_copies, CUBE), x0_copies, x1_copies))

    def couple(x0, matrix):
        return kernel_call(
            couple_kernel, (x0, x1, matrix), [VMEM] * 3, like((half, 2 * stripe), F32), VMEM,
            limit=4, flops=4 * cubes * half * rhs * rhs, moved=6 * MIB,
        )

    given, x0 = tie((couple(x0, summed_other), x0))
    theirs, mine = swap(given), couple(x0, summed)
    c1_copies, c1, rest = kernel_call(
        settle_kernel, (core, mine, theirs, z0c, z1c), [SMEM] + [VMEM] * 4,
        [like(piece), like((stripe, rhs)), like((stripe, rhs), F32)], [VMEM] * 3,
        limit=2, moved=MIB,
    )
    c1_copies, x0_own, x1_own = tie((c1_copies, x0_copies[0], x1_copies[0]))
    own_c1 = spread(c1_copies, PLANE)

    def own_rows(half_rows):
        pair = in_core_order(half_rows, swap(half_rows), 0).reshape(rhs, 2 * stripe)
        rows = pair.T
        return jnp.where(me == 0, rows[:stripe], rows[stripe:])

    root_solution = jnp.stack([own_rows(x0_own), own_rows(x1_own)])[:, None]
    own_c1, root_solution = tie((own_c1, root_solution))
    child_solution = kernel_call(
        closing_kernel, (core, own_c1, swap(own_c1), top, rest, c1),
        [SMEM] + [VMEM] * 5, like(child_rhs.shape), VMEM, limit=2, moved=MIB,
    )
    return child_solution, root_solution


def solution(mesh):
    leaf, front = mesh.devices.shape
    fine = Mesh(mesh.devices.reshape((leaf, 4, front // 8, 2)), ALL)
    subtree = P("y", None, ("x", "z", "c"), None, None)
    ancestor = P(None, ALL, None, None)
    in_specs = (
        subtree,
        subtree,
        subtree,
        subtree,
        subtree,
        P("y", ("x", "z", "c"), None),
        P("y", ("x", "z", "c"), None),
        P("y", ("x", "z", "c")),
        ancestor,
        ancestor,
        ancestor,
        ancestor,
    )
    return jax.shard_map(
        body, mesh=fine, in_specs=in_specs, out_specs=(subtree, ancestor), check_vma=False
    )
```

```python
import functools

import jax
import jax.numpy as jnp
from jax import lax
from jax.experimental import pallas as pl
from jax.experimental.pallas import tpu as pltpu
from jax.sharding import Mesh
from jax.sharding import PartitionSpec as P

F32 = jnp.float32
BF16 = jnp.bfloat16
ALL = ("y", "x", "z", "c")
PLANE = ("x", "z")
CUBE = ("y", "x", "z")
VMEM = pl.BlockSpec(memory_space=pltpu.VMEM)
SMEM = pl.BlockSpec(memory_space=pltpu.SMEM)
HBM = pl.BlockSpec(memory_space=pltpu.HBM)
DMA = pltpu.SemaphoreType.DMA
MIB = 1 << 20
BATCH = 8
tie = lax.optimization_barrier


def swap(array):
    return lax.ppermute(array, "c", [(0, 1), (1, 0)])


def spread(copies, axes):
    return lax.all_to_all(copies, axes, 0, 0)


def in_core_order(own, other, axis):
    first = lax.axis_index("c") == 0
    return jnp.stack([jnp.where(first, own, other), jnp.where(first, other, own)], axis=axis)


def rows_of(array, block, first, last):
    lead = array.ndim - 4
    start = (0,) * lead + (block, 0, 0, first)
    stop = (1,) * lead + (block + 1, 1, array.shape[-2], last)
    return lax.slice(array, start, stop).reshape(array.shape[-2], last - first)


def like(shape, dtype=BF16):
    return jax.ShapeDtypeStruct(shape, dtype)


def kernel_call(body, args, specs, shapes, out_specs, scratch=(), limit=None, flops=0, moved=0):
    return pl.pallas_call(
        body,
        out_shape=shapes,
        in_specs=specs,
        out_specs=out_specs,
        scratch_shapes=list(scratch),
        compiler_params=pltpu.CompilerParams(
            vmem_limit_bytes=None if limit is None else limit * MIB
        ),
        cost_estimate=pl.CostEstimate(flops=flops, bytes_accessed=moved, transcendentals=0),
    )(*args)


def by_core(core_ref, own_refs, other_refs, work):
    @pl.when(core_ref[0] == 0)
    def _():
        work(own_refs, other_refs)

    @pl.when(core_ref[0] != 0)
    def _():
        work(other_refs, own_refs)


def plane_dot(matrix_ref, first_ref, second_ref, rows):
    total = None
    for p in range(first_ref.shape[0] // 2):
        block = jnp.concatenate(
            [
                first_ref[2 * p, 0:rows],
                second_ref[2 * p, 0:rows],
                first_ref[2 * p + 1, 0:rows],
                second_ref[2 * p + 1, 0:rows],
            ],
            axis=0,
        )
        term = jnp.dot(
            matrix_ref[:, p * 4 * rows : (p + 1) * 4 * rows], block, preferred_element_type=F32
        )
        total = term if total is None else total + term
    return total


def opening_kernel(rhs_ref, owner_ref, slot_ref, out_ref, second_ref):
    second_ref[...] = rhs_ref[0, 1, 0].astype(F32)
    row = lax.broadcasted_iota(jnp.int32, (8, 128), 0)
    marks = jnp.where(row == 0, owner_ref[...], jnp.where(row == 1, slot_ref[...], 0))
    marks = marks.astype(F32).astype(BF16)
    rows = rhs_ref.shape[3]
    for j in range(out_ref.shape[0]):
        out_ref[j, 0:rows] = rhs_ref[0, 0, 0]
        out_ref[j, rows : rows + 8] = marks


def turn_kernel(core_ref, rhs_ref, kept_ref, given_ref):
    both = jnp.concatenate(
        [rhs_ref[0, 0].astype(F32).T, rhs_ref[1, 0].astype(F32).T], axis=1
    ).astype(BF16)
    half = both.shape[0] // 2

    @pl.when(core_ref[0] == 0)
    def _():
        kept_ref[...] = both[:half]
        given_ref[...] = both[half:]

    @pl.when(core_ref[0] != 0)
    def _():
        kept_ref[...] = both[half:]
        given_ref[...] = both[:half]


def advance_kernel(core_ref, own_ref, other_ref, low_ref, rhs_ref, out_ref):
    rows = out_ref.shape[1]

    def work(first, second):
        total = rhs_ref[...] - plane_dot(low_ref, first, second, rows)
        value = total.astype(BF16)
        for j in range(out_ref.shape[0]):
            out_ref[j] = value

    by_core(core_ref, own_ref, other_ref, work)


def aside_kernel(
    rows, kr, core_ref, own_ref, other_ref, update_ref, inverse_ref, owner_ref, slot_ref,
    part_ref, z0_ref, index_ref, repeats_ref, select_ref, targets_ref, low_ref, diag_ref, sems
):
    kc = low_ref.shape[1]
    copies = [
        pltpu.make_async_copy(update_ref.at[0, :, pl.ds(0, kc)], low_ref, sems.at[0]),
        pltpu.make_async_copy(inverse_ref.at[0, 0, 0], diag_ref, sems.at[1]),
    ]
    for copy in copies:
        copy.start()

    held = owner_ref.shape[1]
    owner = owner_ref[...].astype(F32)
    owners = jnp.broadcast_to(owner, (held, held))
    above = lax.broadcasted_iota(jnp.int32, (held, held), 0) < lax.broadcasted_iota(
        jnp.int32, (held, held), 1
    )
    same = jnp.where((owners == owners.T) & above, 1.0, 0.0)
    place = owner * 2.0 + jnp.sum(same, axis=0, keepdims=True)
    row = lax.broadcasted_iota(jnp.int32, (select_ref.shape[0], held), 0)
    wanted = (row // 8 * 4 + row % 4).astype(F32)
    select_ref[...] = jnp.where(wanted == place, 1.0, 0.0).astype(BF16)
    slot = slot_ref[...]
    target = slot // rows * (2 * rows) + owner_ref[...] % 2 * rows + slot % rows + 1
    targets_ref[...] = jnp.broadcast_to(target.astype(F32), (held, held)).T.astype(BF16)


    def work(first, second):
        for j in range(own_ref.shape[0]):
            for c, source in enumerate((first, second)):
                marks = source[j, rows : rows + 8].astype(F32).astype(jnp.int32)
                owner, slot = marks[0:1], marks[1:2]
                index_ref[2 * j + c : 2 * j + c + 1, :] = (
                    (slot // rows) * kr + owner * rows + slot % rows
                )
        index = index_ref[...]
        lane = lax.broadcasted_iota(jnp.int32, index.shape, 1) % BATCH
        found = jnp.zeros(index.shape, jnp.int32)
        for d in range(1, BATCH):
            again = (pltpu.roll(index, d, 1) == index) & (lane >= d)
            found = jnp.maximum(found, jnp.where(again, 1, 0))
        repeats_ref[...] = jnp.broadcast_to(
            jnp.max(found, axis=1, keepdims=True), repeats_ref.shape
        )
        copies[0].wait()
        part_ref[...] = plane_dot(low_ref, first, second, rows)
        copies[1].wait()
        z0_ref[...] = plane_dot(diag_ref, first, second, rows).astype(BF16).astype(F32)

    by_core(core_ref, own_ref, other_ref, work)


def contribute_kernel(
    core_ref, own_ref, other_ref, update_ref, inverse_ref, part_ref, select_ref, targets_ref,
    out_ref, z1_ref, diag_ref, sem
):
    later = pltpu.make_async_copy(inverse_ref.at[0, 1, 0], diag_ref, sem)
    later.start()
    rows = own_ref.shape[1]
    high_ref = update_ref.at[0, :, pl.ds(diag_ref.shape[1], diag_ref.shape[1])]

    def work(first, second):
        contribution = -(part_ref[...] + plane_dot(high_ref, first, second, rows))
        contribution = contribution.astype(BF16)
        half = contribution.shape[1] // 2
        targets = targets_ref[:, :half]
        source = jnp.concatenate(
            [contribution[:, :half], targets, contribution[:, half:], targets], axis=1
        )
        both = jnp.dot(select_ref[...], source, preferred_element_type=F32)
        lanes = 2 * half
        upper = lax.broadcasted_iota(jnp.int32, (both.shape[0], lanes), 0) % 8 >= 4
        out_ref[...] = jnp.where(upper, both[:, lanes:], both[:, :lanes]).astype(BF16)
        later.wait()
        z1_ref[...] = plane_dot(diag_ref, first, second, rows).astype(BF16).astype(F32)

    by_core(core_ref, own_ref, other_ref, work)


def unpack_kernel(core_ref, arrived_ref, kept_ref, got_ref, copies_ref, right_ref):
    half, lanes = right_ref.shape
    arrived = arrived_ref[...]
    code = arrived[:, half : half + 1].astype(F32)
    lane = lax.broadcasted_iota(jnp.int32, (arrived.shape[0], 2 * lanes), 1).astype(F32)
    lands = jnp.where(code == lane + 1.0, 1.0, 0.0).astype(BF16)
    received = lax.dot_general(
        arrived, lands, (((0,), (0,)), ((), ())), preferred_element_type=F32
    )[:half]

    def work(first, second):
        bases = [
            jnp.concatenate(
                [first[:, r * half : (r + 1) * half], second[:, r * half : (r + 1) * half]], axis=1
            ).astype(F32)
            for r in range(2)
        ]
        value = (bases[0] + received[:, :lanes]).astype(BF16)
        for j in range(copies_ref.shape[0]):
            copies_ref[j] = value
        right_ref[...] = bases[1] + received[:, lanes:]

    by_core(core_ref, kept_ref, got_ref, work)


def build_kernel(index_ref, repeats_ref, coupling_ref, out_ref, raw_ref, turned_ref, sums_ref, done_ref, sems):
    rows, width = sums_ref.shape
    half = width // 2
    loads = [
        pltpu.make_async_copy(
            coupling_ref.at[0, r, 0], raw_ref.at[pl.ds(r * half, half)], sems.at[r]
        )
        for r in range(2)
    ]
    for load in loads:
        load.start()

    def clear(i, carry):
        sums_ref[pl.ds(pl.multiple_of(i * 128, 128), 128), :] = jnp.zeros((128, width), F32)
        return carry

    lax.fori_loop(0, rows // 128, clear, 0, unroll=4)
    for load in loads:
        load.wait()
    for i in range(turned_ref.shape[0] // 128):
        part = slice(i * 128, (i + 1) * 128)
        turned_ref[part, :] = raw_ref[:, part].astype(F32).T

    def add_line(line, carry):
        start = pl.multiple_of(line * 128, 128)

        def add_apart(group, carry):
            base = pl.multiple_of(start + group * BATCH, BATCH)
            block = turned_ref[pl.ds(base, BATCH), :]
            at = [pl.ds(index_ref[base + j], 1) for j in range(BATCH)]
            values = [sums_ref[at[j], :] + block[j : j + 1] for j in range(BATCH)]
            for j in range(BATCH):
                sums_ref[at[j], :] = values[j]
            return carry

        def add_in_turn(group, carry):
            base = pl.multiple_of(start + group * BATCH, BATCH)
            block = turned_ref[pl.ds(base, BATCH), :]
            for j in range(BATCH):
                at = pl.ds(index_ref[base + j], 1)
                sums_ref[at, :] = sums_ref[at, :] + block[j : j + 1]
            return carry

        @pl.when(repeats_ref[line] == 0)
        def _():
            lax.fori_loop(0, 128 // BATCH, add_apart, 0, unroll=4)

        @pl.when(repeats_ref[line] != 0)
        def _():
            lax.fori_loop(0, 128 // BATCH, add_in_turn, 0)

        return carry

    lax.fori_loop(0, turned_ref.shape[0] // 128, add_line, 0)
    parts = sems.shape[0] - 2
    size = rows // parts
    stores = []
    for i in range(parts):
        part = pl.ds(i * size, size)
        done_ref[part, :] = sums_ref[part, :].astype(BF16)
        store = pltpu.make_async_copy(done_ref.at[part], out_ref.at[part], sems.at[2 + i])
        store.start()
        stores.append(store)
    for store in stores:
        store.wait()


def build_coupling(index, repeats, coupling, root_rows):
    rows, columns = 2 * coupling.shape[-2], coupling.shape[-1]
    return kernel_call(
        build_kernel,
        (index, repeats, coupling),
        [SMEM, SMEM, HBM],
        like((root_rows, rows)),
        HBM,
        scratch=[
            pltpu.VMEM((rows, columns), BF16),
            pltpu.VMEM((columns, rows), F32),
            pltpu.VMEM((root_rows, rows), F32),
            pltpu.VMEM((root_rows, rows), BF16),
            DMA((10,)),
        ],
        limit=60,
        moved=30 * MIB,
    )


def pair_dot(blocks_ref, start, stop, rights):
    lanes = blocks_ref.shape[2]
    total = None
    for i in range(start // 2, stop // 2):
        left = jnp.concatenate([blocks_ref[2 * i], blocks_ref[2 * i + 1]], axis=1)
        term = rights(left, slice(i * 2 * lanes, (i + 1) * 2 * lanes))
        total = term if total is None else total + term
    return total


def against(*parts):
    return lambda left, columns: lax.dot_general(
        left,
        jnp.concatenate([part[:, columns] for part in parts], axis=0),
        (((1,), (1,)), ((), ())),
        preferred_element_type=F32,
    )


def ordered(core_ref, total):
    return jnp.where(core_ref[0] == 0, total, pltpu.roll(total, total.shape[1] // 2, 1))


def write_copies(copies_ref, value):
    for j in range(copies_ref.shape[0]):
        copies_ref[j] = value


def first_product_kernel(core_ref, blocks_ref, own_ref, other_ref, base_ref, copies_ref):
    total = pair_dot(blocks_ref, 0, blocks_ref.shape[0], against(own_ref, other_ref))
    write_copies(copies_ref, (base_ref[...] - ordered(core_ref, total)).astype(BF16))


def product_kernel(core_ref, blocks_ref, own_ref, other_ref, copies_ref):
    rights = against(own_ref.at[1, 0], other_ref.at[1, 0])
    total = pair_dot(blocks_ref, 0, blocks_ref.shape[0], rights)
    write_copies(copies_ref, ordered(core_ref, total).astype(BF16))


def last_product_kernel(
    core_ref, r0_ref, x1_ref, own_ref, other_ref, upper_own_ref, upper_other_ref, copies_ref
):
    chips = x1_ref.shape[0]
    diagonal = pair_dot(r0_ref, 0, chips, against(own_ref.at[0, 0], other_ref.at[0, 0]))
    diagonal = diagonal.astype(BF16).astype(F32)
    total = diagonal - pair_dot(x1_ref, 0, chips, against(upper_own_ref, upper_other_ref))
    write_copies(copies_ref, ordered(core_ref, total).astype(BF16))


def couple_kernel(x0_ref, x1_ref, matrix_ref, out_ref):
    count, half, lanes = x0_ref.shape
    total = None
    for start, blocks_ref in ((0, x0_ref), (count * lanes, x1_ref)):

        def rights(left, columns):
            rows = slice(start + columns.start, start + columns.stop)
            return jnp.dot(left, matrix_ref[rows, :], preferred_element_type=F32)

        term = pair_dot(blocks_ref, 0, count, rights)
        total = term if total is None else total + term
    out_ref[...] = total


def settle_kernel(core_ref, mine_ref, got_ref, z0_ref, z1_ref, copies_ref, c1_ref, rest_ref):
    stripe = z0_ref.shape[0]

    def work(first, second):
        both = jnp.concatenate([first[...], second[...]], axis=0).T
        rest_ref[...] = z0_ref[...] - both[:stripe]
        value = (z1_ref[...] - both[stripe:]).astype(BF16)
        write_copies(copies_ref, value)
        c1_ref[...] = value

    by_core(core_ref, mine_ref, got_ref, work)


def closing_kernel(core_ref, own_ref, other_ref, top_ref, rest_ref, c1_ref, out_ref):
    out_ref[0, 1, 0] = c1_ref[...]

    def work(first, second):
        total = rest_ref[...] - plane_dot(top_ref, first, second, own_ref.shape[1])
        out_ref[0, 0, 0] = total.astype(BF16)

    by_core(core_ref, own_ref, other_ref, work)


def body(
    child_rhs,
    child_lower,
    child_inverse,
    child_upper,
    child_coupling,
    child_update,
    update_owner,
    update_slot,
    root_rhs,
    root_lower,
    root_inverse,
    root_upper,
):
    planes = lax.axis_size("x") * lax.axis_size("z")
    cubes = planes * lax.axis_size("y")
    devices = cubes * 2
    stripe, rhs = root_rhs.shape[2:]
    half = rhs // 2
    kc = child_inverse.shape[-1]
    kr = root_inverse.shape[-1]
    nc = child_lower.shape[-1]
    held = update_slot.shape[1]
    owner = update_owner.reshape(1, held)
    slot = update_slot
    me = lax.axis_index("c")
    core = me.astype(jnp.int32).reshape(1)
    piece = (planes, stripe, rhs)

    opened, second = kernel_call(
        opening_kernel, (child_rhs, owner, slot), [VMEM] * 3,
        [like((planes, stripe + 8, rhs)), like((stripe, rhs), F32)], [VMEM] * 2,
    )
    opened, child_lower = tie((opened, child_lower))
    own_first = spread(opened, PLANE)
    low = rows_of(child_lower, 1, 0, kc)
    own_first, low = tie((own_first, low))
    other_first = swap(own_first)
    y1_copies = kernel_call(
        advance_kernel, (core, own_first, other_first, low, second), [SMEM] + [VMEM] * 4,
        like(piece), VMEM, limit=2, moved=MIB,
    )
    y1_copies, root_rhs, child_upper = tie((y1_copies, root_rhs, child_upper))
    own_second = spread(y1_copies, PLANE)

    part, z0c, index, repeats, select, targets = kernel_call(
        functools.partial(aside_kernel, stripe, kr),
        (core, own_first, other_first, child_update, child_inverse, owner, slot),
        [SMEM, VMEM, VMEM, HBM, HBM, VMEM, VMEM],
        [
            like((held, rhs), F32),
            like((stripe, rhs), F32),
            like((2 * planes, held), jnp.int32),
            like((2 * planes, held), jnp.int32),
            like((devices * 4, held)),
            like((held, held)),
        ],
        [VMEM] * 6,
        scratch=[pltpu.VMEM((held, kc), BF16), pltpu.VMEM((stripe, kc), BF16), DMA((2,))],
        limit=4, moved=2 * MIB,
    )
    index, repeats = index.reshape(-1), repeats[:, 0]
    kept, given = kernel_call(
        turn_kernel, (core, root_rhs), [SMEM, VMEM], [like((half, rhs))] * 2, [VMEM] * 2,
        limit=2, moved=MIB,
    )
    top = rows_of(child_upper, 0, kc, nc)
    own_second, part, z0c, index, repeats, select, targets, kept, given, top = tie(
        (own_second, part, z0c, index, repeats, select, targets, kept, given, top)
    )
    other_second = swap(own_second)

    packed, z1c = kernel_call(
        contribute_kernel,
        (core, own_second, other_second, child_update, child_inverse, part, select, targets),
        [SMEM, VMEM, VMEM, VMEM, HBM] + [VMEM] * 3,
        [like((devices * 4, rhs)), like((stripe, rhs), F32)], [VMEM] * 2,
        scratch=[pltpu.VMEM((stripe, kc), BF16), DMA],
        limit=4, moved=MIB,
    )
    packed, z1c, root_lower, root_upper, given = tie(
        (packed, z1c, root_lower, root_upper, given)
    )
    arrived = spread(packed.reshape(devices, 4, rhs), ALL)
    got = swap(given)
    lower_own = rows_of(root_lower, 1, 0, kr)
    upper_own = rows_of(root_upper, 0, kr, 2 * kr)
    arrived, lower_own, upper_own, got = tie((arrived, lower_own, upper_own, got))

    r0_copies, right = kernel_call(
        unpack_kernel, (core, arrived.reshape(devices * 4, rhs), kept, got), [SMEM] + [VMEM] * 3,
        [like((cubes, half, rhs)), like((half, rhs), F32)], [VMEM] * 2, limit=4, moved=MIB,
    )
    r0_copies, index, repeats, lower_own = tie((r0_copies, index, repeats, lower_own))
    lower_other = swap(lower_own)
    summed = build_coupling(index, repeats, child_coupling, 2 * kr)
    whole = (cubes, half, rhs)
    work = dict(flops=2 * cubes * half * rhs * rhs, moved=4 * MIB)
    r0, summed, lower_other = tie((spread(r0_copies, CUBE), summed, lower_other))
    r1_copies = kernel_call(
        first_product_kernel, (core, r0, lower_own, lower_other, right),
        [SMEM] + [VMEM] * 4, like(whole), VMEM, limit=4, **work,
    )
    r1_copies, inverse, upper_own = tie((r1_copies, root_inverse, upper_own))
    inverse_other, upper_other = swap(inverse), swap(upper_own)
    r1, inverse_other, upper_other = tie((spread(r1_copies, CUBE), inverse_other, upper_other))
    x1_copies = kernel_call(
        product_kernel, (core, r1, root_inverse, inverse_other), [SMEM] + [VMEM] * 3,
        like(whole), VMEM, limit=4, **work,
    )
    x1_copies, summed = tie((x1_copies, summed))
    summed_other = swap(summed)
    x1, summed_other = tie((spread(x1_copies, CUBE), summed_other))
    x0_copies = kernel_call(
        last_product_kernel, (core, r0, x1, root_inverse, inverse_other, upper_own, upper_other),
        [SMEM] + [VMEM] * 6, like(whole), VMEM, limit=4, **work,
    )
    x0, x0_copies, x1_copies = tie((spread(x0_copies, CUBE), x0_copies, x1_copies))

    def couple(x0, matrix):
        return kernel_call(
            couple_kernel, (x0, x1, matrix), [VMEM] * 3, like((half, 2 * stripe), F32), VMEM,
            limit=4, flops=4 * cubes * half * rhs * rhs, moved=6 * MIB,
        )

    given, x0 = tie((couple(x0, summed_other), x0))
    theirs, mine = swap(given), couple(x0, summed)
    c1_copies, c1, rest = kernel_call(
        settle_kernel, (core, mine, theirs, z0c, z1c), [SMEM] + [VMEM] * 4,
        [like(piece), like((stripe, rhs)), like((stripe, rhs), F32)], [VMEM] * 3,
        limit=2, moved=MIB,
    )
    c1_copies, x0_own, x1_own = tie((c1_copies, x0_copies[0], x1_copies[0]))
    own_c1 = spread(c1_copies, PLANE)

    def own_rows(half_rows):
        pair = in_core_order(half_rows, swap(half_rows), 0).reshape(rhs, 2 * stripe)
        rows = pair.T
        return jnp.where(me == 0, rows[:stripe], rows[stripe:])

    root_solution = jnp.stack([own_rows(x0_own), own_rows(x1_own)])[:, None]
    own_c1, root_solution = tie((own_c1, root_solution))
    child_solution = kernel_call(
        closing_kernel, (core, own_c1, swap(own_c1), top, rest, c1),
        [SMEM] + [VMEM] * 5, like(child_rhs.shape), VMEM, limit=2, moved=MIB,
    )
    return child_solution, root_solution


def solution(mesh):
    leaf, front = mesh.devices.shape
    fine = Mesh(mesh.devices.reshape((leaf, 4, front // 8, 2)), ALL)
    subtree = P("y", None, ("x", "z", "c"), None, None)
    ancestor = P(None, ALL, None, None)
    in_specs = (
        subtree,
        subtree,
        subtree,
        subtree,
        subtree,
        P("y", ("x", "z", "c"), None),
        P("y", ("x", "z", "c"), None),
        P("y", ("x", "z", "c")),
        ancestor,
        ancestor,
        ancestor,
        ancestor,
    )
    return jax.shard_map(
        body, mesh=fine, in_specs=in_specs, out_specs=(subtree, ancestor), check_vma=False
    )
```

```python
import functools

import jax
import jax.numpy as jnp
from jax import lax
from jax.experimental import pallas as pl
from jax.experimental.pallas import tpu as pltpu
from jax.sharding import Mesh
from jax.sharding import PartitionSpec as P

F32 = jnp.float32
BF16 = jnp.bfloat16
ALL = ("y", "x", "z", "c")
PLANE = ("x", "z")
CUBE = ("y", "x", "z")
VMEM = pl.BlockSpec(memory_space=pltpu.VMEM)
SMEM = pl.BlockSpec(memory_space=pltpu.SMEM)
HBM = pl.BlockSpec(memory_space=pltpu.HBM)
DMA = pltpu.SemaphoreType.DMA
MIB = 1 << 20
BATCH = 8
tie = lax.optimization_barrier


def swap(array):
    return lax.ppermute(array, "c", [(0, 1), (1, 0)])


def spread(copies, axes):
    return lax.all_to_all(copies, axes, 0, 0)


def in_core_order(own, other, axis):
    first = lax.axis_index("c") == 0
    return jnp.stack([jnp.where(first, own, other), jnp.where(first, other, own)], axis=axis)


def rows_of(array, block, first, last):
    lead = array.ndim - 4
    start = (0,) * lead + (block, 0, 0, first)
    stop = (1,) * lead + (block + 1, 1, array.shape[-2], last)
    return lax.slice(array, start, stop).reshape(array.shape[-2], last - first)


def like(shape, dtype=BF16):
    return jax.ShapeDtypeStruct(shape, dtype)


def kernel_call(body, args, specs, shapes, out_specs, scratch=(), limit=None, flops=0, moved=0):
    return pl.pallas_call(
        body,
        out_shape=shapes,
        in_specs=specs,
        out_specs=out_specs,
        scratch_shapes=list(scratch),
        compiler_params=pltpu.CompilerParams(
            vmem_limit_bytes=None if limit is None else limit * MIB
        ),
        cost_estimate=pl.CostEstimate(flops=flops, bytes_accessed=moved, transcendentals=0),
    )(*args)


def by_core(core_ref, own_refs, other_refs, work):
    @pl.when(core_ref[0] == 0)
    def _():
        work(own_refs, other_refs)

    @pl.when(core_ref[0] != 0)
    def _():
        work(other_refs, own_refs)


def plane_dot(matrix_ref, first_ref, second_ref, rows):
    total = None
    for p in range(first_ref.shape[0] // 2):
        block = jnp.concatenate(
            [
                first_ref[2 * p, 0:rows],
                second_ref[2 * p, 0:rows],
                first_ref[2 * p + 1, 0:rows],
                second_ref[2 * p + 1, 0:rows],
            ],
            axis=0,
        )
        term = jnp.dot(
            matrix_ref[:, p * 4 * rows : (p + 1) * 4 * rows], block, preferred_element_type=F32
        )
        total = term if total is None else total + term
    return total


def opening_kernel(rhs_ref, owner_ref, slot_ref, out_ref):
    row = lax.broadcasted_iota(jnp.int32, (8, 128), 0)
    marks = jnp.where(row == 0, owner_ref[...], jnp.where(row == 1, slot_ref[...], 0))
    marks = marks.astype(F32).astype(BF16)
    rows = rhs_ref.shape[3]
    for j in range(out_ref.shape[0]):
        out_ref[j, 0:rows] = rhs_ref[0, 0, 0]
        out_ref[j, rows : rows + 8] = marks


def turn_kernel(core_ref, rhs_ref, kept_ref, given_ref):
    both = jnp.concatenate(
        [rhs_ref[0, 0].astype(F32).T, rhs_ref[1, 0].astype(F32).T], axis=1
    ).astype(BF16)
    half = both.shape[0] // 2

    @pl.when(core_ref[0] == 0)
    def _():
        kept_ref[...] = both[:half]
        given_ref[...] = both[half:]

    @pl.when(core_ref[0] != 0)
    def _():
        kept_ref[...] = both[half:]
        given_ref[...] = both[:half]


def advance_kernel(core_ref, own_ref, other_ref, low_ref, rhs_ref, out_ref):
    rows = out_ref.shape[1]

    def work(first, second):
        total = rhs_ref[0, 1, 0].astype(F32) - plane_dot(low_ref, first, second, rows)
        value = total.astype(BF16)
        for j in range(out_ref.shape[0]):
            out_ref[j] = value

    by_core(core_ref, own_ref, other_ref, work)


def aside_kernel(
    rows, kr, core_ref, own_ref, other_ref, update_ref, inverse_ref, owner_ref, slot_ref,
    part_ref, z0_ref, index_ref, repeats_ref, select_ref, targets_ref, low_ref, diag_ref, sems
):
    kc = low_ref.shape[1]
    copies = [
        pltpu.make_async_copy(update_ref.at[0, :, pl.ds(0, kc)], low_ref, sems.at[0]),
        pltpu.make_async_copy(inverse_ref.at[0, 0, 0], diag_ref, sems.at[1]),
    ]
    for copy in copies:
        copy.start()

    held = owner_ref.shape[1]
    owner = owner_ref[...].astype(F32)
    owners = jnp.broadcast_to(owner, (held, held))
    above = lax.broadcasted_iota(jnp.int32, (held, held), 0) < lax.broadcasted_iota(
        jnp.int32, (held, held), 1
    )
    same = jnp.where((owners == owners.T) & above, 1.0, 0.0)
    place = owner * 2.0 + jnp.sum(same, axis=0, keepdims=True)
    row = lax.broadcasted_iota(jnp.int32, (select_ref.shape[0], held), 0)
    wanted = (row // 8 * 4 + row % 4).astype(F32)
    select_ref[...] = jnp.where(wanted == place, 1.0, 0.0).astype(BF16)
    slot = slot_ref[...]
    target = slot // rows * (2 * rows) + owner_ref[...] % 2 * rows + slot % rows + 1
    targets_ref[...] = jnp.broadcast_to(target.astype(F32), (held, held)).T.astype(BF16)


    def work(first, second):
        for j in range(own_ref.shape[0]):
            for c, source in enumerate((first, second)):
                marks = source[j, rows : rows + 8].astype(F32).astype(jnp.int32)
                owner, slot = marks[0:1], marks[1:2]
                index_ref[2 * j + c : 2 * j + c + 1, :] = (
                    (slot // rows) * kr + owner * rows + slot % rows
                )
        index = index_ref[...]
        lane = lax.broadcasted_iota(jnp.int32, index.shape, 1) % BATCH
        found = jnp.zeros(index.shape, jnp.int32)
        for d in range(1, BATCH):
            again = (pltpu.roll(index, d, 1) == index) & (lane >= d)
            found = jnp.maximum(found, jnp.where(again, 1, 0))
        repeats_ref[...] = jnp.broadcast_to(
            jnp.max(found, axis=1, keepdims=True), repeats_ref.shape
        )
        copies[0].wait()
        part_ref[...] = plane_dot(low_ref, first, second, rows)
        copies[1].wait()
        z0_ref[...] = plane_dot(diag_ref, first, second, rows).astype(BF16).astype(F32)

    by_core(core_ref, own_ref, other_ref, work)


def contribute_kernel(
    core_ref, own_ref, other_ref, update_ref, part_ref, select_ref, targets_ref,
    out_ref, high_ref, sem
):
    kc = high_ref.shape[1]
    load = pltpu.make_async_copy(update_ref.at[0, :, pl.ds(kc, kc)], high_ref, sem)
    load.start()
    rows = own_ref.shape[1]
    load.wait()

    def work(first, second):
        contribution = -(part_ref[...] + plane_dot(high_ref, first, second, rows))
        contribution = contribution.astype(BF16)
        half = contribution.shape[1] // 2
        targets = targets_ref[:, :half]
        source = jnp.concatenate(
            [contribution[:, :half], targets, contribution[:, half:], targets], axis=1
        )
        both = jnp.dot(select_ref[...], source, preferred_element_type=F32)
        lanes = 2 * half
        upper = lax.broadcasted_iota(jnp.int32, (both.shape[0], lanes), 0) % 8 >= 4
        out_ref[...] = jnp.where(upper, both[:, lanes:], both[:, :lanes]).astype(BF16)

    by_core(core_ref, own_ref, other_ref, work)


def diagonal_kernel(core_ref, own_ref, other_ref, inverse_ref, z1_ref, diag_ref, sem):
    load = pltpu.make_async_copy(inverse_ref.at[0, 1, 0], diag_ref, sem)
    load.start()
    load.wait()

    def work(first, second):
        total = plane_dot(diag_ref, first, second, own_ref.shape[1])
        z1_ref[...] = total.astype(BF16).astype(F32)

    by_core(core_ref, own_ref, other_ref, work)


def unpack_kernel(core_ref, arrived_ref, kept_ref, got_ref, copies_ref, right_ref):
    half, lanes = right_ref.shape
    arrived = arrived_ref[...]
    code = arrived[:, half : half + 1].astype(F32)
    lane = lax.broadcasted_iota(jnp.int32, (arrived.shape[0], 2 * lanes), 1).astype(F32)
    lands = jnp.where(code == lane + 1.0, 1.0, 0.0).astype(BF16)
    received = lax.dot_general(
        arrived, lands, (((0,), (0,)), ((), ())), preferred_element_type=F32
    )[:half]

    def work(first, second):
        bases = [
            jnp.concatenate(
                [first[:, r * half : (r + 1) * half], second[:, r * half : (r + 1) * half]], axis=1
            ).astype(F32)
            for r in range(2)
        ]
        value = (bases[0] + received[:, :lanes]).astype(BF16)
        for j in range(copies_ref.shape[0]):
            copies_ref[j] = value
        right_ref[...] = bases[1] + received[:, lanes:]

    by_core(core_ref, kept_ref, got_ref, work)


def build_kernel(index_ref, repeats_ref, coupling_ref, out_ref, raw_ref, turned_ref, sums_ref, done_ref, sems):
    rows, width = sums_ref.shape
    half = width // 2
    loads = [
        pltpu.make_async_copy(
            coupling_ref.at[0, r, 0], raw_ref.at[pl.ds(r * half, half)], sems.at[r]
        )
        for r in range(2)
    ]
    for load in loads:
        load.start()

    def clear(i, carry):
        sums_ref[pl.ds(pl.multiple_of(i * 128, 128), 128), :] = jnp.zeros((128, width), F32)
        return carry

    lax.fori_loop(0, rows // 128, clear, 0, unroll=4)
    for load in loads:
        load.wait()
    for i in range(turned_ref.shape[0] // 128):
        part = slice(i * 128, (i + 1) * 128)
        turned_ref[part, :] = raw_ref[:, part].astype(F32).T

    def add_line(line, carry):
        start = pl.multiple_of(line * 128, 128)

        def add_apart(group, carry):
            base = pl.multiple_of(start + group * BATCH, BATCH)
            block = turned_ref[pl.ds(base, BATCH), :]
            at = [pl.ds(index_ref[base + j], 1) for j in range(BATCH)]
            values = [sums_ref[at[j], :] + block[j : j + 1] for j in range(BATCH)]
            for j in range(BATCH):
                sums_ref[at[j], :] = values[j]
            return carry

        def add_in_turn(group, carry):
            base = pl.multiple_of(start + group * BATCH, BATCH)
            block = turned_ref[pl.ds(base, BATCH), :]
            for j in range(BATCH):
                at = pl.ds(index_ref[base + j], 1)
                sums_ref[at, :] = sums_ref[at, :] + block[j : j + 1]
            return carry

        @pl.when(repeats_ref[line] == 0)
        def _():
            lax.fori_loop(0, 128 // BATCH, add_apart, 0, unroll=4)

        @pl.when(repeats_ref[line] != 0)
        def _():
            lax.fori_loop(0, 128 // BATCH, add_in_turn, 0)

        return carry

    lax.fori_loop(0, turned_ref.shape[0] // 128, add_line, 0)
    parts = sems.shape[0] - 2
    size = rows // parts
    stores = []
    for i in range(parts):
        part = pl.ds(i * size, size)
        done_ref[part, :] = sums_ref[part, :].astype(BF16)
        store = pltpu.make_async_copy(done_ref.at[part], out_ref.at[part], sems.at[2 + i])
        store.start()
        stores.append(store)
    for store in stores:
        store.wait()


def build_coupling(index, repeats, coupling, root_rows):
    rows, columns = 2 * coupling.shape[-2], coupling.shape[-1]
    return kernel_call(
        build_kernel,
        (index, repeats, coupling),
        [SMEM, SMEM, HBM],
        like((root_rows, rows)),
        HBM,
        scratch=[
            pltpu.VMEM((rows, columns), BF16),
            pltpu.VMEM((columns, rows), F32),
            pltpu.VMEM((root_rows, rows), F32),
            pltpu.VMEM((root_rows, rows), BF16),
            DMA((10,)),
        ],
        limit=60,
        moved=30 * MIB,
    )


def pair_dot(blocks_ref, start, stop, rights):
    lanes = blocks_ref.shape[2]
    total = None
    for i in range(start // 2, stop // 2):
        left = jnp.concatenate([blocks_ref[2 * i], blocks_ref[2 * i + 1]], axis=1)
        term = rights(left, slice(i * 2 * lanes, (i + 1) * 2 * lanes))
        total = term if total is None else total + term
    return total


def against(*parts):
    return lambda left, columns: lax.dot_general(
        left,
        jnp.concatenate([part[:, columns] for part in parts], axis=0),
        (((1,), (1,)), ((), ())),
        preferred_element_type=F32,
    )


def ordered(core_ref, total):
    return jnp.where(core_ref[0] == 0, total, pltpu.roll(total, total.shape[1] // 2, 1))


def write_copies(copies_ref, value):
    for j in range(copies_ref.shape[0]):
        copies_ref[j] = value


def first_product_kernel(core_ref, blocks_ref, own_ref, other_ref, base_ref, copies_ref):
    total = pair_dot(blocks_ref, 0, blocks_ref.shape[0], against(own_ref, other_ref))
    write_copies(copies_ref, (base_ref[...] - ordered(core_ref, total)).astype(BF16))


def product_kernel(core_ref, blocks_ref, own_ref, other_ref, copies_ref):
    rights = against(own_ref.at[1, 0], other_ref.at[1, 0])
    total = pair_dot(blocks_ref, 0, blocks_ref.shape[0], rights)
    write_copies(copies_ref, ordered(core_ref, total).astype(BF16))


def last_product_kernel(
    core_ref, r0_ref, x1_ref, own_ref, other_ref, upper_own_ref, upper_other_ref, copies_ref
):
    chips = x1_ref.shape[0]
    diagonal = pair_dot(r0_ref, 0, chips, against(own_ref.at[0, 0], other_ref.at[0, 0]))
    diagonal = diagonal.astype(BF16).astype(F32)
    total = diagonal - pair_dot(x1_ref, 0, chips, against(upper_own_ref, upper_other_ref))
    write_copies(copies_ref, ordered(core_ref, total).astype(BF16))


def couple_kernel(x0_ref, x1_ref, matrix_ref, out_ref):
    count, half, lanes = x0_ref.shape
    total = None
    for start, blocks_ref in ((0, x0_ref), (count * lanes, x1_ref)):

        def rights(left, columns):
            rows = slice(start + columns.start, start + columns.stop)
            return jnp.dot(left, matrix_ref[rows, :], preferred_element_type=F32)

        term = pair_dot(blocks_ref, 0, count, rights)
        total = term if total is None else total + term
    out_ref[...] = total


def settle_kernel(core_ref, mine_ref, got_ref, z0_ref, z1_ref, copies_ref, c1_ref, rest_ref):
    stripe = z0_ref.shape[0]

    def work(first, second):
        both = jnp.concatenate([first[...], second[...]], axis=0).T
        rest_ref[...] = z0_ref[...] - both[:stripe]
        value = (z1_ref[...] - both[stripe:]).astype(BF16)
        write_copies(copies_ref, value)
        c1_ref[...] = value

    by_core(core_ref, mine_ref, got_ref, work)


def closing_kernel(core_ref, own_ref, other_ref, top_ref, rest_ref, c1_ref, out_ref):
    out_ref[0, 1, 0] = c1_ref[...]

    def work(first, second):
        total = rest_ref[...] - plane_dot(top_ref, first, second, own_ref.shape[1])
        out_ref[0, 0, 0] = total.astype(BF16)

    by_core(core_ref, own_ref, other_ref, work)


def body(
    child_rhs,
    child_lower,
    child_inverse,
    child_upper,
    child_coupling,
    child_update,
    update_owner,
    update_slot,
    root_rhs,
    root_lower,
    root_inverse,
    root_upper,
):
    planes = lax.axis_size("x") * lax.axis_size("z")
    cubes = planes * lax.axis_size("y")
    devices = cubes * 2
    stripe, rhs = root_rhs.shape[2:]
    half = rhs // 2
    kc = child_inverse.shape[-1]
    kr = root_inverse.shape[-1]
    nc = child_lower.shape[-1]
    held = update_slot.shape[1]
    owner = update_owner.reshape(1, held)
    slot = update_slot
    me = lax.axis_index("c")
    core = me.astype(jnp.int32).reshape(1)
    piece = (planes, stripe, rhs)

    opened = kernel_call(
        opening_kernel, (child_rhs, owner, slot), [VMEM] * 3,
        like((planes, stripe + 8, rhs)), VMEM,
    )
    opened, root_rhs, root_lower, root_inverse, root_upper, child_lower, child_upper = tie(
        (opened, root_rhs, root_lower, root_inverse, root_upper, child_lower, child_upper)
    )
    own_first = spread(opened, PLANE)
    kept, given = kernel_call(
        turn_kernel, (core, root_rhs), [SMEM, VMEM], [like((half, rhs))] * 2, [VMEM] * 2,
        limit=2, moved=MIB,
    )
    low = rows_of(child_lower, 1, 0, kc)
    top = rows_of(child_upper, 0, kc, nc)
    lower_own = rows_of(root_lower, 1, 0, kr)
    upper_own = rows_of(root_upper, 0, kr, 2 * kr)
    own_first, lower_own, upper_own, kept, given, low, top = tie(
        (own_first, lower_own, upper_own, kept, given, low, top)
    )
    other_first = swap(own_first)
    y1_copies = kernel_call(
        advance_kernel, (core, own_first, other_first, low, child_rhs), [SMEM] + [VMEM] * 4,
        like(piece), VMEM, limit=2, moved=MIB,
    )
    y1_copies, given = tie((y1_copies, given))
    own_second = spread(y1_copies, PLANE)

    part, z0c, index, repeats, select, targets = kernel_call(
        functools.partial(aside_kernel, stripe, kr),
        (core, own_first, other_first, child_update, child_inverse, owner, slot),
        [SMEM, VMEM, VMEM, HBM, HBM, VMEM, VMEM],
        [
            like((held, rhs), F32),
            like((stripe, rhs), F32),
            like((2 * planes, held), jnp.int32),
            like((2 * planes, held), jnp.int32),
            like((devices * 4, held)),
            like((held, held)),
        ],
        [VMEM] * 6,
        scratch=[pltpu.VMEM((held, kc), BF16), pltpu.VMEM((stripe, kc), BF16), DMA((2,))],
        limit=4, moved=2 * MIB,
    )
    index, repeats = index.reshape(-1), repeats[:, 0]
    got = swap(given)
    own_second, part, z0c, index, repeats, select, targets, got = tie(
        (own_second, part, z0c, index, repeats, select, targets, got)
    )
    other_second = swap(own_second)

    packed = kernel_call(
        contribute_kernel, (core, own_second, other_second, child_update, part, select, targets),
        [SMEM, VMEM, VMEM, HBM] + [VMEM] * 3, like((devices * 4, rhs)), VMEM,
        scratch=[pltpu.VMEM((held, kc), BF16), DMA], limit=4, moved=MIB,
    )
    packed, lower_own, own_second, other_second = tie(
        (packed, lower_own, own_second, other_second)
    )
    arrived = spread(packed.reshape(devices, 4, rhs), ALL)
    z1c = kernel_call(
        diagonal_kernel, (core, own_second, other_second, child_inverse),
        [SMEM, VMEM, VMEM, HBM], like((stripe, rhs), F32), VMEM,
        scratch=[pltpu.VMEM((stripe, kc), BF16), DMA], limit=4, moved=MIB,
    )
    arrived, z1c = tie((arrived, z1c))
    lower_other = swap(lower_own)

    r0_copies, right = kernel_call(
        unpack_kernel, (core, arrived.reshape(devices * 4, rhs), kept, got), [SMEM] + [VMEM] * 3,
        [like((cubes, half, rhs)), like((half, rhs), F32)], [VMEM] * 2, limit=4, moved=MIB,
    )
    r0_copies, index, repeats = tie((r0_copies, index, repeats))
    summed = build_coupling(index, repeats, child_coupling, 2 * kr)
    whole = (cubes, half, rhs)
    work = dict(flops=2 * cubes * half * rhs * rhs, moved=4 * MIB)
    r0, summed, lower_other = tie((spread(r0_copies, CUBE), summed, lower_other))
    r1_copies = kernel_call(
        first_product_kernel, (core, r0, lower_own, lower_other, right),
        [SMEM] + [VMEM] * 4, like(whole), VMEM, limit=4, **work,
    )
    r1_copies, inverse, upper_own = tie((r1_copies, root_inverse, upper_own))
    inverse_other, upper_other = swap(inverse), swap(upper_own)
    r1, inverse_other, upper_other = tie((spread(r1_copies, CUBE), inverse_other, upper_other))
    x1_copies = kernel_call(
        product_kernel, (core, r1, root_inverse, inverse_other), [SMEM] + [VMEM] * 3,
        like(whole), VMEM, limit=4, **work,
    )
    x1_copies, summed = tie((x1_copies, summed))
    summed_other = swap(summed)
    x1, summed_other = tie((spread(x1_copies, CUBE), summed_other))
    x0_copies = kernel_call(
        last_product_kernel, (core, r0, x1, root_inverse, inverse_other, upper_own, upper_other),
        [SMEM] + [VMEM] * 6, like(whole), VMEM, limit=4, **work,
    )
    x0, x0_copies, x1_copies = tie((spread(x0_copies, CUBE), x0_copies, x1_copies))

    def couple(x0, matrix):
        return kernel_call(
            couple_kernel, (x0, x1, matrix), [VMEM] * 3, like((half, 2 * stripe), F32), VMEM,
            limit=4, flops=4 * cubes * half * rhs * rhs, moved=6 * MIB,
        )

    given, x0 = tie((couple(x0, summed_other), x0))
    theirs, mine = swap(given), couple(x0, summed)
    c1_copies, c1, rest = kernel_call(
        settle_kernel, (core, mine, theirs, z0c, z1c), [SMEM] + [VMEM] * 4,
        [like(piece), like((stripe, rhs)), like((stripe, rhs), F32)], [VMEM] * 3,
        limit=2, moved=MIB,
    )
    c1_copies, x0_own, x1_own = tie((c1_copies, x0_copies[0], x1_copies[0]))
    own_c1 = spread(c1_copies, PLANE)

    def own_rows(half_rows):
        pair = in_core_order(half_rows, swap(half_rows), 0).reshape(rhs, 2 * stripe)
        rows = pair.T
        return jnp.where(me == 0, rows[:stripe], rows[stripe:])

    root_solution = jnp.stack([own_rows(x0_own), own_rows(x1_own)])[:, None]
    own_c1, root_solution = tie((own_c1, root_solution))
    child_solution = kernel_call(
        closing_kernel, (core, own_c1, swap(own_c1), top, rest, c1),
        [SMEM] + [VMEM] * 5, like(child_rhs.shape), VMEM, limit=2, moved=MIB,
    )
    return child_solution, root_solution


def solution(mesh):
    leaf, front = mesh.devices.shape
    fine = Mesh(mesh.devices.reshape((leaf, 4, front // 8, 2)), ALL)
    subtree = P("y", None, ("x", "z", "c"), None, None)
    ancestor = P(None, ALL, None, None)
    in_specs = (
        subtree,
        subtree,
        subtree,
        subtree,
        subtree,
        P("y", ("x", "z", "c"), None),
        P("y", ("x", "z", "c"), None),
        P("y", ("x", "z", "c")),
        ancestor,
        ancestor,
        ancestor,
        ancestor,
    )
    return jax.shard_map(
        body, mesh=fine, in_specs=in_specs, out_specs=(subtree, ancestor), check_vma=False
    )
```

```python
import functools

import jax
import jax.numpy as jnp
from jax import lax
from jax.experimental import pallas as pl
from jax.experimental.pallas import tpu as pltpu
from jax.sharding import Mesh
from jax.sharding import PartitionSpec as P

F32 = jnp.float32
BF16 = jnp.bfloat16
ALL = ("y", "x", "z", "c")
PLANE = ("x", "z")
CUBE = ("y", "x", "z")
VMEM = pl.BlockSpec(memory_space=pltpu.VMEM)
SMEM = pl.BlockSpec(memory_space=pltpu.SMEM)
HBM = pl.BlockSpec(memory_space=pltpu.HBM)
DMA = pltpu.SemaphoreType.DMA
MIB = 1 << 20
BATCH = 8
tie = lax.optimization_barrier


def swap(array):
    return lax.ppermute(array, "c", [(0, 1), (1, 0)])


def spread(copies, axes):
    return lax.all_to_all(copies, axes, 0, 0)


def in_core_order(own, other, axis):
    first = lax.axis_index("c") == 0
    return jnp.stack([jnp.where(first, own, other), jnp.where(first, other, own)], axis=axis)


def rows_of(array, block, first, last):
    lead = array.ndim - 4
    start = (0,) * lead + (block, 0, 0, first)
    stop = (1,) * lead + (block + 1, 1, array.shape[-2], last)
    return lax.slice(array, start, stop).reshape(array.shape[-2], last - first)


def like(shape, dtype=BF16):
    return jax.ShapeDtypeStruct(shape, dtype)


def kernel_call(body, args, specs, shapes, out_specs, scratch=(), limit=None, flops=0, moved=0):
    return pl.pallas_call(
        body,
        out_shape=shapes,
        in_specs=specs,
        out_specs=out_specs,
        scratch_shapes=list(scratch),
        compiler_params=pltpu.CompilerParams(
            vmem_limit_bytes=None if limit is None else limit * MIB
        ),
        cost_estimate=pl.CostEstimate(flops=flops, bytes_accessed=moved, transcendentals=0),
    )(*args)


def by_core(core_ref, own_refs, other_refs, work):
    @pl.when(core_ref[0] == 0)
    def _():
        work(own_refs, other_refs)

    @pl.when(core_ref[0] != 0)
    def _():
        work(other_refs, own_refs)


def plane_dot(matrix_ref, first_ref, second_ref, rows):
    total = None
    for p in range(first_ref.shape[0] // 2):
        block = jnp.concatenate(
            [
                first_ref[2 * p, 0:rows],
                second_ref[2 * p, 0:rows],
                first_ref[2 * p + 1, 0:rows],
                second_ref[2 * p + 1, 0:rows],
            ],
            axis=0,
        )
        term = jnp.dot(
            matrix_ref[:, p * 4 * rows : (p + 1) * 4 * rows], block, preferred_element_type=F32
        )
        total = term if total is None else total + term
    return total


def opening_kernel(rhs_ref, owner_ref, slot_ref, out_ref):
    row = lax.broadcasted_iota(jnp.int32, (8, 128), 0)
    marks = jnp.where(row == 0, owner_ref[...], jnp.where(row == 1, slot_ref[...], 0))
    marks = marks.astype(F32).astype(BF16)
    rows = rhs_ref.shape[3]
    for j in range(out_ref.shape[0]):
        out_ref[j, 0:rows] = rhs_ref[0, 0, 0]
        out_ref[j, rows : rows + 8] = marks


def turn_kernel(core_ref, rhs_ref, kept_ref, given_ref):
    both = jnp.concatenate(
        [rhs_ref[0, 0].astype(F32).T, rhs_ref[1, 0].astype(F32).T], axis=1
    ).astype(BF16)
    half = both.shape[0] // 2

    @pl.when(core_ref[0] == 0)
    def _():
        kept_ref[...] = both[:half]
        given_ref[...] = both[half:]

    @pl.when(core_ref[0] != 0)
    def _():
        kept_ref[...] = both[half:]
        given_ref[...] = both[:half]


def advance_kernel(core_ref, own_ref, other_ref, low_ref, rhs_ref, out_ref):
    rows = out_ref.shape[1]

    def work(first, second):
        total = rhs_ref[0, 1, 0].astype(F32) - plane_dot(low_ref, first, second, rows)
        value = total.astype(BF16)
        for j in range(out_ref.shape[0]):
            out_ref[j] = value

    by_core(core_ref, own_ref, other_ref, work)


def aside_kernel(
    rows, kr, core_ref, own_ref, other_ref, update_ref, inverse_ref, owner_ref, slot_ref,
    part_ref, z0_ref, index_ref, repeats_ref, select_ref, targets_ref, low_ref, diag_ref, sems
):
    kc = low_ref.shape[1]
    copies = [
        pltpu.make_async_copy(update_ref.at[0, :, pl.ds(0, kc)], low_ref, sems.at[0]),
        pltpu.make_async_copy(inverse_ref.at[0, 0, 0], diag_ref, sems.at[1]),
    ]
    for copy in copies:
        copy.start()

    held = owner_ref.shape[1]
    owner = owner_ref[...].astype(F32)
    owners = jnp.broadcast_to(owner, (held, held))
    above = lax.broadcasted_iota(jnp.int32, (held, held), 0) < lax.broadcasted_iota(
        jnp.int32, (held, held), 1
    )
    same = jnp.where((owners == owners.T) & above, 1.0, 0.0)
    place = owner * 2.0 + jnp.sum(same, axis=0, keepdims=True)
    row = lax.broadcasted_iota(jnp.int32, (select_ref.shape[0], held), 0)
    wanted = (row // 8 * 4 + row % 4).astype(F32)
    select_ref[...] = jnp.where(wanted == place, 1.0, 0.0).astype(BF16)
    slot = slot_ref[...]
    target = slot // rows * (2 * rows) + owner_ref[...] % 2 * rows + slot % rows + 1
    targets_ref[...] = jnp.broadcast_to(target.astype(F32), (held, held)).T.astype(BF16)


    def work(first, second):
        for j in range(own_ref.shape[0]):
            for c, source in enumerate((first, second)):
                marks = source[j, rows : rows + 8].astype(F32).astype(jnp.int32)
                owner, slot = marks[0:1], marks[1:2]
                index_ref[2 * j + c : 2 * j + c + 1, :] = (
                    (slot // rows) * kr + owner * rows + slot % rows
                )
        index = index_ref[...]
        lane = lax.broadcasted_iota(jnp.int32, index.shape, 1) % BATCH
        found = jnp.zeros(index.shape, jnp.int32)
        for d in range(1, BATCH):
            again = (pltpu.roll(index, d, 1) == index) & (lane >= d)
            found = jnp.maximum(found, jnp.where(again, 1, 0))
        repeats_ref[...] = jnp.broadcast_to(
            jnp.max(found, axis=1, keepdims=True), repeats_ref.shape
        )
        copies[0].wait()
        part_ref[...] = plane_dot(low_ref, first, second, rows)
        copies[1].wait()
        z0_ref[...] = plane_dot(diag_ref, first, second, rows).astype(BF16).astype(F32)

    by_core(core_ref, own_ref, other_ref, work)


def contribute_kernel(
    core_ref, own_ref, other_ref, update_ref, part_ref, select_ref, targets_ref,
    out_ref, high_ref, sem
):
    kc = high_ref.shape[1]
    load = pltpu.make_async_copy(update_ref.at[0, :, pl.ds(kc, kc)], high_ref, sem)
    load.start()
    rows = own_ref.shape[1]
    load.wait()

    def work(first, second):
        contribution = -(part_ref[...] + plane_dot(high_ref, first, second, rows))
        contribution = contribution.astype(BF16)
        half = contribution.shape[1] // 2
        targets = targets_ref[:, :half]
        source = jnp.concatenate(
            [contribution[:, :half], targets, contribution[:, half:], targets], axis=1
        )
        both = jnp.dot(select_ref[...], source, preferred_element_type=F32)
        lanes = 2 * half
        upper = lax.broadcasted_iota(jnp.int32, (both.shape[0], lanes), 0) % 8 >= 4
        out_ref[...] = jnp.where(upper, both[:, lanes:], both[:, :lanes]).astype(BF16)

    by_core(core_ref, own_ref, other_ref, work)


def diagonal_kernel(core_ref, own_ref, other_ref, inverse_ref, z1_ref, diag_ref, sem):
    load = pltpu.make_async_copy(inverse_ref.at[0, 1, 0], diag_ref, sem)
    load.start()
    load.wait()

    def work(first, second):
        total = plane_dot(diag_ref, first, second, own_ref.shape[1])
        z1_ref[...] = total.astype(BF16).astype(F32)

    by_core(core_ref, own_ref, other_ref, work)


def unpack_kernel(core_ref, arrived_ref, kept_ref, got_ref, copies_ref, right_ref):
    half, lanes = right_ref.shape
    arrived = arrived_ref[...]
    code = arrived[:, half : half + 1].astype(F32)
    lane = lax.broadcasted_iota(jnp.int32, (arrived.shape[0], 2 * lanes), 1).astype(F32)
    lands = jnp.where(code == lane + 1.0, 1.0, 0.0).astype(BF16)
    received = lax.dot_general(
        arrived, lands, (((0,), (0,)), ((), ())), preferred_element_type=F32
    )[:half]

    def work(first, second):
        bases = [
            jnp.concatenate(
                [first[:, r * half : (r + 1) * half], second[:, r * half : (r + 1) * half]], axis=1
            ).astype(F32)
            for r in range(2)
        ]
        value = (bases[0] + received[:, :lanes]).astype(BF16)
        for j in range(copies_ref.shape[0]):
            copies_ref[j] = value
        right_ref[...] = bases[1] + received[:, lanes:]

    by_core(core_ref, kept_ref, got_ref, work)


def build_kernel(index_ref, repeats_ref, coupling_ref, out_ref, raw_ref, turned_ref, sums_ref, done_ref, sems):
    rows, width = sums_ref.shape
    half = width // 2
    loads = [
        pltpu.make_async_copy(
            coupling_ref.at[0, r, 0], raw_ref.at[pl.ds(r * half, half)], sems.at[r]
        )
        for r in range(2)
    ]
    for load in loads:
        load.start()

    def clear(i, carry):
        sums_ref[pl.ds(pl.multiple_of(i * 128, 128), 128), :] = jnp.zeros((128, width), F32)
        return carry

    lax.fori_loop(0, rows // 128, clear, 0, unroll=4)
    for load in loads:
        load.wait()
    for i in range(turned_ref.shape[0] // 128):
        part = slice(i * 128, (i + 1) * 128)
        turned_ref[part, :] = raw_ref[:, part].astype(F32).T

    def add_line(line, carry):
        start = pl.multiple_of(line * 128, 128)

        def add_apart(group, carry):
            base = pl.multiple_of(start + group * BATCH, BATCH)
            block = turned_ref[pl.ds(base, BATCH), :]
            at = [pl.ds(index_ref[base + j], 1) for j in range(BATCH)]
            values = [sums_ref[at[j], :] + block[j : j + 1] for j in range(BATCH)]
            for j in range(BATCH):
                sums_ref[at[j], :] = values[j]
            return carry

        def add_in_turn(group, carry):
            base = pl.multiple_of(start + group * BATCH, BATCH)
            block = turned_ref[pl.ds(base, BATCH), :]
            for j in range(BATCH):
                at = pl.ds(index_ref[base + j], 1)
                sums_ref[at, :] = sums_ref[at, :] + block[j : j + 1]
            return carry

        @pl.when(repeats_ref[line] == 0)
        def _():
            lax.fori_loop(0, 128 // BATCH, add_apart, 0, unroll=4)

        @pl.when(repeats_ref[line] != 0)
        def _():
            lax.fori_loop(0, 128 // BATCH, add_in_turn, 0)

        return carry

    lax.fori_loop(0, turned_ref.shape[0] // 128, add_line, 0)
    parts = sems.shape[0] - 2
    size = rows // parts
    stores = []
    for i in range(parts):
        part = pl.ds(i * size, size)
        done_ref[part, :] = sums_ref[part, :].astype(BF16)
        store = pltpu.make_async_copy(done_ref.at[part], out_ref.at[part], sems.at[2 + i])
        store.start()
        stores.append(store)
    for store in stores:
        store.wait()


def build_coupling(index, repeats, coupling, root_rows):
    rows, columns = 2 * coupling.shape[-2], coupling.shape[-1]
    return kernel_call(
        build_kernel,
        (index, repeats, coupling),
        [SMEM, SMEM, HBM],
        like((root_rows, rows)),
        HBM,
        scratch=[
            pltpu.VMEM((rows, columns), BF16),
            pltpu.VMEM((columns, rows), F32),
            pltpu.VMEM((root_rows, rows), F32),
            pltpu.VMEM((root_rows, rows), BF16),
            DMA((10,)),
        ],
        limit=60,
        moved=30 * MIB,
    )


def pair_dot(blocks_ref, start, stop, rights):
    lanes = blocks_ref.shape[2]
    total = None
    for i in range(start // 2, stop // 2):
        left = jnp.concatenate([blocks_ref[2 * i], blocks_ref[2 * i + 1]], axis=1)
        term = rights(left, slice(i * 2 * lanes, (i + 1) * 2 * lanes))
        total = term if total is None else total + term
    return total


def against(*parts):
    return lambda left, columns: lax.dot_general(
        left,
        jnp.concatenate([part[:, columns] for part in parts], axis=0),
        (((1,), (1,)), ((), ())),
        preferred_element_type=F32,
    )


def ordered(core_ref, total):
    return jnp.where(core_ref[0] == 0, total, pltpu.roll(total, total.shape[1] // 2, 1))


def write_copies(copies_ref, value):
    for j in range(copies_ref.shape[0]):
        copies_ref[j] = value


def first_product_kernel(core_ref, blocks_ref, own_ref, other_ref, base_ref, copies_ref):
    total = pair_dot(blocks_ref, 0, blocks_ref.shape[0], against(own_ref, other_ref))
    write_copies(copies_ref, (base_ref[...] - ordered(core_ref, total)).astype(BF16))


def product_kernel(core_ref, blocks_ref, own_ref, other_ref, copies_ref):
    rights = against(own_ref.at[1, 0], other_ref.at[1, 0])
    total = pair_dot(blocks_ref, 0, blocks_ref.shape[0], rights)
    write_copies(copies_ref, ordered(core_ref, total).astype(BF16))


def last_product_kernel(
    core_ref, r0_ref, x1_ref, own_ref, other_ref, upper_own_ref, upper_other_ref, copies_ref
):
    chips = x1_ref.shape[0]
    diagonal = pair_dot(r0_ref, 0, chips, against(own_ref.at[0, 0], other_ref.at[0, 0]))
    diagonal = diagonal.astype(BF16).astype(F32)
    total = diagonal - pair_dot(x1_ref, 0, chips, against(upper_own_ref, upper_other_ref))
    write_copies(copies_ref, ordered(core_ref, total).astype(BF16))


def couple_kernel(x0_ref, x1_ref, matrix_ref, out_ref):
    count, half, lanes = x0_ref.shape
    total = None
    for start, blocks_ref in ((0, x0_ref), (count * lanes, x1_ref)):

        def rights(left, columns):
            rows = slice(start + columns.start, start + columns.stop)
            return jnp.dot(left, matrix_ref[rows, :], preferred_element_type=F32)

        term = pair_dot(blocks_ref, 0, count, rights)
        total = term if total is None else total + term
    out_ref[...] = total


def settle_kernel(core_ref, mine_ref, got_ref, z0_ref, z1_ref, copies_ref, c1_ref, rest_ref):
    stripe = z0_ref.shape[0]

    def work(first, second):
        both = jnp.concatenate([first[...], second[...]], axis=0).T
        rest_ref[...] = z0_ref[...] - both[:stripe]
        value = (z1_ref[...] - both[stripe:]).astype(BF16)
        write_copies(copies_ref, value)
        c1_ref[...] = value

    by_core(core_ref, mine_ref, got_ref, work)


def closing_kernel(core_ref, own_ref, other_ref, top_ref, rest_ref, c1_ref, out_ref):
    out_ref[0, 1, 0] = c1_ref[...]

    def work(first, second):
        total = rest_ref[...] - plane_dot(top_ref, first, second, own_ref.shape[1])
        out_ref[0, 0, 0] = total.astype(BF16)

    by_core(core_ref, own_ref, other_ref, work)


def body(
    child_rhs,
    child_lower,
    child_inverse,
    child_upper,
    child_coupling,
    child_update,
    update_owner,
    update_slot,
    root_rhs,
    root_lower,
    root_inverse,
    root_upper,
):
    planes = lax.axis_size("x") * lax.axis_size("z")
    cubes = planes * lax.axis_size("y")
    devices = cubes * 2
    stripe, rhs = root_rhs.shape[2:]
    half = rhs // 2
    kc = child_inverse.shape[-1]
    kr = root_inverse.shape[-1]
    nc = child_lower.shape[-1]
    held = update_slot.shape[1]
    owner = update_owner.reshape(1, held)
    slot = update_slot
    me = lax.axis_index("c")
    core = me.astype(jnp.int32).reshape(1)
    piece = (planes, stripe, rhs)

    opened = kernel_call(
        opening_kernel, (child_rhs, owner, slot), [VMEM] * 3,
        like((planes, stripe + 8, rhs)), VMEM,
    )
    opened, root_rhs, root_lower, root_inverse, root_upper, child_lower, child_upper = tie(
        (opened, root_rhs, root_lower, root_inverse, root_upper, child_lower, child_upper)
    )
    own_first = spread(opened, PLANE)
    kept, given = kernel_call(
        turn_kernel, (core, root_rhs), [SMEM, VMEM], [like((half, rhs))] * 2, [VMEM] * 2,
        limit=2, moved=MIB,
    )
    low = rows_of(child_lower, 1, 0, kc)
    top = rows_of(child_upper, 0, kc, nc)
    lower_own = rows_of(root_lower, 1, 0, kr)
    upper_own = rows_of(root_upper, 0, kr, 2 * kr)
    own_first, lower_own, upper_own, kept, given, low, top = tie(
        (own_first, lower_own, upper_own, kept, given, low, top)
    )
    other_first = swap(own_first)
    y1_copies = kernel_call(
        advance_kernel, (core, own_first, other_first, low, child_rhs), [SMEM] + [VMEM] * 4,
        like(piece), VMEM, limit=2, moved=MIB,
    )
    y1_copies, given = tie((y1_copies, given))
    own_second = spread(y1_copies, PLANE)

    part, z0c, index, repeats, select, targets = kernel_call(
        functools.partial(aside_kernel, stripe, kr),
        (core, own_first, other_first, child_update, child_inverse, owner, slot),
        [SMEM, VMEM, VMEM, HBM, HBM, VMEM, VMEM],
        [
            like((held, rhs), F32),
            like((stripe, rhs), F32),
            like((2 * planes, held), jnp.int32),
            like((2 * planes, held), jnp.int32),
            like((devices * 4, held)),
            like((held, held)),
        ],
        [VMEM] * 6,
        scratch=[pltpu.VMEM((held, kc), BF16), pltpu.VMEM((stripe, kc), BF16), DMA((2,))],
        limit=4, moved=2 * MIB,
    )
    index, repeats = index.reshape(-1), repeats[:, 0]
    got = swap(given)
    own_second, part, z0c, index, repeats, select, targets, got = tie(
        (own_second, part, z0c, index, repeats, select, targets, got)
    )
    other_second = swap(own_second)

    packed = kernel_call(
        contribute_kernel, (core, own_second, other_second, child_update, part, select, targets),
        [SMEM, VMEM, VMEM, HBM] + [VMEM] * 3, like((devices * 4, rhs)), VMEM,
        scratch=[pltpu.VMEM((held, kc), BF16), DMA], limit=4, moved=MIB,
    )
    packed, lower_own, own_second, other_second = tie(
        (packed, lower_own, own_second, other_second)
    )
    arrived = spread(packed.reshape(devices, 4, rhs), ALL)
    z1c = kernel_call(
        diagonal_kernel, (core, own_second, other_second, child_inverse),
        [SMEM, VMEM, VMEM, HBM], like((stripe, rhs), F32), VMEM,
        scratch=[pltpu.VMEM((stripe, kc), BF16), DMA], limit=4, moved=MIB,
    )
    arrived, z1c = tie((arrived, z1c))
    lower_other = swap(lower_own)

    r0_copies, right = kernel_call(
        unpack_kernel, (core, arrived.reshape(devices * 4, rhs), kept, got), [SMEM] + [VMEM] * 3,
        [like((cubes, half, rhs)), like((half, rhs), F32)], [VMEM] * 2, limit=4, moved=MIB,
    )
    r0_copies, index, repeats = tie((r0_copies, index, repeats))
    summed = build_coupling(index, repeats, child_coupling, 2 * kr)
    whole = (cubes, half, rhs)
    work = dict(flops=2 * cubes * half * rhs * rhs, moved=4 * MIB)
    r0, summed, lower_other = tie((spread(r0_copies, CUBE), summed, lower_other))
    r1_copies = kernel_call(
        first_product_kernel, (core, r0, lower_own, lower_other, right),
        [SMEM] + [VMEM] * 4, like(whole), VMEM, limit=4, **work,
    )
    r1_copies, inverse, upper_own = tie((r1_copies, root_inverse, upper_own))
    inverse_other, upper_other = swap(inverse), swap(upper_own)
    r1, inverse_other, upper_other = tie((spread(r1_copies, CUBE), inverse_other, upper_other))
    x1_copies = kernel_call(
        product_kernel, (core, r1, root_inverse, inverse_other), [SMEM] + [VMEM] * 3,
        like(whole), VMEM, limit=4, **work,
    )
    x1_copies, summed = tie((x1_copies, summed))
    summed_other = swap(summed)
    x1, summed_other = tie((spread(x1_copies, CUBE), summed_other))
    x0_copies = kernel_call(
        last_product_kernel, (core, r0, x1, root_inverse, inverse_other, upper_own, upper_other),
        [SMEM] + [VMEM] * 6, like(whole), VMEM, limit=4, **work,
    )
    x0, x0_copies, x1_copies = tie((spread(x0_copies, CUBE), x0_copies, x1_copies))

    def couple(x0, matrix):
        return kernel_call(
            couple_kernel, (x0, x1, matrix), [VMEM] * 3, like((half, 2 * stripe), F32), VMEM,
            limit=4, flops=4 * cubes * half * rhs * rhs, moved=6 * MIB,
        )

    given, x0 = tie((couple(x0, summed_other), x0))
    theirs, mine = swap(given), couple(x0, summed)
    c1_copies, c1, rest = kernel_call(
        settle_kernel, (core, mine, theirs, z0c, z1c), [SMEM] + [VMEM] * 4,
        [like(piece), like((stripe, rhs)), like((stripe, rhs), F32)], [VMEM] * 3,
        limit=2, moved=MIB,
    )
    c1_copies, x_own = tie((c1_copies, jnp.stack([x0_copies[0], x1_copies[0]])))
    own_c1 = spread(c1_copies, PLANE)

    pair = in_core_order(x_own, swap(x_own), 1).reshape(2, rhs, 2 * stripe)
    rows = jnp.swapaxes(pair, 1, 2)
    root_solution = jnp.where(me == 0, rows[:, :stripe], rows[:, stripe:])[:, None]
    own_c1, root_solution = tie((own_c1, root_solution))
    child_solution = kernel_call(
        closing_kernel, (core, own_c1, swap(own_c1), top, rest, c1),
        [SMEM] + [VMEM] * 5, like(child_rhs.shape), VMEM, limit=2, moved=MIB,
    )
    return child_solution, root_solution


def solution(mesh):
    leaf, front = mesh.devices.shape
    fine = Mesh(mesh.devices.reshape((leaf, 4, front // 8, 2)), ALL)
    subtree = P("y", None, ("x", "z", "c"), None, None)
    ancestor = P(None, ALL, None, None)
    in_specs = (
        subtree,
        subtree,
        subtree,
        subtree,
        subtree,
        P("y", ("x", "z", "c"), None),
        P("y", ("x", "z", "c"), None),
        P("y", ("x", "z", "c")),
        ancestor,
        ancestor,
        ancestor,
        ancestor,
    )
    return jax.shard_map(
        body, mesh=fine, in_specs=in_specs, out_specs=(subtree, ancestor), check_vma=False
    )
```
